512 devices in a mesh: slab: 16 (over z, x_hi), blk: 32 (over y, x_lo, core).
Axes of the slice: x: 4 (x_hi: 2, x_lo: 2; x = x_hi * 2 + x_lo), y: 8, z: 8, core: 2. Of those that a mesh axis runs over, the one named last changes fastest.
Arguments:
- fixed_image: bfloat16 [1024, 512, 128], P('blk', 'slab'), may hold values from -6 to 6
- moving_image: bfloat16 [1024, 512, 128], P('blk', 'slab'), may hold values from -6 to 6
- fetch_owner: int32 [32, 16, 4, 4], P('blk', 'slab'), may hold values from 0 to 31, as said below
- fetch_block: int32 [32, 16, 4, 4], P('blk', 'slab'), may hold values from 0 to 3
- fetch_count: int32 [32, 16, 4], P('blk', 'slab'), may hold values from 1 to 4, as said below
- interp_level: int32 [32, 16, 4, 3, 4], P('blk', 'slab'), may hold values from 0 to 7
- block_mask: int32 [32, 16, 4], P('blk', 'slab'), may hold values 0 or 1
Outputs:
- update: float32 [3, 1024, 512, 128], P(None, 'blk', 'slab')
The draws below stay inside these ranges and needn't reach their ends.
Inputs may be any that keep to these rules, and one draw needn't show every extreme that they name: `fetch_owner`: entries k < fetch_count of one device's lists name any one owner at most 2 times in all; in every draw some owner is named exactly 2 times by every device of its slab. Entries k >= fetch_count are not read. `fetch_count`: every device has a block whose list holds 4 entries.
All inputs are finite; a program needn't handle non-finite values. No bound on the sum of `block_mask` on one device may be relied on, other than what follows from the above.
Results may differ from the reference program's by a relative error of at most 0.006.
Values may be sent and summed in bfloat16 or wider, within the bound.
No kernel may reach another device: no remote copies, remote signals or barrier semaphores. Data moves between devices by JAX's collectives and lax.ppermute only.
A program may use at most 64 MiB of HBM per device.

```python
import math
import jax
import jax.numpy as jnp
from jax import lax

BLOCK_SIDE = 32
BLOCKS_DEV = 4
MAX_LIST = 4
LEVELS = 8
BOX_RADIUS = 2
SMOOTH_RADIUS = 3
PEER_SLOTS = 2
WIDTH_X = 1024
WIDTH_Z = 512
WIDTH_Y = 128
N_SLAB = 16
N_BLK = 32


def list_layout(key):
    base_key = jax.random.fold_in(key, 4101)
    key_count, key_full, key_hot, key_order, key_owner = jax.random.split(base_key, 5)
    entry_total = BLOCKS_DEV * MAX_LIST
    counts = jax.random.randint(key_count, (N_BLK, N_SLAB, BLOCKS_DEV), 1, MAX_LIST + 1)
    full_at = jax.random.randint(key_full, (N_BLK, N_SLAB, 1), 0, BLOCKS_DEV)
    counts = jnp.where(jnp.arange(BLOCKS_DEV)[None, None, :] == full_at, MAX_LIST, counts).astype(jnp.int32)
    in_list = (jnp.arange(MAX_LIST)[None, None, None, :] < counts[..., None]).reshape(N_BLK, N_SLAB, entry_total)
    scores = jax.random.randint(key_order, (N_BLK, N_SLAB, entry_total), 0, 2 ** 20) * entry_total + jnp.arange(entry_total)[None, None, :]
    scores = jnp.where(in_list, scores, scores + 2 ** 30)
    order_pos = jnp.argsort(scores, axis=-1)
    list_rank = jnp.argsort(order_pos, axis=-1).astype(jnp.int32)
    hot_owner = jax.random.randint(key_hot, (N_SLAB,), 0, N_BLK)
    owner_scores = jax.random.randint(key_owner, (N_BLK, N_SLAB, N_BLK), 0, 2 ** 20) * N_BLK + jnp.arange(N_BLK)[None, None, :]
    owner_scores = jnp.where(jnp.arange(N_BLK)[None, None, :] == hot_owner[None, :, None], 2 ** 30, owner_scores)
    owner_order = jnp.argsort(owner_scores, axis=-1).astype(jnp.int32)
    other_pos = jnp.mod(jnp.maximum(list_rank - PEER_SLOTS, 0), N_BLK - 1)
    other_owner = jnp.take_along_axis(owner_order, other_pos, axis=-1)
    owners = jnp.where(list_rank < PEER_SLOTS, hot_owner[None, :, None], other_owner)
    return (owners.reshape(N_BLK, N_SLAB, BLOCKS_DEV, MAX_LIST).astype(jnp.int32), counts)


def draw_fetch_owner(key, part):
    return list_layout(key)[0]


def draw_fetch_count(key, part):
    return list_layout(key)[1]


def plant(drawn, rng, low, top_value):
    dims = drawn.shape
    index_at = [jax.random.randint(jax.random.fold_in(rng, axis), (), 0, dims[axis]) for axis in range(len(dims))]
    drawn = drawn.at[tuple(index_at)].set(low)
    longest = dims.index(max(dims))
    index_at[longest] = (index_at[longest] + 1) % dims[longest]
    return drawn.at[tuple(index_at)].set(top_value)


def level_of(own_key, shape, shards, low, high):
    def one(axis_at, shards_of):
        heights = jax.random.uniform(jax.random.fold_in(jax.random.fold_in(own_key, 6), axis_at), (shards_of,), jnp.float32, low / len(shards), high / len(shards))
        return jnp.repeat(jnp.exp(heights), shape[axis_at] // shards_of).reshape((-1,) + (1,) * (len(shape) - axis_at - 1))

    loudness = one(*shards[0])
    for cut in shards[1:]:
        loudness = loudness * one(*cut)
    return loudness


def noise(own_key, shape, deviation, most, shards=(), held_as=jnp.bfloat16):
    loudness = level_of(own_key, shape, shards, -0.22, 0.18) if shards else 1.0
    entries = jax.random.normal(own_key, shape, jnp.float32) * deviation * loudness
    return jnp.minimum(jnp.maximum(entries, -most), most).astype(held_as)


def setup_inputs(seed: int = 0) -> dict:
    key_of = jax.random.split(jax.random.key(seed), 8)
    return {
        "fixed_image": noise(key_of[0], (WIDTH_X, WIDTH_Z, WIDTH_Y), 1.0, 6.0, ((0, 32), (1, 16))),
        "moving_image": noise(key_of[1], (WIDTH_X, WIDTH_Z, WIDTH_Y), 1.0, 6.0, ((0, 32), (1, 16))),
        "fetch_owner": draw_fetch_owner(jax.random.fold_in(key_of[7], 71), 0),
        "fetch_block": plant(jax.random.randint(key_of[3], (N_BLK, N_SLAB, BLOCKS_DEV, MAX_LIST), 0, BLOCKS_DEV), jax.random.fold_in(key_of[3], 1), 0, BLOCKS_DEV - 1).astype(jnp.int32),
        "fetch_count": draw_fetch_count(jax.random.fold_in(key_of[7], 71), 0),
        "interp_level": plant(jax.random.randint(key_of[5], (N_BLK, N_SLAB, BLOCKS_DEV, 3, MAX_LIST), 0, LEVELS), jax.random.fold_in(key_of[5], 1), 0, LEVELS - 1).astype(jnp.int32),
        "block_mask": plant((jax.random.randint(key_of[6], (N_BLK, N_SLAB, BLOCKS_DEV), 0, 4) < 3).astype(jnp.int32), jax.random.fold_in(key_of[6], 1), 0, 1),
    }


sigma_smooth = 1.5
step_length = 2.0
var_eps = 1e-05
peak_eps = 1e-06

def smooth_weights(radius):
    weights_raw = [math.exp(-(offset * offset) / (2.0 * sigma_smooth * sigma_smooth)) for offset in range(-radius, radius + 1)]
    weights_total = sum(weights_raw)
    return [weight_one / weights_total for weight_one in weights_raw]

def window_sum(volume, axis_pos, length, weights):
    result = weights[0] * lax.slice_in_dim(volume, 0, length, axis=axis_pos)
    for offset in range(1, len(weights)):
        result = result + weights[offset] * lax.slice_in_dim(volume, offset, offset + length, axis=axis_pos)
    return result

def resample(blocks, fractions):
    for axis_step in range(3):
        axis_now = blocks.ndim - 3 + axis_step
        side_len = blocks.shape[axis_now]
        shifted = jnp.concatenate([lax.slice_in_dim(blocks, 1, side_len, axis=axis_now), lax.slice_in_dim(blocks, side_len - 1, side_len, axis=axis_now)], axis=axis_now)
        factor = fractions[..., axis_step][..., None, None, None]
        blocks = (1.0 - factor) * blocks + factor * shifted
    return blocks

def reference(fixed_image, moving_image, fetch_owner, fetch_block, fetch_count, interp_level, block_mask):
    block_side = BLOCK_SIDE
    blocks_all = moving_image.reshape(N_BLK, block_side, N_SLAB, block_side, BLOCKS_DEV, block_side).transpose(2, 0, 4, 1, 3, 5)
    packed_all = (blocks_all, fetch_owner.transpose(1, 0, 2, 3), fetch_block.transpose(1, 0, 2, 3), fetch_count.transpose(1, 0, 2), interp_level.transpose(1, 0, 2, 3, 4))

    def one_slab(packed):
        slab_blocks, owners, indices, counts, levels = packed
        sources = slab_blocks[owners, indices].astype(jnp.float32)
        fractions = jnp.swapaxes(levels.astype(jnp.float32) / LEVELS, -1, -2)
        resampled = resample(sources, fractions)
        in_list = jnp.arange(MAX_LIST)[None, None, :] < counts[:, :, None]
        weights = jnp.where(in_list, 1.0, 0.0) / counts[:, :, None].astype(jnp.float32)
        return lax.optimization_barrier(jnp.sum(resampled * weights[..., None, None, None], axis=2))
    warped_blocks = lax.map(one_slab, packed_all)
    warped = warped_blocks.astype(jnp.bfloat16).transpose(1, 3, 0, 4, 2, 5).reshape(WIDTH_X, WIDTH_Z, WIDTH_Y)
    warped = lax.optimization_barrier(warped)
    radius = BOX_RADIUS
    box_ones = [1.0] * (2 * radius + 1)
    count_box = float((2 * radius + 1) ** 3)

    def boxed(volume):
        padded = jnp.pad(volume, radius)
        result = window_sum(padded, 0, WIDTH_X, box_ones)
        result = window_sum(result, 1, WIDTH_Z, box_ones)
        return window_sum(result, 2, WIDTH_Y, box_ones)
    fixed_f = fixed_image.astype(jnp.float32)
    moving_f = warped.astype(jnp.float32)
    mean_fixed = boxed(fixed_f) / count_box
    mean_moving = boxed(moving_f) / count_box
    var_fixed = boxed(fixed_f * fixed_f) / count_box - mean_fixed * mean_fixed + var_eps
    var_moving = boxed(moving_f * moving_f) / count_box - mean_moving * mean_moving + var_eps
    covariance = boxed(fixed_f * moving_f) / count_box - mean_fixed * mean_moving
    padded_m = jnp.pad(moving_f, 1)
    grad_x = (padded_m[2:, 1:-1, 1:-1] - padded_m[:-2, 1:-1, 1:-1]) * 0.5
    grad_z = (padded_m[1:-1, 2:, 1:-1] - padded_m[1:-1, :-2, 1:-1]) * 0.5
    grad_y = (padded_m[1:-1, 1:-1, 2:] - padded_m[1:-1, 1:-1, :-2]) * 0.5
    mask_voxel = jnp.broadcast_to(block_mask.astype(jnp.float32)[:, None, :, None, :, None], (N_BLK, block_side, N_SLAB, block_side, BLOCKS_DEV, block_side)).reshape(WIDTH_X, WIDTH_Z, WIDTH_Y)
    scalar_term = mask_voxel * 2.0 * covariance / (var_fixed * var_moving) * (fixed_f - mean_fixed - covariance / var_moving * (moving_f - mean_moving))
    forces = jnp.stack([scalar_term * grad_x, scalar_term * grad_z, scalar_term * grad_y]).astype(jnp.bfloat16)
    forces = lax.optimization_barrier(forces)
    smooth_taps = smooth_weights(SMOOTH_RADIUS)
    reach = SMOOTH_RADIUS
    padded_s = jnp.pad(forces.astype(jnp.float32), ((0, 0), (reach, reach), (reach, reach), (reach, reach)))
    smoothed = window_sum(padded_s, 1, WIDTH_X, smooth_taps)
    smoothed = window_sum(smoothed, 2, WIDTH_Z, smooth_taps)
    smoothed = window_sum(smoothed, 3, WIDTH_Y, smooth_taps)
    norms = jnp.sqrt(smoothed[0] * smoothed[0] + smoothed[1] * smoothed[1] + smoothed[2] * smoothed[2])
    peak_norm = jnp.max(norms)
    return step_length * smoothed / (peak_norm + peak_eps)
```

```python
import math

import jax
import jax.numpy as jnp
from jax import lax
from jax.sharding import PartitionSpec as P

LEVELS = 8
BOX_RADIUS = 2
SMOOTH_RADIUS = 3
RIM = BOX_RADIUS + SMOOTH_RADIUS

sigma_smooth = 1.5
step_length = 2.0
var_eps = 1e-05
peak_eps = 1e-06


def smooth_weights(radius):
    raw = [math.exp(-(t * t) / (2.0 * sigma_smooth * sigma_smooth)) for t in range(-radius, radius + 1)]
    total = sum(raw)
    return [one / total for one in raw]


def window_sum(volume, axis_pos, length, weights):
    result = weights[0] * lax.slice_in_dim(volume, 0, length, axis=axis_pos)
    for offset in range(1, len(weights)):
        result = result + weights[offset] * lax.slice_in_dim(volume, offset, offset + length, axis=axis_pos)
    return result


def shift_up(axis):
    n = lax.axis_size(axis)
    return [(i, i + 1) for i in range(n - 1)]


def shift_down(axis):
    n = lax.axis_size(axis)
    return [(i + 1, i) for i in range(n - 1)]


def next_along(a, axis):
    size = a.shape[axis]
    return jnp.concatenate(
        [lax.slice_in_dim(a, 1, size, axis=axis), lax.slice_in_dim(a, size - 1, size, axis=axis)], axis=axis
    )


def request_row(fetch_owner, fetch_block, fetch_count, interp_level):
    blocks, slots = fetch_owner.shape
    in_list = jnp.arange(slots)[None, :] < fetch_count[:, None]
    ids = jnp.where(in_list, fetch_owner * blocks + fetch_block, -1)
    row = jnp.concatenate([ids.reshape(-1), interp_level.reshape(-1), fetch_count.reshape(-1)])
    return jnp.pad(row, (0, 128 - row.shape[0])).astype(jnp.bfloat16)


def coefficients(rows, blocks, slots):
    n = rows.shape[0]
    rows = rows.astype(jnp.float32)
    e = blocks * slots
    ids = rows[:, :e].reshape(n, blocks, slots)
    lev = rows[:, e : 4 * e].reshape(n, blocks, 3, slots)
    count = rows[:, 4 * e : 4 * e + blocks]
    hit = (ids[..., None] == jnp.arange(n * blocks).astype(jnp.float32)).astype(jnp.float32)
    pair = jnp.stack([LEVELS - lev, lev], axis=3)
    wx, wz, wy = pair[:, :, 0], pair[:, :, 1], pair[:, :, 2]
    prod = wz[:, :, :, None, None, :] * wx[:, :, None, :, None, :] * wy[:, :, None, None, :, :]
    c = jnp.sum(prod[..., None] * hit[:, :, None, None, None], axis=5)
    c = c.reshape(n * blocks, 8 * n * blocks)
    hi = jnp.floor(c / 16.0) * 16.0
    both = jnp.concatenate([hi, c - hi], axis=0).astype(jnp.bfloat16)
    return both, (1.0 / count).reshape(n * blocks, 1) / float(LEVELS**3)


def warp(moving_t, row):
    side, _, width = moving_t.shape
    owners = lax.axis_size("blk")
    blocks = width // side
    payload = jnp.concatenate(
        [moving_t, next_along(moving_t, 0), jnp.broadcast_to(row[None, None, :], (side, 2, width))], axis=1
    )
    got = lax.all_to_all(payload, "blk", split_axis=0, concat_axis=0, tiled=True)
    c, scale = coefficients(got[:, 2 * side, :], blocks, 4)
    src = got[:, : 2 * side].reshape(owners, 2, side, blocks, side).transpose(1, 0, 3, 2, 4)
    corners = []
    for dz in range(2):
        for dx in range(2):
            one = src[dz]
            if dx:
                one = next_along(one, 2)
            for dy in range(2):
                corners.append(next_along(one, 3) if dy else one)
    s = jnp.stack(corners).reshape(8 * owners * blocks, side * side)
    acc = jnp.dot(c, s, preferred_element_type=jnp.float32)
    m = owners * blocks
    w = ((acc[:m] + acc[m:]) * scale).astype(jnp.bfloat16)
    w = w.reshape(owners, blocks, side, side).transpose(0, 2, 1, 3).reshape(owners, side, width)
    zero = jnp.zeros((1, RIM, width), jnp.bfloat16)
    before = jnp.concatenate([zero, w[:-1, side - RIM :]], axis=0)
    after = jnp.concatenate([w[1:, :RIM], zero], axis=0)
    w = jnp.concatenate([before, w, after], axis=1)
    return lax.all_to_all(w, "blk", split_axis=0, concat_axis=0, tiled=True)


def per_device(fixed_image, moving_image, fetch_owner, fetch_block, fetch_count, interp_level, block_mask):
    side = fixed_image.shape[0]
    width = fixed_image.shape[2]
    blocks = fetch_count.shape[2]
    ext = side + 2 * RIM
    mid = side + 2 * SMOOTH_RADIUS
    row = request_row(fetch_owner[0, 0], fetch_block[0, 0], fetch_count[0, 0], interp_level[0, 0])
    warped = warp(moving_image.transpose(1, 0, 2), row)

    mask_row = jnp.repeat(block_mask.reshape(blocks), side).astype(jnp.bfloat16)
    fixed_t = fixed_image.transpose(1, 0, 2)
    tail = jnp.concatenate([fixed_t[side - RIM :].reshape(-1, width), mask_row[None]], axis=0)
    head = jnp.concatenate([fixed_t[:RIM].reshape(-1, width), mask_row[None]], axis=0)
    below = lax.ppermute(tail, "slab", shift_up("slab"))
    above = lax.ppermute(head, "slab", shift_down("slab"))
    fixed_z = jnp.concatenate(
        [below[:-1].reshape(RIM, side, width), fixed_t, above[:-1].reshape(RIM, side, width)], axis=0
    )
    masks = jnp.stack([below[-1], mask_row, above[-1]])
    tail = jnp.concatenate([fixed_z[:, side - RIM :].reshape(-1, width), masks], axis=0)
    head = jnp.concatenate([fixed_z[:, :RIM].reshape(-1, width), masks], axis=0)
    left = lax.ppermute(tail, "blk", shift_up("blk"))
    right = lax.ppermute(head, "blk", shift_down("blk"))
    fixed = jnp.concatenate(
        [left[:-3].reshape(ext, RIM, width), fixed_z, right[:-3].reshape(ext, RIM, width)], axis=1
    ).astype(jnp.float32)
    masks = jnp.stack([left[-3:], masks, right[-3:]], axis=1).astype(jnp.float32)
    mask = jnp.repeat(jnp.repeat(masks, jnp.array([SMOOTH_RADIUS, side, SMOOTH_RADIUS]), axis=0, total_repeat_length=mid),
                      jnp.array([SMOOTH_RADIUS, side, SMOOTH_RADIUS]), axis=1, total_repeat_length=mid)

    below = lax.ppermute(warped[side - RIM :], "slab", shift_up("slab"))
    above = lax.ppermute(warped[:RIM], "slab", shift_down("slab"))
    moving = jnp.concatenate([below, warped, above], axis=0).astype(jnp.float32)

    ones = [1.0] * (2 * BOX_RADIUS + 1)
    n = float(len(ones) ** 3)

    def box(a):
        a = window_sum(a, 0, mid, ones)
        a = window_sum(a, 1, mid, ones)
        a = jnp.pad(a, ((0, 0), (0, 0), (BOX_RADIUS, BOX_RADIUS)))
        return window_sum(a, 2, width, ones)

    mean_f = box(fixed) / n
    mean_m = box(moving) / n
    var_f = box(fixed * fixed) / n - mean_f * mean_f + var_eps
    var_m = box(moving * moving) / n - mean_m * mean_m + var_eps
    cov = box(fixed * moving) / n - mean_f * mean_m
    r = BOX_RADIUS
    here = (slice(r, r + mid), slice(r, r + mid))
    grad_z = (moving[r + 1 : r + 1 + mid, here[1]] - moving[r - 1 : r - 1 + mid, here[1]]) * 0.5
    grad_x = (moving[here[0], r + 1 : r + 1 + mid] - moving[here[0], r - 1 : r - 1 + mid]) * 0.5
    padded = jnp.pad(moving[here], ((0, 0), (0, 0), (1, 1)))
    grad_y = (padded[:, :, 2:] - padded[:, :, :-2]) * 0.5
    term = mask * 2.0 * cov / (var_f * var_m) * (fixed[here] - mean_f - cov / var_m * (moving[here] - mean_m))
    force = jnp.stack([term * grad_x, term * grad_z, term * grad_y]).astype(jnp.bfloat16).astype(jnp.float32)
    taps = smooth_weights(SMOOTH_RADIUS)
    s = window_sum(force, 2, side, taps)
    s = window_sum(s, 1, side, taps)
    s = window_sum(jnp.pad(s, ((0, 0), (0, 0), (0, 0), (SMOOTH_RADIUS, SMOOTH_RADIUS))), 3, width, taps)
    peak = jnp.max(jnp.sqrt(s[0] * s[0] + s[1] * s[1] + s[2] * s[2]))
    for axis in ("blk", "slab"):
        tile = jnp.broadcast_to(peak, (lax.axis_size(axis), 1, 128))
        peak = jnp.max(lax.all_to_all(tile, axis, split_axis=0, concat_axis=0, tiled=True))
    return (step_length * s / (peak + peak_eps)).transpose(0, 2, 1, 3)


def solution(mesh):
    in_specs = (
        P("blk", "slab", None),
        P("blk", "slab", None),
        P("blk", "slab", None, None),
        P("blk", "slab", None, None),
        P("blk", "slab", None),
        P("blk", "slab", None, None, None),
        P("blk", "slab", None),
    )
    return jax.shard_map(
        per_device, mesh=mesh, in_specs=in_specs, out_specs=P(None, "blk", "slab", None), check_vma=False
    )
```

```python
import math

import jax
import jax.numpy as jnp
from jax import lax
from jax.experimental import pallas as pl
from jax.experimental.pallas import tpu as pltpu
from jax.sharding import PartitionSpec as P

LEVELS = 8
BOX_RADIUS = 2
SMOOTH_RADIUS = 3
RIM = BOX_RADIUS + SMOOTH_RADIUS

sigma_smooth = 1.5
step_length = 2.0
var_eps = 1e-05
peak_eps = 1e-06


def smooth_weights(radius):
    raw = [math.exp(-(t * t) / (2.0 * sigma_smooth * sigma_smooth)) for t in range(-radius, radius + 1)]
    total = sum(raw)
    return [one / total for one in raw]


def window_sum(volume, axis_pos, length, weights):
    result = weights[0] * lax.slice_in_dim(volume, 0, length, axis=axis_pos)
    for offset in range(1, len(weights)):
        result = result + weights[offset] * lax.slice_in_dim(volume, offset, offset + length, axis=axis_pos)
    return result


def shift_up(axis):
    n = lax.axis_size(axis)
    return [(i, i + 1) for i in range(n - 1)]


def shift_down(axis):
    n = lax.axis_size(axis)
    return [(i + 1, i) for i in range(n - 1)]


SIDE = 32
WIDTH = 128
BLOCKS = WIDTH // SIDE
SLOTS = 4
OWNERS = 32
SENT = 2 * SIDE + 2
PITCH = 72
EXT = SIDE + 2 * RIM
OUT_PITCH = 48


def in_vmem():
    return pl.BlockSpec(memory_space=pltpu.VMEM)


def in_smem():
    return pl.BlockSpec(memory_space=pltpu.SMEM)


def pack_kernel(owner_ref, block_ref, count_ref, level_ref, moving_ref, out_ref, wide):
    lane = lax.broadcasted_iota(jnp.int32, (2, WIDTH), 1)
    row = jnp.zeros((2, WIDTH), jnp.int32)
    e = BLOCKS * SLOTS
    for g in range(BLOCKS):
        count = count_ref[0, 0, g]
        row = jnp.where(lane == 4 * e + g, count, row)
        for k in range(SLOTS):
            name = block_ref[0, 0, g, k] * OWNERS + owner_ref[0, 0, g, k]
            row = jnp.where(lane == g * SLOTS + k, jnp.where(k < count, name, -1), row)
            for axis in range(3):
                at = e + (g * 3 + axis) * SLOTS + k
                row = jnp.where(lane == at, level_ref[0, 0, g, axis, k], row)
    row = row.astype(jnp.float32).astype(jnp.bfloat16)
    for x in range(SIDE):
        wide[pl.ds(x * SIDE, SIDE), :] = moving_ref[x].astype(jnp.float32)
    for z in range(SIDE):
        plane = wide[pl.ds(z, SIDE, stride=SIDE), :].astype(jnp.bfloat16)
        out_ref[z, 0:SIDE, :] = plane
        if z > 0:
            out_ref[z - 1, SIDE : 2 * SIDE, :] = plane
        if z == SIDE - 1:
            out_ref[z, SIDE : 2 * SIDE, :] = plane
        out_ref[z, 2 * SIDE : SENT, :] = row


def pack(owner, block, count, level, moving):
    return pl.pallas_call(
        pack_kernel,
        out_shape=jax.ShapeDtypeStruct((OWNERS, SENT, WIDTH), jnp.bfloat16),
        in_specs=[in_smem()] * 4 + [in_vmem()],
        out_specs=in_vmem(),
        scratch_shapes=[pltpu.VMEM((SIDE * SIDE, WIDTH), jnp.float32)],
        name="pack",
    )(owner, block, count, level, moving)


def exchange_groups(parts, lane):
    turned = [[p] + [pltpu.roll(p, SIDE * s, 1) for s in range(1, BLOCKS)] for p in parts]
    out = []
    for b in range(BLOCKS):
        pick = [turned[a][(a - b) % BLOCKS] for a in range(BLOCKS)]
        out.append(
            jnp.where(
                lane < 2 * SIDE,
                jnp.where(lane < SIDE, pick[0], pick[1]),
                jnp.where(lane < 3 * SIDE, pick[2], pick[3]),
            )
        )
    return out


def hold_kernel(got_ref, out_ref, wide, source, coef, mixed, spread):
    strip = SIDE // BLOCKS
    rows = OWNERS * BLOCKS
    lane = lax.broadcasted_iota(jnp.int32, (OWNERS, WIDTH), 1)
    last_y = lane % SIDE == SIDE - 1
    for o in range(OWNERS):
        wide[pl.ds(o * PITCH, SENT), :] = got_ref[o].astype(jnp.float32)

    lists = wide[pl.ds(2 * SIDE, OWNERS, stride=PITCH), :]
    where_k = lane.astype(jnp.float32)
    e = BLOCKS * SLOTS
    top = float(LEVELS)
    scales = []
    for g in range(BLOCKS):
        total = {}
        for k in range(SLOTS):
            at = g * SLOTS + k
            name = lists[:, at : at + 1]
            base = e + g * 3 * SLOTS + k
            lx, lz, ly = (lists[:, base + a * SLOTS : base + a * SLOTS + 1] for a in range(3))
            hit = jnp.where(where_k == name, 1.0, 0.0)
            for dx in range(2):
                ax = hit * (lx if dx else top - lx)
                for dz in range(2):
                    az = ax * (lz if dz else top - lz)
                    for dy in range(2):
                        ay = az * (ly if dy else top - ly)
                        key = (dx, dz, dy)
                        total[key] = ay if k == 0 else total[key] + ay
        for (dx, dz, dy), c in total.items():
            hi = jnp.floor(c * (1.0 / 16.0)) * 16.0
            col = pl.ds((dz * 2 + dy) * WIDTH, WIDTH)
            coef[dx, pl.ds(g * OWNERS, OWNERS), col] = hi.astype(jnp.bfloat16)
            coef[dx, pl.ds(rows + g * OWNERS, OWNERS), col] = (c - hi).astype(jnp.bfloat16)
        count = lists[:, 4 * e + g : 4 * e + g + 1]
        scales.append((1.0 / count) * (1.0 / LEVELS**3))

    for dz in range(2):
        for t in range(strip):
            parts = [
                wide[pl.ds(dz * SIDE + strip * q + t, OWNERS, stride=PITCH), :] for q in range(BLOCKS)
            ]
            for g, u in enumerate(exchange_groups(parts, lane)):
                v = jnp.where(last_y, u, pltpu.roll(u, WIDTH - 1, 1))
                for dy, a in enumerate((u, v)):
                    r0 = (dz * 2 + dy) * rows + g * OWNERS
                    source[pl.ds(r0, OWNERS), pl.ds(t * WIDTH, WIDTH)] = a.astype(jnp.bfloat16)
    tall = lax.broadcasted_iota(jnp.int32, (rows, WIDTH), 1)
    for i in range(4):
        first = source[pl.ds(i * rows, rows), 0:WIDTH].astype(jnp.float32)
        final = source[pl.ds(i * rows, rows), pl.ds((strip - 1) * WIDTH, WIDTH)].astype(jnp.float32)
        after = jnp.where(tall >= WIDTH - SIDE, final, pltpu.roll(first, WIDTH - SIDE, 1))
        source[pl.ds(i * rows, rows), pl.ds(strip * WIDTH, WIDTH)] = after.astype(jnp.bfloat16)

    piece = 2 * WIDTH
    for n in range(strip * WIDTH // piece):
        acc = jnp.dot(coef[0], source[:, pl.ds(n * piece, piece)], preferred_element_type=jnp.float32)
        acc += jnp.dot(coef[1], source[:, pl.ds(n * piece + WIDTH, piece)], preferred_element_type=jnp.float32)
        for g in range(BLOCKS):
            lo = rows + g * OWNERS
            part = acc[g * OWNERS : (g + 1) * OWNERS] + acc[lo : lo + OWNERS]
            mixed[pl.ds(g * OWNERS, OWNERS), pl.ds(n * piece, piece)] = part * scales[g]

    spread[pl.ds(OUT_PITCH, 8), :] = jnp.zeros((8, WIDTH), jnp.float32)
    spread[pl.ds(OWNERS * OUT_PITCH + SIDE, 16), :] = jnp.zeros((16, WIDTH), jnp.float32)
    for t in range(strip):
        parts = [mixed[pl.ds(g * OWNERS, OWNERS), pl.ds(t * WIDTH, WIDTH)] for g in range(BLOCKS)]
        for q, w in enumerate(exchange_groups(parts, lane)):
            x = strip * q + t
            spread[pl.ds(OUT_PITCH + RIM + x, OWNERS, stride=OUT_PITCH), :] = w
            if x >= SIDE - RIM:
                spread[pl.ds(2 * OUT_PITCH + x - SIDE + RIM, OWNERS, stride=OUT_PITCH), :] = w
            if x < RIM:
                spread[pl.ds(SIDE + RIM + x, OWNERS, stride=OUT_PITCH), :] = w
    for r in range(OWNERS):
        out_ref[r] = spread[pl.ds((r + 1) * OUT_PITCH, EXT), :].astype(jnp.bfloat16)


def hold(got):
    strip = SIDE // BLOCKS
    rows = OWNERS * BLOCKS
    return pl.pallas_call(
        hold_kernel,
        out_shape=jax.ShapeDtypeStruct((OWNERS, EXT, WIDTH), jnp.bfloat16),
        in_specs=[in_vmem()],
        out_specs=in_vmem(),
        scratch_shapes=[
            pltpu.VMEM((OWNERS * PITCH, WIDTH), jnp.float32),
            pltpu.VMEM((4 * rows, (strip + 1) * WIDTH), jnp.bfloat16),
            pltpu.VMEM((2, 2 * rows, 4 * rows), jnp.bfloat16),
            pltpu.VMEM((rows, strip * WIDTH), jnp.float32),
            pltpu.VMEM(((OWNERS + 2) * OUT_PITCH, WIDTH), jnp.float32),
        ],
        name="hold",
    )(got)


def per_device(fixed_image, moving_image, fetch_owner, fetch_block, fetch_count, interp_level, block_mask):
    side = fixed_image.shape[0]
    width = fixed_image.shape[2]
    blocks = fetch_count.shape[2]
    ext = side + 2 * RIM
    mid = side + 2 * SMOOTH_RADIUS
    sent = pack(fetch_owner, fetch_block, fetch_count, interp_level, moving_image)
    got = lax.all_to_all(sent, "blk", split_axis=0, concat_axis=0, tiled=True)
    warped = lax.all_to_all(hold(got), "blk", split_axis=0, concat_axis=0, tiled=True)

    mask_row = jnp.repeat(block_mask.reshape(blocks), side).astype(jnp.bfloat16)
    fixed_t = fixed_image.transpose(1, 0, 2)
    tail = jnp.concatenate([fixed_t[side - RIM :].reshape(-1, width), mask_row[None]], axis=0)
    head = jnp.concatenate([fixed_t[:RIM].reshape(-1, width), mask_row[None]], axis=0)
    below = lax.ppermute(tail, "slab", shift_up("slab"))
    above = lax.ppermute(head, "slab", shift_down("slab"))
    fixed_z = jnp.concatenate(
        [below[:-1].reshape(RIM, side, width), fixed_t, above[:-1].reshape(RIM, side, width)], axis=0
    )
    masks = jnp.stack([below[-1], mask_row, above[-1]])
    tail = jnp.concatenate([fixed_z[:, side - RIM :].reshape(-1, width), masks], axis=0)
    head = jnp.concatenate([fixed_z[:, :RIM].reshape(-1, width), masks], axis=0)
    left = lax.ppermute(tail, "blk", shift_up("blk"))
    right = lax.ppermute(head, "blk", shift_down("blk"))
    fixed = jnp.concatenate(
        [left[:-3].reshape(ext, RIM, width), fixed_z, right[:-3].reshape(ext, RIM, width)], axis=1
    ).astype(jnp.float32)
    masks = jnp.stack([left[-3:], masks, right[-3:]], axis=1).astype(jnp.float32)
    mask = jnp.repeat(jnp.repeat(masks, jnp.array([SMOOTH_RADIUS, side, SMOOTH_RADIUS]), axis=0, total_repeat_length=mid),
                      jnp.array([SMOOTH_RADIUS, side, SMOOTH_RADIUS]), axis=1, total_repeat_length=mid)

    below = lax.ppermute(warped[side - RIM :], "slab", shift_up("slab"))
    above = lax.ppermute(warped[:RIM], "slab", shift_down("slab"))
    moving = jnp.concatenate([below, warped, above], axis=0).astype(jnp.float32)

    ones = [1.0] * (2 * BOX_RADIUS + 1)
    n = float(len(ones) ** 3)

    def box(a):
        a = window_sum(a, 0, mid, ones)
        a = window_sum(a, 1, mid, ones)
        a = jnp.pad(a, ((0, 0), (0, 0), (BOX_RADIUS, BOX_RADIUS)))
        return window_sum(a, 2, width, ones)

    mean_f = box(fixed) / n
    mean_m = box(moving) / n
    var_f = box(fixed * fixed) / n - mean_f * mean_f + var_eps
    var_m = box(moving * moving) / n - mean_m * mean_m + var_eps
    cov = box(fixed * moving) / n - mean_f * mean_m
    r = BOX_RADIUS
    here = (slice(r, r + mid), slice(r, r + mid))
    grad_z = (moving[r + 1 : r + 1 + mid, here[1]] - moving[r - 1 : r - 1 + mid, here[1]]) * 0.5
    grad_x = (moving[here[0], r + 1 : r + 1 + mid] - moving[here[0], r - 1 : r - 1 + mid]) * 0.5
    padded = jnp.pad(moving[here], ((0, 0), (0, 0), (1, 1)))
    grad_y = (padded[:, :, 2:] - padded[:, :, :-2]) * 0.5
    term = mask * 2.0 * cov / (var_f * var_m) * (fixed[here] - mean_f - cov / var_m * (moving[here] - mean_m))
    force = jnp.stack([term * grad_x, term * grad_z, term * grad_y]).astype(jnp.bfloat16).astype(jnp.float32)
    taps = smooth_weights(SMOOTH_RADIUS)
    s = window_sum(force, 2, side, taps)
    s = window_sum(s, 1, side, taps)
    s = window_sum(jnp.pad(s, ((0, 0), (0, 0), (0, 0), (SMOOTH_RADIUS, SMOOTH_RADIUS))), 3, width, taps)
    peak = jnp.max(jnp.sqrt(s[0] * s[0] + s[1] * s[1] + s[2] * s[2]))
    for axis in ("blk", "slab"):
        tile = jnp.broadcast_to(peak, (lax.axis_size(axis), 1, 128))
        peak = jnp.max(lax.all_to_all(tile, axis, split_axis=0, concat_axis=0, tiled=True))
    return (step_length * s / (peak + peak_eps)).transpose(0, 2, 1, 3)


def solution(mesh):
    in_specs = (
        P("blk", "slab", None),
        P("blk", "slab", None),
        P("blk", "slab", None, None),
        P("blk", "slab", None, None),
        P("blk", "slab", None),
        P("blk", "slab", None, None, None),
        P("blk", "slab", None),
    )
    return jax.shard_map(
        per_device, mesh=mesh, in_specs=in_specs, out_specs=P(None, "blk", "slab", None), check_vma=False
    )
```

```python
import math

import jax
import jax.numpy as jnp
from jax import lax
from jax.experimental import pallas as pl
from jax.experimental.pallas import tpu as pltpu
from jax.sharding import PartitionSpec as P


LEVELS = 8
BOX_RADIUS = 2
SMOOTH_RADIUS = 3
RIM = BOX_RADIUS + SMOOTH_RADIUS

sigma_smooth = 1.5
step_length = 2.0
var_eps = 1e-05
peak_eps = 1e-06


def smooth_weights(radius):
    raw = [math.exp(-(t * t) / (2.0 * sigma_smooth * sigma_smooth)) for t in range(-radius, radius + 1)]
    total = sum(raw)
    return [one / total for one in raw]


def shift_up(axis):
    n = lax.axis_size(axis)
    return [(i, i + 1) for i in range(n - 1)]


def shift_down(axis):
    n = lax.axis_size(axis)
    return [(i + 1, i) for i in range(n - 1)]


SIDE = 32
WIDTH = 128
BLOCKS = WIDTH // SIDE
SLOTS = 4
OWNERS = 32
SENT = 2 * SIDE + 2
PITCH = 72
EXT = SIDE + 2 * RIM
OUT_PITCH = 48


MID = SIDE + 2 * SMOOTH_RADIUS
INNER = SIDE - 2 * BOX_RADIUS
CORE = INNER - 2 * SMOOTH_RADIUS
ROW = OUT_PITCH
MIB = 1 << 20


def params(mib):
    return pltpu.CompilerParams(vmem_limit_bytes=mib * MIB)


def cost(flops, nbytes):
    return pl.CostEstimate(flops=flops, bytes_accessed=nbytes, transcendentals=0)


def in_vmem():
    return pl.BlockSpec(memory_space=pltpu.VMEM)


def in_smem():
    return pl.BlockSpec(memory_space=pltpu.SMEM)


def pack_kernel(owner_ref, block_ref, count_ref, level_ref, moving_ref, out_ref, wide):
    lane = lax.broadcasted_iota(jnp.int32, (2, WIDTH), 1)
    row = jnp.zeros((2, WIDTH), jnp.int32)
    e = BLOCKS * SLOTS
    for g in range(BLOCKS):
        count = count_ref[0, 0, g]
        row = jnp.where(lane == 4 * e + g, count, row)
        for k in range(SLOTS):
            name = block_ref[0, 0, g, k] * OWNERS + owner_ref[0, 0, g, k]
            row = jnp.where(lane == g * SLOTS + k, jnp.where(k < count, name, -1), row)
            for axis in range(3):
                at = e + (g * 3 + axis) * SLOTS + k
                row = jnp.where(lane == at, level_ref[0, 0, g, axis, k], row)
    row = row.astype(jnp.float32).astype(jnp.bfloat16)
    for x in range(SIDE):
        wide[pl.ds(x * SIDE, SIDE), :] = moving_ref[x].astype(jnp.float32)
    for z in range(SIDE):
        plane = wide[pl.ds(z, SIDE, stride=SIDE), :].astype(jnp.bfloat16)
        out_ref[z, 0:SIDE, :] = plane
        if z > 0:
            out_ref[z - 1, SIDE : 2 * SIDE, :] = plane
        if z == SIDE - 1:
            out_ref[z, SIDE : 2 * SIDE, :] = plane
        out_ref[z, 2 * SIDE : SENT, :] = row


def pack(owner, block, count, level, moving):
    return pl.pallas_call(
        pack_kernel,
        out_shape=jax.ShapeDtypeStruct((OWNERS, SENT, WIDTH), jnp.bfloat16),
        in_specs=[in_smem()] * 4 + [in_vmem()],
        out_specs=in_vmem(),
        scratch_shapes=[pltpu.VMEM((SIDE * SIDE, WIDTH), jnp.float32)],
        compiler_params=params(8),
        name="pack",
    )(owner, block, count, level, moving)


def exchange_groups(parts, lane):
    turned = [[p] + [pltpu.roll(p, SIDE * s, 1) for s in range(1, BLOCKS)] for p in parts]
    out = []
    for b in range(BLOCKS):
        pick = [turned[a][(a - b) % BLOCKS] for a in range(BLOCKS)]
        out.append(
            jnp.where(
                lane < 2 * SIDE,
                jnp.where(lane < SIDE, pick[0], pick[1]),
                jnp.where(lane < 3 * SIDE, pick[2], pick[3]),
            )
        )
    return out


def hold_kernel(got_ref, out_ref, wide, source, coef, mixed, spread):
    strip = SIDE // BLOCKS
    rows = OWNERS * BLOCKS
    lane = lax.broadcasted_iota(jnp.int32, (OWNERS, WIDTH), 1)
    last_y = lane % SIDE == SIDE - 1
    for o in range(OWNERS):
        wide[pl.ds(o * PITCH, SENT), :] = got_ref[o].astype(jnp.float32)

    lists = wide[pl.ds(2 * SIDE, OWNERS, stride=PITCH), :]
    where_k = lane.astype(jnp.float32)
    e = BLOCKS * SLOTS
    top = float(LEVELS)
    scales = []
    for g in range(BLOCKS):
        total = {}
        for k in range(SLOTS):
            at = g * SLOTS + k
            name = lists[:, at : at + 1]
            base = e + g * 3 * SLOTS + k
            lx, lz, ly = (lists[:, base + a * SLOTS : base + a * SLOTS + 1] for a in range(3))
            hit = jnp.where(where_k == name, 1.0, 0.0)
            for dx in range(2):
                ax = hit * (lx if dx else top - lx)
                for dz in range(2):
                    az = ax * (lz if dz else top - lz)
                    for dy in range(2):
                        ay = az * (ly if dy else top - ly)
                        key = (dx, dz, dy)
                        total[key] = ay if k == 0 else total[key] + ay
        for (dx, dz, dy), c in total.items():
            hi = jnp.floor(c * (1.0 / 16.0)) * 16.0
            col = pl.ds((dz * 2 + dy) * WIDTH, WIDTH)
            coef[dx, pl.ds(g * OWNERS, OWNERS), col] = hi.astype(jnp.bfloat16)
            coef[dx, pl.ds(rows + g * OWNERS, OWNERS), col] = (c - hi).astype(jnp.bfloat16)
        count = lists[:, 4 * e + g : 4 * e + g + 1]
        scales.append((1.0 / count) * (1.0 / LEVELS**3))

    for dz in range(2):
        for t in range(strip):
            parts = [
                wide[pl.ds(dz * SIDE + strip * q + t, OWNERS, stride=PITCH), :] for q in range(BLOCKS)
            ]
            for g, u in enumerate(exchange_groups(parts, lane)):
                v = jnp.where(last_y, u, pltpu.roll(u, WIDTH - 1, 1))
                for dy, a in enumerate((u, v)):
                    r0 = (dz * 2 + dy) * rows + g * OWNERS
                    source[pl.ds(r0, OWNERS), pl.ds(t * WIDTH, WIDTH)] = a.astype(jnp.bfloat16)
    tall = lax.broadcasted_iota(jnp.int32, (rows, WIDTH), 1)
    for i in range(4):
        first = source[pl.ds(i * rows, rows), 0:WIDTH].astype(jnp.float32)
        final = source[pl.ds(i * rows, rows), pl.ds((strip - 1) * WIDTH, WIDTH)].astype(jnp.float32)
        after = jnp.where(tall >= WIDTH - SIDE, final, pltpu.roll(first, WIDTH - SIDE, 1))
        source[pl.ds(i * rows, rows), pl.ds(strip * WIDTH, WIDTH)] = after.astype(jnp.bfloat16)

    piece = 2 * WIDTH
    for n in range(strip * WIDTH // piece):
        acc = jnp.dot(coef[0], source[:, pl.ds(n * piece, piece)], preferred_element_type=jnp.float32)
        acc += jnp.dot(coef[1], source[:, pl.ds(n * piece + WIDTH, piece)], preferred_element_type=jnp.float32)
        for g in range(BLOCKS):
            lo = rows + g * OWNERS
            part = acc[g * OWNERS : (g + 1) * OWNERS] + acc[lo : lo + OWNERS]
            mixed[pl.ds(g * OWNERS, OWNERS), pl.ds(n * piece, piece)] = part * scales[g]

    spread[pl.ds(OUT_PITCH, 8), :] = jnp.zeros((8, WIDTH), jnp.float32)
    spread[pl.ds(OWNERS * OUT_PITCH + SIDE, 16), :] = jnp.zeros((16, WIDTH), jnp.float32)
    for i in range(EXT, OUT_PITCH):
        spread[pl.ds(OUT_PITCH + i, OWNERS, stride=OUT_PITCH), :] = jnp.zeros((OWNERS, WIDTH), jnp.float32)
    for t in range(strip):
        parts = [mixed[pl.ds(g * OWNERS, OWNERS), pl.ds(t * WIDTH, WIDTH)] for g in range(BLOCKS)]
        for q, w in enumerate(exchange_groups(parts, lane)):
            x = strip * q + t
            spread[pl.ds(OUT_PITCH + RIM + x, OWNERS, stride=OUT_PITCH), :] = w
            if x >= SIDE - RIM:
                spread[pl.ds(2 * OUT_PITCH + x - SIDE + RIM, OWNERS, stride=OUT_PITCH), :] = w
            if x < RIM:
                spread[pl.ds(SIDE + RIM + x, OWNERS, stride=OUT_PITCH), :] = w
    for r in range(OWNERS):
        out_ref[r] = spread[pl.ds((r + 1) * OUT_PITCH, OUT_PITCH), :].astype(jnp.bfloat16)


def hold(got):
    strip = SIDE // BLOCKS
    rows = OWNERS * BLOCKS
    return pl.pallas_call(
        hold_kernel,
        out_shape=jax.ShapeDtypeStruct((OWNERS, OUT_PITCH, WIDTH), jnp.bfloat16),
        in_specs=[in_vmem()],
        out_specs=in_vmem(),
        scratch_shapes=[
            pltpu.VMEM((OWNERS * PITCH, WIDTH), jnp.float32),
            pltpu.VMEM((4 * rows, (strip + 1) * WIDTH), jnp.bfloat16),
            pltpu.VMEM((2, 2 * rows, 4 * rows), jnp.bfloat16),
            pltpu.VMEM((rows, strip * WIDTH), jnp.float32),
            pltpu.VMEM(((OWNERS + 2) * OUT_PITCH, WIDTH), jnp.float32),
        ],
        compiler_params=params(16),
        name="hold",
    )(got)


def distance():
    i = lax.broadcasted_iota(jnp.int32, (WIDTH, WIDTH), 0)
    j = lax.broadcasted_iota(jnp.int32, (WIDTH, WIDTH), 1)
    return jnp.abs(i - j)


def box_band():
    one = jnp.where(distance() <= BOX_RADIUS, 1.0, 0.0).astype(jnp.bfloat16)
    return one, jnp.concatenate([one, one], axis=0)


def smooth_band():
    d = distance()
    taps = smooth_weights(SMOOTH_RADIUS)
    left = jnp.zeros((WIDTH, WIDTH), jnp.float32)
    for t in range(SMOOTH_RADIUS + 1):
        left = jnp.where(d == t, taps[SMOOTH_RADIUS + t], left)
    parts = []
    for _ in range(3):
        part = left.astype(jnp.bfloat16)
        parts.append(part)
        left = left - part.astype(jnp.float32)
    return jnp.concatenate(parts, axis=0)


def times(a, band):
    return jnp.dot(a, band, preferred_element_type=jnp.float32)


def halves(product):
    hi = product.astype(jnp.bfloat16)
    return jnp.concatenate([hi, (product - hi.astype(jnp.float32)).astype(jnp.bfloat16)], axis=1)


def rows_at(i):
    if isinstance(i, int):
        return pl.ds(i * ROW, ROW)
    return pl.ds(pl.multiple_of(i * ROW, ROW), ROW)


def along(a, step):
    return pltpu.roll(a, (-step) % ROW, 0)


def box_zx(ref, which, i):
    r = [ref[which, rows_at(i + t), :] for t in range(2 * BOX_RADIUS + 1)]
    a = ((r[0] + r[1]) + (r[2] + r[3])) + r[4]
    two = a + along(a, -1)
    return ((along(two, -1) + a) + along(two, 2)) * (1.0 / (2 * BOX_RADIUS + 1) ** 3)


def fixed_kernel(fixed_ref, mask_ref, mean_ref, away_ref, gain_ref, sums):
    one, twice = box_band()
    chunk = 3 * ROW

    def by_y(i, carry):
        rows = pl.ds(pl.multiple_of(i * chunk, chunk), chunk)
        f = fixed_ref[rows, :]
        sums[0, rows, :] = times(f, one)
        wide = f.astype(jnp.float32)
        sums[1, rows, :] = times(halves(wide * wide), twice)
        return carry

    lax.fori_loop(0, EXT // 3, by_y, 0)

    def by_z(i, carry):
        mean = box_zx(sums, 0, i)
        var = box_zx(sums, 1, i) - mean * mean + var_eps
        part = jnp.where(i < SMOOTH_RADIUS, 0, jnp.where(i < SMOOTH_RADIUS + SIDE, 1, 2))
        mean_ref[rows_at(i), :] = mean
        away_ref[rows_at(i), :] = fixed_ref[rows_at(i + BOX_RADIUS), :].astype(jnp.float32) - mean
        gain_ref[rows_at(i), :] = mask_ref[rows_at(part), :] * 2.0 / var
        return carry

    lax.fori_loop(0, MID, by_z, 0)


def fixed_part(fixed, mask):
    out = jax.ShapeDtypeStruct((MID * ROW, WIDTH), jnp.float32)
    return pl.pallas_call(
        fixed_kernel,
        out_shape=[out] * 3,
        in_specs=[in_vmem()] * 2,
        out_specs=[in_vmem()] * 3,
        scratch_shapes=[pltpu.VMEM((2, EXT * ROW, WIDTH), jnp.float32)],
        compiler_params=params(12),
        cost_estimate=cost(5_000_000_000, 4_000_000),
        name="fixed_part",
    )(fixed, mask)


def sums_by_y(m, f, wide, sums, rows, bands):
    mw = m.astype(jnp.float32)
    wide[rows, :] = mw
    sums[0, rows, :] = times(m, bands[0])
    sums[1, rows, :] = times(halves(mw * mw), bands[1])
    sums[2, rows, :] = times(halves(mw * f.astype(jnp.float32)), bands[1])


def force_row(wide, sums, i, mean_ref, away_ref, gain_ref, j, force, k):
    mean = box_zx(sums, 0, i)
    var = box_zx(sums, 1, i) - mean * mean + var_eps
    cov = box_zx(sums, 2, i) - mean_ref[rows_at(j), :] * mean
    q = cov / var
    m = wide[rows_at(i + BOX_RADIUS), :]
    term = (0.5 * gain_ref[rows_at(j), :]) * q * (away_ref[rows_at(j), :] - q * (m - mean))
    lane = lax.broadcasted_iota(jnp.int32, (ROW, WIDTH), 1)
    up = jnp.where(lane == WIDTH - 1, 0.0, pltpu.roll(m, WIDTH - 1, 1))
    down = jnp.where(lane == 0, 0.0, pltpu.roll(m, 1, 1))
    force[0, rows_at(k), :] = (term * (along(m, 1) - along(m, -1))).astype(jnp.bfloat16)
    z_step = wide[rows_at(i + BOX_RADIUS + 1), :] - wide[rows_at(i + BOX_RADIUS - 1), :]
    force[1, rows_at(k), :] = (term * z_step).astype(jnp.bfloat16)
    force[2, rows_at(k), :] = (term * (up - down)).astype(jnp.bfloat16)


def smooth_row(smooth_y, i, out_ref, z, peak):
    taps = smooth_weights(SMOOTH_RADIUS)[SMOOTH_RADIUS:]
    total = None
    for c in range(3):
        g = [smooth_y[c, rows_at(i + t), :] for t in range(2 * SMOOTH_RADIUS + 1)]
        mid = SMOOTH_RADIUS
        s = taps[0] * g[mid]
        for t in range(1, SMOOTH_RADIUS + 1):
            s += taps[t] * (g[mid - t] + g[mid + t])
        a = taps[0] * along(s, RIM)
        for t in range(1, SMOOTH_RADIUS + 1):
            a += taps[t] * (along(s, RIM - t) + along(s, RIM + t))
        a = a[:SIDE]
        at = (c * SIDE + z) * SIDE
        out_ref[pl.ds(at if isinstance(at, int) else pl.multiple_of(at, SIDE), SIDE), :] = a
        total = a * a if total is None else total + a * a
    return jnp.maximum(peak, total)


def inner_kernel(warped_ref, fixed_ref, mean_ref, away_ref, gain_ref, out_ref, edge_ref, peak_ref, wide, sums, force, smooth_y):
    bands = box_band()
    triple = smooth_band()
    chunk = 4 * ROW

    def by_y(i, carry):
        rows = pl.ds(pl.multiple_of(i * chunk, chunk), chunk)
        f = fixed_ref[pl.ds(pl.multiple_of(i * chunk + RIM * ROW, ROW), chunk), :]
        sums_by_y(warped_ref[rows, :], f, wide, sums, rows, bands)
        return carry

    lax.fori_loop(0, SIDE // 4, by_y, 0)

    def by_z(i, carry):
        force_row(wide, sums, i, mean_ref, away_ref, gain_ref, i + RIM, force, i)
        return carry

    lax.fori_loop(0, INNER, by_z, 0)

    def smooth(i, carry):
        rows = pl.ds(pl.multiple_of(i * chunk, chunk), chunk)
        for c in range(3):
            f = force[c, rows, :]
            smooth_y[c, rows, :] = times(jnp.concatenate([f, f, f], axis=1), triple)
        return carry

    lax.fori_loop(0, INNER // 4, smooth, 0)
    kept = 2 * SMOOTH_RADIUS * ROW
    for c in range(3):
        edge_ref[c, 0:kept, :] = smooth_y[c, 0:kept, :]
        edge_ref[c, kept : 2 * kept, :] = smooth_y[c, INNER * ROW - kept : INNER * ROW, :]
    peak_ref[...] = lax.fori_loop(
        0, CORE, lambda i, peak: smooth_row(smooth_y, i, out_ref, i + RIM, peak), jnp.zeros((SIDE, WIDTH), jnp.float32)
    )


def rim_kernel(below_ref, above_ref, warped_ref, fixed_ref, mean_ref, away_ref, gain_ref, edge_ref, first_ref, out_ref, peak_ref, wide, sums, force, smooth_y):
    bands = box_band()
    triple = smooth_band()
    own = RIM - 1
    stack = RIM + own
    for ref, start, count, at, f_at in (
        (below_ref, 0, RIM, 0, 0),
        (warped_ref, 0, own, RIM, RIM),
        (warped_ref, SIDE - own, own, stack, RIM + SIDE - own),
        (above_ref, 0, RIM, stack + own, RIM + SIDE),
    ):
        m = ref[pl.ds(start * ROW, count * ROW), :]
        f = fixed_ref[pl.ds(f_at * ROW, count * ROW), :]
        sums_by_y(m, f, wide, sums, pl.ds(at * ROW, count * ROW), bands)

    def by_z(i, carry):
        side = jnp.where(i < RIM, 0, 1)
        j = i - RIM * side
        force_row(wide, sums, stack * side + j, mean_ref, away_ref, gain_ref, (MID - RIM) * side + j, force, i)
        return carry

    lax.fori_loop(0, 2 * RIM, by_z, 0)
    kept = 2 * SMOOTH_RADIUS
    tall = RIM + kept
    for c in range(3):
        for side in range(2):
            f = force[c, pl.ds(side * RIM * ROW, RIM * ROW), :]
            new = (side * tall + (kept if side else 0)) * ROW
            smooth_y[c, pl.ds(new, RIM * ROW), :] = times(jnp.concatenate([f, f, f], axis=1), triple)
            old = (side * tall + (0 if side else RIM)) * ROW
            smooth_y[c, pl.ds(old, kept * ROW), :] = edge_ref[c, pl.ds(side * kept * ROW, kept * ROW), :]

    def smooth(i, peak):
        side = jnp.where(i < RIM, 0, 1)
        j = i - RIM * side
        return smooth_row(smooth_y, tall * side + j, out_ref, (SIDE - RIM) * side + j, peak)

    peak = lax.fori_loop(0, 2 * RIM, smooth, first_ref[...])
    top = jnp.max(jnp.max(peak, axis=0, keepdims=True), axis=1, keepdims=True)
    peak_ref[...] = jnp.broadcast_to(top.reshape(1, 1, 1), peak_ref.shape)


def inner(warped, fixed, mean, away, gain):
    return pl.pallas_call(
        inner_kernel,
        out_shape=[
            jax.ShapeDtypeStruct((3 * SIDE * SIDE, WIDTH), jnp.float32),
            jax.ShapeDtypeStruct((3, 4 * SMOOTH_RADIUS * ROW, WIDTH), jnp.float32),
            jax.ShapeDtypeStruct((SIDE, WIDTH), jnp.float32),
        ],
        in_specs=[in_vmem()] * 5,
        out_specs=[in_vmem()] * 3,
        scratch_shapes=[
            pltpu.VMEM((SIDE * ROW, WIDTH), jnp.float32),
            pltpu.VMEM((3, SIDE * ROW, WIDTH), jnp.float32),
            pltpu.VMEM((3, INNER * ROW, WIDTH), jnp.bfloat16),
            pltpu.VMEM((3, INNER * ROW, WIDTH), jnp.float32),
        ],
        compiler_params=params(20),
        cost_estimate=cost(10_000_000_000, 8_000_000),
        name="inner",
    )(warped, fixed, mean, away, gain)


def rim(below, above, warped, fixed, mean, away, gain, edge, first):
    stack = 2 * (2 * RIM - 1) * ROW
    tall = 2 * (RIM + 2 * SMOOTH_RADIUS) * ROW
    return pl.pallas_call(
        rim_kernel,
        out_shape=[
            jax.ShapeDtypeStruct((3 * SIDE * SIDE, WIDTH), jnp.float32),
            jax.ShapeDtypeStruct((OWNERS, 1, WIDTH), jnp.float32),
        ],
        in_specs=[in_vmem()] * 9,
        out_specs=[in_vmem()] * 2,
        scratch_shapes=[
            pltpu.VMEM((stack, WIDTH), jnp.float32),
            pltpu.VMEM((3, stack, WIDTH), jnp.float32),
            pltpu.VMEM((3, 2 * RIM * ROW, WIDTH), jnp.bfloat16),
            pltpu.VMEM((3, tall, WIDTH), jnp.float32),
        ],
        compiler_params=params(20),
        name="rim",
    )(below, above, warped, fixed, mean, away, gain, edge, first)


def relay_kernel(in_ref, out_ref):
    a = jnp.max(in_ref[...].reshape(in_ref.shape[0], WIDTH), axis=0, keepdims=True)
    out_ref[...] = jnp.broadcast_to(a.reshape(1, 1, WIDTH), out_ref.shape)


def relay(tiles, count):
    return pl.pallas_call(
        relay_kernel,
        out_shape=jax.ShapeDtypeStruct((count, 1, WIDTH), jnp.float32),
        in_specs=[in_vmem()],
        out_specs=in_vmem(),
        compiler_params=params(1),
        name="relay",
    )(tiles)


STEP_X = 8


def finish_kernel(peaks_ref, core_ref, rim_ref, out_ref):
    x0 = pl.program_id(0) * STEP_X
    peak = jnp.sqrt(jnp.max(peaks_ref[...].reshape(peaks_ref.shape[0], WIDTH), axis=0, keepdims=True))
    scale = step_length / (peak + peak_eps)
    z = lax.broadcasted_iota(jnp.int32, (SIDE, WIDTH), 0)
    at_rim = (z < RIM) | (z >= SIDE - RIM)
    for c in range(3):
        for x in range(STEP_X):
            rows = pl.ds(c * SIDE * SIDE + x0 + x, SIDE, stride=SIDE)
            out_ref[c, x] = jnp.where(at_rim, rim_ref[rows, :], core_ref[rows, :]) * scale


def finish(peaks, core, rims):
    return pl.pallas_call(
        finish_kernel,
        out_shape=jax.ShapeDtypeStruct((3, SIDE, SIDE, WIDTH), jnp.float32),
        grid=(SIDE // STEP_X,),
        in_specs=[in_vmem()] * 3,
        out_specs=pl.BlockSpec((3, STEP_X, SIDE, WIDTH), lambda i: (0, i, 0, 0)),
        compiler_params=params(12),
        name="finish",
    )(peaks, core, rims)


def per_device(fixed_image, moving_image, fetch_owner, fetch_block, fetch_count, interp_level, block_mask):
    side, width, ext = SIDE, WIDTH, EXT
    sent = pack(fetch_owner, fetch_block, fetch_count, interp_level, moving_image)
    got = lax.all_to_all(sent, "blk", split_axis=0, concat_axis=0, tiled=True)

    mask_row = jnp.repeat(block_mask.reshape(BLOCKS), side).astype(jnp.bfloat16)
    fixed_t = fixed_image.transpose(1, 0, 2)
    tail = jnp.concatenate([fixed_t[side - RIM :].reshape(-1, width), mask_row[None]], axis=0)
    head = jnp.concatenate([fixed_t[:RIM].reshape(-1, width), mask_row[None]], axis=0)
    below = lax.ppermute(tail, "slab", shift_up("slab"))
    above = lax.ppermute(head, "slab", shift_down("slab"))
    fixed_z = jnp.concatenate(
        [below[:-1].reshape(RIM, side, width), fixed_t, above[:-1].reshape(RIM, side, width)], axis=0
    )
    masks = jnp.stack([below[-1], mask_row, above[-1]])

    held = hold(got)
    fixed_z, masks, _ = lax.optimization_barrier((fixed_z, masks, held))
    warped = lax.all_to_all(held, "blk", split_axis=0, concat_axis=0, tiled=True)

    tail = jnp.concatenate([fixed_z[:, side - RIM :].reshape(-1, width), masks], axis=0)
    head = jnp.concatenate([fixed_z[:, :RIM].reshape(-1, width), masks], axis=0)
    left = lax.ppermute(tail, "blk", shift_up("blk"))
    right = lax.ppermute(head, "blk", shift_down("blk"))
    fixed = jnp.concatenate(
        [
            left[:-3].reshape(ext, RIM, width),
            fixed_z,
            right[:-3].reshape(ext, RIM, width),
            jnp.zeros((ext, ROW - ext, width), jnp.bfloat16),
        ],
        axis=1,
    ).reshape(ext * ROW, width)
    spread_x = lambda a, n: jnp.broadcast_to(a[:, None], (3, n, width)).astype(jnp.float32)
    mask = jnp.concatenate(
        [
            jnp.zeros((3, BOX_RADIUS, width), jnp.float32),
            spread_x(left[-3:], SMOOTH_RADIUS),
            spread_x(masks, side),
            spread_x(right[-3:], SMOOTH_RADIUS),
            jnp.zeros((3, ROW - MID - BOX_RADIUS, width), jnp.float32),
        ],
        axis=1,
    ).reshape(3 * ROW, width)
    mean, away, gain = fixed_part(fixed, mask)

    below = lax.ppermute(warped[side - RIM :], "slab", shift_up("slab"))
    above = lax.ppermute(warped[:RIM], "slab", shift_down("slab"))
    flat = warped.reshape(side * ROW, width)
    core, edge, first = inner(flat, fixed, mean, away, gain)
    rims, peak = rim(
        below.reshape(RIM * ROW, width), above.reshape(RIM * ROW, width), flat, fixed, mean, away, gain, edge, first
    )
    peak = lax.all_to_all(peak, "blk", split_axis=0, concat_axis=0, tiled=True)
    peak = relay(peak, lax.axis_size("slab"))
    peak = lax.all_to_all(peak, "slab", split_axis=0, concat_axis=0, tiled=True)
    return finish(peak, core, rims)


def solution(mesh):
    in_specs = (
        P("blk", "slab", None),
        P("blk", "slab", None),
        P("blk", "slab", None, None),
        P("blk", "slab", None, None),
        P("blk", "slab", None),
        P("blk", "slab", None, None, None),
        P("blk", "slab", None),
    )
    return jax.shard_map(
        per_device, mesh=mesh, in_specs=in_specs, out_specs=P(None, "blk", "slab", None), check_vma=False
    )
```

```python
import math

import jax
import jax.numpy as jnp
from jax import lax
from jax.experimental import pallas as pl
from jax.experimental.pallas import tpu as pltpu
from jax.sharding import PartitionSpec as P

LEVELS = 8
BOX_RADIUS = 2
SMOOTH_RADIUS = 3
RIM = BOX_RADIUS + SMOOTH_RADIUS

sigma_smooth = 1.5
step_length = 2.0
var_eps = 1e-05
peak_eps = 1e-06


def smooth_weights(radius):
    raw = [math.exp(-(t * t) / (2.0 * sigma_smooth * sigma_smooth)) for t in range(-radius, radius + 1)]
    total = sum(raw)
    return [one / total for one in raw]


def shift_up(axis):
    n = lax.axis_size(axis)
    return [(i, i + 1) for i in range(n - 1)]


def shift_down(axis):
    n = lax.axis_size(axis)
    return [(i + 1, i) for i in range(n - 1)]


SIDE = 32
WIDTH = 128
BLOCKS = WIDTH // SIDE
SLOTS = 4
OWNERS = 32
DEEP = 2
HALF = SIDE // 2
TAKEN = DEEP + 1
SENT = TAKEN * HALF + TAKEN + 1
PITCH = 56
EXT = SIDE + 2 * RIM
OUT_PITCH = 48
PART = OUT_PITCH // DEEP
MID = SIDE + 2 * SMOOTH_RADIUS
INNER = SIDE - 2 * BOX_RADIUS
CORE = INNER - 2 * SMOOTH_RADIUS
ROW = OUT_PITCH
MIB = 1 << 20


def params(mib):
    return pltpu.CompilerParams(vmem_limit_bytes=mib * MIB)


def cost(flops, nbytes):
    return pl.CostEstimate(flops=flops, bytes_accessed=nbytes, transcendentals=0)


def in_vmem():
    return pl.BlockSpec(memory_space=pltpu.VMEM)


def in_smem():
    return pl.BlockSpec(memory_space=pltpu.SMEM)


def pack_kernel(owner_ref, block_ref, count_ref, level_ref, moving_ref, out_ref, wide):
    lane = lax.broadcasted_iota(jnp.int32, (TAKEN + 1, WIDTH), 1)
    row = jnp.zeros((TAKEN + 1, WIDTH), jnp.int32)
    e = BLOCKS * SLOTS
    for g in range(BLOCKS):
        count = count_ref[0, 0, g]
        row = jnp.where(lane == 4 * e + g, count, row)
        for k in range(SLOTS):
            name = block_ref[0, 0, g, k] * OWNERS + owner_ref[0, 0, g, k]
            row = jnp.where(lane == g * SLOTS + k, jnp.where(k < count, name, -1), row)
            for axis in range(3):
                at = e + (g * 3 + axis) * SLOTS + k
                row = jnp.where(lane == at, level_ref[0, 0, g, axis, k], row)
    row = row.astype(jnp.float32)
    for x in range(SIDE):
        wide[pl.ds(x * SIDE, SIDE), :] = moving_ref[x].astype(jnp.float32)
    place = lax.broadcasted_iota(jnp.int32, (TAKEN + 1, WIDTH), 0)
    for z in range(SIDE):
        plane = wide[pl.ds(z, SIDE, stride=SIDE), :].astype(jnp.bfloat16)
        spots = [(z // DEEP, z % DEEP)]
        if z % DEEP == 0 and z > 0:
            spots.append((z // DEEP - 1, DEEP))
        if z == SIDE - 1:
            spots.append((z // DEEP, DEEP))
        for pair, at in spots:
            for half in range(2):
                out_ref[pair * 2 + half, at * HALF : (at + 1) * HALF, :] = plane[half * HALF : (half + 1) * HALF]
    for pair in range(SIDE // DEEP):
        for half in range(2):
            x = min((half + 1) * HALF, SIDE - 1)
            if pair < SIDE // DEEP - 1:
                extra = wide[pl.ds(x * SIDE + pair * DEEP, TAKEN + 1), :]
            else:
                two = wide[pl.ds(x * SIDE + pair * DEEP, DEEP), :]
                extra = jnp.concatenate([two, two[1:2], two[1:2]], axis=0)
            extra = jnp.where(place == TAKEN, row, extra)
            out_ref[pair * 2 + half, TAKEN * HALF : SENT, :] = extra.astype(jnp.bfloat16)


def pack(owner, block, count, level, moving):
    return pl.pallas_call(
        pack_kernel,
        out_shape=jax.ShapeDtypeStruct((OWNERS, SENT, WIDTH), jnp.bfloat16),
        in_specs=[in_smem()] * 4 + [in_vmem()],
        out_specs=in_vmem(),
        scratch_shapes=[pltpu.VMEM((SIDE * SIDE, WIDTH), jnp.float32)],
        name="pack",
    )(owner, block, count, level, moving)


def exchange_groups(parts, lane):
    turned = [[p] + [pltpu.roll(p, SIDE * s, 1) for s in range(1, BLOCKS)] for p in parts]
    out = []
    for b in range(BLOCKS):
        pick = [turned[a][(a - b) % BLOCKS] for a in range(BLOCKS)]
        out.append(
            jnp.where(
                lane < 2 * SIDE,
                jnp.where(lane < SIDE, pick[0], pick[1]),
                jnp.where(lane < 3 * SIDE, pick[2], pick[3]),
            )
        )
    return out


def hold_kernel(half_ref, got_ref, out_ref, wide, source, coef, mixed, spread):
    strip = HALF // BLOCKS
    rows = OWNERS * BLOCKS
    lane = lax.broadcasted_iota(jnp.int32, (OWNERS, WIDTH), 1)
    last_y = lane % SIDE == SIDE - 1
    for o in range(OWNERS):
        wide[pl.ds(o * PITCH, SENT), :] = got_ref[o].astype(jnp.float32)

    lists = wide[pl.ds(SENT - 1, OWNERS, stride=PITCH), :]
    where_k = lane.astype(jnp.float32)
    e = BLOCKS * SLOTS
    top = float(LEVELS)
    scales = []
    for g in range(BLOCKS):
        total = {}
        for k in range(SLOTS):
            at = g * SLOTS + k
            name = lists[:, at : at + 1]
            base = e + g * 3 * SLOTS + k
            lx, lz, ly = (lists[:, base + a * SLOTS : base + a * SLOTS + 1] for a in range(3))
            hit = jnp.where(where_k == name, 1.0, 0.0)
            for dx in range(2):
                ax = hit * (lx if dx else top - lx)
                for dz in range(2):
                    az = ax * (lz if dz else top - lz)
                    for dy in range(2):
                        ay = az * (ly if dy else top - ly)
                        key = (dx, dz, dy)
                        total[key] = ay if k == 0 else total[key] + ay
        for (dx, dz, dy), c in total.items():
            hi = jnp.floor(c * (1.0 / 16.0)) * 16.0
            col = pl.ds(dy * WIDTH, WIDTH)
            coef[dz * 2 + dx, pl.ds(g * OWNERS, OWNERS), col] = hi.astype(jnp.bfloat16)
            coef[dz * 2 + dx, pl.ds(rows + g * OWNERS, OWNERS), col] = (c - hi).astype(jnp.bfloat16)
        count = lists[:, 4 * e + g : 4 * e + g + 1]
        scales.append((1.0 / count) * (1.0 / LEVELS**3))

    wrap = strip + 1
    for z in range(TAKEN):
        for t in range(wrap):
            at = [strip * q + t for q in range(BLOCKS)]
            parts = [
                wide[pl.ds(z * HALF + x if x < HALF else TAKEN * HALF + z, OWNERS, stride=PITCH), :] for x in at
            ]
            for g, u in enumerate(exchange_groups(parts, lane)):
                v = jnp.where(last_y, u, pltpu.roll(u, WIDTH - 1, 1))
                for dy, a in enumerate((u, v)):
                    source[pl.ds(dy * rows + g * OWNERS, OWNERS), pl.ds((z * wrap + t) * WIDTH, WIDTH)] = a.astype(
                        jnp.bfloat16
                    )

    piece = 2 * WIDTH
    for z in range(DEEP):
        for t in range(0, strip, 2):
            acc = None
            for dz in range(2):
                for dx in range(2):
                    col = ((z + dz) * wrap + t + dx) * WIDTH
                    one = jnp.dot(
                        coef[dz * 2 + dx], source[:, pl.ds(col, piece)], preferred_element_type=jnp.float32
                    )
                    acc = one if acc is None else acc + one
            for g in range(BLOCKS):
                lo = rows + g * OWNERS
                part = acc[g * OWNERS : (g + 1) * OWNERS] + acc[lo : lo + OWNERS]
                mixed[pl.ds(g * OWNERS, OWNERS), pl.ds((z * strip + t) * WIDTH, piece)] = part * scales[g]

    for r in range(OWNERS):
        for z in range(DEEP):
            spread[pl.ds((r + 1) * OUT_PITCH + z * PART + HALF, PART - HALF), :] = jnp.zeros(
                (PART - HALF, WIDTH), jnp.float32
            )
    for z in range(DEEP):
        for t in range(strip):
            parts = [
                mixed[pl.ds(g * OWNERS, OWNERS), pl.ds((z * strip + t) * WIDTH, WIDTH)] for g in range(BLOCKS)
            ]
            for q, w in enumerate(exchange_groups(parts, lane)):
                spread[pl.ds(OUT_PITCH + z * PART + strip * q + t, OWNERS, stride=OUT_PITCH), :] = w
    half = half_ref[0]

    @pl.when(half == 0)
    def _():
        for z in range(DEEP):
            for k in range(RIM):
                w = spread[pl.ds(OUT_PITCH + z * PART + k, OWNERS, stride=OUT_PITCH), :]
                spread[pl.ds(z * PART + HALF + k, OWNERS, stride=OUT_PITCH), :] = w

    @pl.when(half == 1)
    def _():
        for z in range(DEEP):
            for k in range(RIM):
                w = spread[pl.ds(OUT_PITCH + z * PART + HALF - RIM + k, OWNERS, stride=OUT_PITCH), :]
                spread[pl.ds(2 * OUT_PITCH + z * PART + PART - RIM + k, OWNERS, stride=OUT_PITCH), :] = w

    for r in range(OWNERS):
        out_ref[r] = spread[pl.ds((r + 1) * OUT_PITCH, OUT_PITCH), :].astype(jnp.bfloat16)


def hold(half, got):
    strip = HALF // BLOCKS
    rows = OWNERS * BLOCKS
    return pl.pallas_call(
        hold_kernel,
        out_shape=jax.ShapeDtypeStruct((OWNERS, OUT_PITCH, WIDTH), jnp.bfloat16),
        in_specs=[in_smem(), in_vmem()],
        out_specs=in_vmem(),
        scratch_shapes=[
            pltpu.VMEM((OWNERS * PITCH, WIDTH), jnp.float32),
            pltpu.VMEM((2 * rows, TAKEN * (strip + 1) * WIDTH), jnp.bfloat16),
            pltpu.VMEM((4, 2 * rows, 2 * rows), jnp.bfloat16),
            pltpu.VMEM((rows, DEEP * strip * WIDTH), jnp.float32),
            pltpu.VMEM(((OWNERS + 2) * OUT_PITCH, WIDTH), jnp.float32),
        ],
        compiler_params=params(12),
        name="hold",
    )(half, got)


def distance():
    i = lax.broadcasted_iota(jnp.int32, (WIDTH, WIDTH), 0)
    j = lax.broadcasted_iota(jnp.int32, (WIDTH, WIDTH), 1)
    return jnp.abs(i - j)


def box_band():
    one = jnp.where(distance() <= BOX_RADIUS, 1.0, 0.0).astype(jnp.bfloat16)
    return one, jnp.concatenate([one, one], axis=0)


def smooth_band():
    d = distance()
    taps = smooth_weights(SMOOTH_RADIUS)
    left = jnp.zeros((WIDTH, WIDTH), jnp.float32)
    for t in range(SMOOTH_RADIUS + 1):
        left = jnp.where(d == t, taps[SMOOTH_RADIUS + t], left)
    parts = []
    for _ in range(3):
        part = left.astype(jnp.bfloat16)
        parts.append(part)
        left = left - part.astype(jnp.float32)
    return jnp.concatenate(parts, axis=0)


def times(a, band):
    return jnp.dot(a, band, preferred_element_type=jnp.float32)


def halves(product):
    hi = product.astype(jnp.bfloat16)
    return jnp.concatenate([hi, (product - hi.astype(jnp.float32)).astype(jnp.bfloat16)], axis=1)


def rows_at(i):
    if isinstance(i, int):
        return pl.ds(i * ROW, ROW)
    return pl.ds(pl.multiple_of(i * ROW, ROW), ROW)


def along(a, step):
    return pltpu.roll(a, (-step) % ROW, 0)


def box_zx(ref, which, i):
    r = [ref[which, rows_at(i + t), :] for t in range(2 * BOX_RADIUS + 1)]
    a = ((r[0] + r[1]) + (r[2] + r[3])) + r[4]
    two = a + along(a, -1)
    return ((along(two, -1) + a) + along(two, 2)) * (1.0 / (2 * BOX_RADIUS + 1) ** 3)


def mask_rows(ref):
    x = lax.broadcasted_iota(jnp.int32, (ROW, WIDTH), 0)
    m = ref[...].astype(jnp.float32)
    right = jnp.where(x < SIDE + SMOOTH_RADIUS, m[1:2], 0.0)
    return jnp.where(x < SIDE, m[0:1], jnp.where(x >= ROW - SMOOTH_RADIUS, m[2:3], right))


def fixed_sums(f, sums, q, rows, bands):
    sums[q, rows, :] = times(f, bands[0])
    wide = f.astype(jnp.float32)
    sums[q + 1, rows, :] = times(halves(wide * wide), bands[1])


def fixed_row(sums, q, i, here, mask, mean_ref, away_ref, gain_ref, k):
    mean = box_zx(sums, q, i)
    var = box_zx(sums, q + 1, i) - mean * mean + var_eps
    mean_ref[rows_at(k), :] = mean
    away_ref[rows_at(k), :] = here - mean
    gain_ref[rows_at(k), :] = mask / var


def fixed_kernel(fixed_ref, mask_ref, mean_ref, away_ref, gain_ref, sums):
    bands = box_band()
    chunk = 4 * ROW

    def by_y(i, carry):
        rows = pl.ds(pl.multiple_of(i * chunk, chunk), chunk)
        fixed_sums(fixed_ref[rows, :], sums, 0, rows, bands)
        return carry

    lax.fori_loop(0, SIDE // 4, by_y, 0)
    mask = mask_rows(mask_ref)

    def by_z(i, carry):
        here = fixed_ref[rows_at(i + BOX_RADIUS), :].astype(jnp.float32)
        fixed_row(sums, 0, i, here, mask, mean_ref, away_ref, gain_ref, i)
        return carry

    lax.fori_loop(0, INNER, by_z, 0)


def fixed_part(fixed, mask):
    out = jax.ShapeDtypeStruct((INNER * ROW, WIDTH), jnp.float32)
    return pl.pallas_call(
        fixed_kernel,
        out_shape=[out] * 3,
        in_specs=[in_vmem()] * 2,
        out_specs=[in_vmem()] * 3,
        scratch_shapes=[pltpu.VMEM((2, SIDE * ROW, WIDTH), jnp.float32)],
        compiler_params=params(8),
        cost_estimate=cost(5_000_000_000, 4_000_000),
        name="fixed_part",
    )(fixed, mask)


def sums_by_y(f, wide, sums, rows, bands):
    mw = wide[rows, :]
    m = mw.astype(jnp.bfloat16)
    sums[0, rows, :] = times(m, bands[0])
    sums[1, rows, :] = times(halves(mw * mw), bands[1])
    sums[2, rows, :] = times(halves(mw * f.astype(jnp.float32)), bands[1])


def force_row(wide, sums, i, mean_ref, away_ref, gain_ref, j, force, k):
    mean = box_zx(sums, 0, i)
    var = box_zx(sums, 1, i) - mean * mean + var_eps
    cov = box_zx(sums, 2, i) - mean_ref[rows_at(j), :] * mean
    q = cov / var
    m = wide[rows_at(i + BOX_RADIUS), :]
    term = gain_ref[rows_at(j), :] * q * (away_ref[rows_at(j), :] - q * (m - mean))
    lane = lax.broadcasted_iota(jnp.int32, (ROW, WIDTH), 1)
    up = jnp.where(lane == WIDTH - 1, 0.0, pltpu.roll(m, WIDTH - 1, 1))
    down = jnp.where(lane == 0, 0.0, pltpu.roll(m, 1, 1))
    force[0, rows_at(k), :] = (term * (along(m, 1) - along(m, -1))).astype(jnp.bfloat16)
    z_step = wide[rows_at(i + BOX_RADIUS + 1), :] - wide[rows_at(i + BOX_RADIUS - 1), :]
    force[1, rows_at(k), :] = (term * z_step).astype(jnp.bfloat16)
    force[2, rows_at(k), :] = (term * (up - down)).astype(jnp.bfloat16)


def smooth_row(smooth_y, i, out_ref, z, peak):
    taps = smooth_weights(SMOOTH_RADIUS)[SMOOTH_RADIUS:]
    total = None
    for c in range(3):
        g = [smooth_y[c, rows_at(i + t), :] for t in range(2 * SMOOTH_RADIUS + 1)]
        mid = SMOOTH_RADIUS
        s = taps[0] * g[mid]
        for t in range(1, SMOOTH_RADIUS + 1):
            s += taps[t] * (g[mid - t] + g[mid + t])
        a = taps[0] * s
        for t in range(1, SMOOTH_RADIUS + 1):
            a += taps[t] * (along(s, -t) + along(s, t))
        a = a[:SIDE]
        out_ref[pl.ds(c * SIDE * SIDE + z, SIDE, stride=SIDE), :] = a
        total = a * a if total is None else total + a * a
    return jnp.maximum(peak, total)


def inner_kernel(warped_ref, fixed_ref, mean_ref, away_ref, gain_ref, out_ref, edge_ref, peak_ref, wide, sums, force, smooth_y):
    bands = box_band()
    triple = smooth_band()
    chunk = 4 * ROW

    def by_y(i, carry):
        for step in range(2):
            pair = 2 * i + step
            for half in range(2):
                for z in range(DEEP):
                    src = (pair * 2 + half) * OUT_PITCH + z * PART
                    dst = (pair * DEEP + z) * ROW
                    own = warped_ref[pl.ds(pl.multiple_of(src, 8), HALF), :]
                    wide[pl.ds(pl.multiple_of(dst + half * HALF, 8), HALF), :] = own.astype(jnp.float32)
                    side = warped_ref[pl.ds(pl.multiple_of(src + HALF, 8), 8), :]
                    wide[pl.ds(pl.multiple_of(dst + SIDE + 8 * half, 8), 8), :] = side.astype(jnp.float32)
        rows = pl.ds(pl.multiple_of(i * chunk, chunk), chunk)
        sums_by_y(fixed_ref[rows, :], wide, sums, rows, bands)
        return carry

    lax.fori_loop(0, SIDE // 4, by_y, 0)

    def by_z(i, carry):
        force_row(wide, sums, i, mean_ref, away_ref, gain_ref, i, force, i)
        return carry

    lax.fori_loop(0, INNER, by_z, 0)

    def smooth(i, carry):
        rows = pl.ds(pl.multiple_of(i * chunk, chunk), chunk)
        for c in range(3):
            f = force[c, rows, :]
            smooth_y[c, rows, :] = times(jnp.concatenate([f, f, f], axis=1), triple)
        return carry

    lax.fori_loop(0, INNER // 4, smooth, 0)
    kept = 2 * SMOOTH_RADIUS * ROW
    for c in range(3):
        edge_ref[c, 0:kept, :] = smooth_y[c, 0:kept, :]
        edge_ref[c, kept : 2 * kept, :] = smooth_y[c, INNER * ROW - kept : INNER * ROW, :]
    peak_ref[...] = lax.fori_loop(
        0, CORE, lambda i, peak: smooth_row(smooth_y, i, out_ref, i + RIM, peak), jnp.zeros((SIDE, WIDTH), jnp.float32)
    )


def rim_kernel(
    below_ref, above_ref, head_ref, tail_ref, mask_ref, edge_ref, first_ref,
    out_ref, peak_ref, wide, fwide, sums, fmean, faway, fgain, force, smooth_y,
):
    bands = box_band()
    triple = smooth_band()
    own = RIM - 1
    stack = RIM + own
    for ref, start, count, at in (
        (below_ref, 0, RIM, 0),
        (head_ref, 0, own, RIM),
        (tail_ref, RIM - own, own, stack),
        (above_ref, 0, RIM, stack + own),
    ):
        rows = pl.ds(at * ROW, count * ROW)
        f = ref[pl.ds((RIM + start) * ROW, count * ROW), :]
        wide[rows, :] = ref[pl.ds(start * ROW, count * ROW), :].astype(jnp.float32)
        fwide[rows, :] = f.astype(jnp.float32)
        sums_by_y(f, wide, sums, rows, bands)
        fixed_sums(f, sums, 3, rows, bands)
    here = mask_rows(mask_ref)
    last = pl.ds(2 * RIM * ROW, 8)
    masks = [mask_rows(below_ref.at[last, :]), here, mask_rows(above_ref.at[last, :])]

    def by_z(i, carry):
        side = jnp.where(i < RIM, 0, 1)
        first = stack * side + i - RIM * side
        outer = jnp.where(side == 0, masks[0], masks[2])
        mask = jnp.where((i >= SMOOTH_RADIUS) & (i < 2 * RIM - SMOOTH_RADIUS), masks[1], outer)
        fixed_row(sums, 3, first, fwide[rows_at(first + BOX_RADIUS), :], mask, fmean, faway, fgain, i)
        force_row(wide, sums, first, fmean, faway, fgain, i, force, i)
        return carry

    lax.fori_loop(0, 2 * RIM, by_z, 0)
    kept = 2 * SMOOTH_RADIUS
    tall = RIM + kept
    for c in range(3):
        for side in range(2):
            f = force[c, pl.ds(side * RIM * ROW, RIM * ROW), :]
            new = (side * tall + (kept if side else 0)) * ROW
            smooth_y[c, pl.ds(new, RIM * ROW), :] = times(jnp.concatenate([f, f, f], axis=1), triple)
            old = (side * tall + (0 if side else RIM)) * ROW
            smooth_y[c, pl.ds(old, kept * ROW), :] = edge_ref[c, pl.ds(side * kept * ROW, kept * ROW), :]

    def smooth(i, peak):
        side = jnp.where(i < RIM, 0, 1)
        j = i - RIM * side
        return smooth_row(smooth_y, tall * side + j, out_ref, (SIDE - RIM) * side + j, peak)

    peak = lax.fori_loop(0, 2 * RIM, smooth, first_ref[...])
    top = jnp.max(jnp.max(peak, axis=0, keepdims=True), axis=1, keepdims=True)
    peak_ref[...] = jnp.broadcast_to(top.reshape(1, 1, 1), peak_ref.shape)


def inner(warped, fixed, mean, away, gain):
    return pl.pallas_call(
        inner_kernel,
        out_shape=[
            jax.ShapeDtypeStruct((3 * SIDE * SIDE, WIDTH), jnp.float32),
            jax.ShapeDtypeStruct((3, 4 * SMOOTH_RADIUS * ROW, WIDTH), jnp.float32),
            jax.ShapeDtypeStruct((SIDE, WIDTH), jnp.float32),
        ],
        in_specs=[in_vmem()] * 5,
        out_specs=[in_vmem()] * 3,
        scratch_shapes=[
            pltpu.VMEM((SIDE * ROW, WIDTH), jnp.float32),
            pltpu.VMEM((3, SIDE * ROW, WIDTH), jnp.float32),
            pltpu.VMEM((3, INNER * ROW, WIDTH), jnp.bfloat16),
            pltpu.VMEM((3, INNER * ROW, WIDTH), jnp.float32),
        ],
        compiler_params=params(14),
        cost_estimate=cost(10_000_000_000, 8_000_000),
        name="inner",
    )(warped, fixed, mean, away, gain)


def rim(below, above, head, tail, mask, edge, first):
    stack = 2 * (2 * RIM - 1) * ROW
    tall = 2 * (RIM + 2 * SMOOTH_RADIUS) * ROW
    return pl.pallas_call(
        rim_kernel,
        out_shape=[
            jax.ShapeDtypeStruct((3 * SIDE * SIDE, WIDTH), jnp.float32),
            jax.ShapeDtypeStruct((OWNERS, 1, WIDTH), jnp.float32),
        ],
        in_specs=[in_vmem()] * 7,
        out_specs=[in_vmem()] * 2,
        scratch_shapes=[pltpu.VMEM((stack, WIDTH), jnp.float32)] * 2
        + [pltpu.VMEM((5, stack, WIDTH), jnp.float32)]
        + [pltpu.VMEM((2 * RIM * ROW, WIDTH), jnp.float32)] * 3
        + [
            pltpu.VMEM((3, 2 * RIM * ROW, WIDTH), jnp.bfloat16),
            pltpu.VMEM((3, tall, WIDTH), jnp.float32),
        ],
        compiler_params=params(14),
        name="rim",
    )(below, above, head, tail, mask, edge, first)


def relay_kernel(in_ref, out_ref):
    a = jnp.max(in_ref[...].reshape(in_ref.shape[0], WIDTH), axis=0, keepdims=True)
    out_ref[...] = jnp.broadcast_to(a.reshape(1, 1, WIDTH), out_ref.shape)


def relay(tiles, count):
    return pl.pallas_call(
        relay_kernel,
        out_shape=jax.ShapeDtypeStruct((count, 1, WIDTH), jnp.float32),
        in_specs=[in_vmem()],
        out_specs=in_vmem(),
        compiler_params=params(1),
        name="relay",
    )(tiles)


STEP_X = 8


def finish_kernel(peaks_ref, core_ref, rim_ref, out_ref):
    x0 = pl.program_id(0) * STEP_X
    peak = jnp.sqrt(jnp.max(peaks_ref[...].reshape(peaks_ref.shape[0], WIDTH), axis=0, keepdims=True))
    scale = step_length / (peak + peak_eps)
    z = lax.broadcasted_iota(jnp.int32, (SIDE, WIDTH), 0)
    at_rim = (z < RIM) | (z >= SIDE - RIM)
    for c in range(3):
        for x in range(STEP_X):
            rows = pl.ds(pl.multiple_of((c * SIDE + x0 + x) * SIDE, SIDE), SIDE)
            out_ref[c, x] = jnp.where(at_rim, rim_ref[rows, :], core_ref[rows, :]) * scale


def finish(peaks, core, rims):
    return pl.pallas_call(
        finish_kernel,
        out_shape=jax.ShapeDtypeStruct((3, SIDE, SIDE, WIDTH), jnp.float32),
        grid=(SIDE // STEP_X,),
        in_specs=[in_vmem()] * 3,
        out_specs=pl.BlockSpec((3, STEP_X, SIDE, WIDTH), lambda i: (0, i, 0, 0)),
        compiler_params=params(12),
        name="finish",
    )(peaks, core, rims)


def per_device(fixed_image, moving_image, fetch_owner, fetch_block, fetch_count, interp_level, block_mask):
    side, width = SIDE, WIDTH
    sent = pack(fetch_owner, fetch_block, fetch_count, interp_level, moving_image)
    got = lax.all_to_all(sent, "blk", split_axis=0, concat_axis=0, tiled=True)

    mask_row = jnp.repeat(block_mask.reshape(BLOCKS), side).astype(jnp.bfloat16)[None]
    last = jnp.concatenate([fixed_image[side - RIM :].reshape(-1, width), mask_row], axis=0)
    first = jnp.concatenate([fixed_image[:RIM].reshape(-1, width), mask_row], axis=0)
    left = lax.ppermute(last, "blk", shift_up("blk"))
    right = lax.ppermute(first, "blk", shift_down("blk"))
    turn = lambda a: a[:-1].reshape(RIM, side, width)
    fixed = jnp.concatenate(
        [fixed_image, turn(right), jnp.zeros((ROW - EXT, side, width), jnp.bfloat16), turn(left)], axis=0
    ).transpose(1, 0, 2)
    masks = jnp.concatenate([mask_row, right[-1:], left[-1:], jnp.zeros((5, width), jnp.bfloat16)], axis=0)
    mean, away, gain = fixed_part(fixed.reshape(side * ROW, width), masks)

    half = (lax.axis_index("blk") % 2).astype(jnp.int32).reshape(1)
    warped = lax.all_to_all(hold(half, got), "blk", split_axis=0, concat_axis=0, tiled=True)

    def z_rows(pairs):
        part = warped.reshape(side // DEEP, 2, DEEP, PART, width)[pairs]
        rows = [part[:, 0, :, :HALF], part[:, 1, :, :HALF], part[:, 0, :, HALF:], part[:, 1, :, HALF:]]
        return jnp.concatenate(rows, axis=2).reshape(-1, ROW, width)

    def message(moving_rows, fixed_rows):
        return jnp.concatenate([moving_rows.reshape(-1, width), fixed_rows.reshape(-1, width), masks], axis=0)

    tail = message(z_rows(slice(side // DEEP - 3, None))[1:], fixed[side - RIM :])
    head = message(z_rows(slice(0, 3))[:RIM], fixed[:RIM])
    below = lax.ppermute(tail, "slab", shift_up("slab"))
    above = lax.ppermute(head, "slab", shift_down("slab"))
    core, edge, top = inner(warped.reshape(side * ROW, width), fixed.reshape(side * ROW, width), mean, away, gain)
    rims, peak = rim(below, above, head, tail, masks, edge, top)
    peak = lax.all_to_all(peak, "blk", split_axis=0, concat_axis=0, tiled=True)
    peak = relay(peak, lax.axis_size("slab"))
    peak = lax.all_to_all(peak, "slab", split_axis=0, concat_axis=0, tiled=True)
    return finish(peak, core, rims)


def solution(mesh):
    in_specs = (
        P("blk", "slab", None),
        P("blk", "slab", None),
        P("blk", "slab", None, None),
        P("blk", "slab", None, None),
        P("blk", "slab", None),
        P("blk", "slab", None, None, None),
        P("blk", "slab", None),
    )
    return jax.shard_map(
        per_device, mesh=mesh, in_specs=in_specs, out_specs=P(None, "blk", "slab", None), check_vma=False
    )
```

```python
import math

import jax
import jax.numpy as jnp
from jax import lax
from jax.experimental import pallas as pl
from jax.experimental.pallas import tpu as pltpu
from jax.sharding import PartitionSpec as P

LEVELS = 8
BOX_RADIUS = 2
SMOOTH_RADIUS = 3
RIM = BOX_RADIUS + SMOOTH_RADIUS

sigma_smooth = 1.5
step_length = 2.0
var_eps = 1e-05
peak_eps = 1e-06


def smooth_weights(radius):
    raw = [math.exp(-(t * t) / (2.0 * sigma_smooth * sigma_smooth)) for t in range(-radius, radius + 1)]
    total = sum(raw)
    return [one / total for one in raw]


def shift_up(axis):
    n = lax.axis_size(axis)
    return [(i, i + 1) for i in range(n - 1)]


def shift_down(axis):
    n = lax.axis_size(axis)
    return [(i + 1, i) for i in range(n - 1)]


SIDE = 32
WIDTH = 128
BLOCKS = WIDTH // SIDE
SLOTS = 4
OWNERS = 32
DEEP = 2
HALF = SIDE // 2
TAKEN = DEEP + 1
SENT = TAKEN * HALF + TAKEN + 1
PITCH = 56
EXT = SIDE + 2 * RIM
OUT_PITCH = 48
PART = OUT_PITCH // DEEP
MID = SIDE + 2 * SMOOTH_RADIUS
INNER = SIDE - 2 * BOX_RADIUS
CORE = INNER - 2 * SMOOTH_RADIUS
ROW = OUT_PITCH
MIB = 1 << 20


def params(mib):
    return pltpu.CompilerParams(vmem_limit_bytes=mib * MIB)


def cost(flops, nbytes):
    return pl.CostEstimate(flops=flops, bytes_accessed=nbytes, transcendentals=0)


def in_vmem():
    return pl.BlockSpec(memory_space=pltpu.VMEM)


def in_smem():
    return pl.BlockSpec(memory_space=pltpu.SMEM)


def pack_kernel(owner_ref, block_ref, count_ref, level_ref, moving_ref, out_ref, wide):
    lane = lax.broadcasted_iota(jnp.int32, (TAKEN + 1, WIDTH), 1)
    row = jnp.zeros((TAKEN + 1, WIDTH), jnp.int32)
    e = BLOCKS * SLOTS
    for g in range(BLOCKS):
        count = count_ref[0, 0, g]
        row = jnp.where(lane == 4 * e + g, count, row)
        for k in range(SLOTS):
            name = block_ref[0, 0, g, k] * OWNERS + owner_ref[0, 0, g, k]
            row = jnp.where(lane == g * SLOTS + k, jnp.where(k < count, name, -1), row)
            for axis in range(3):
                at = e + (g * 3 + axis) * SLOTS + k
                row = jnp.where(lane == at, level_ref[0, 0, axis, g, k], row)
    row = row.astype(jnp.float32)
    for x in range(SIDE):
        wide[pl.ds(x * SIDE, SIDE), :] = moving_ref[x].astype(jnp.float32)
    place = lax.broadcasted_iota(jnp.int32, (TAKEN + 1, WIDTH), 0)
    for z in range(SIDE):
        plane = wide[pl.ds(z, SIDE, stride=SIDE), :].astype(jnp.bfloat16)
        spots = [(z // DEEP, z % DEEP)]
        if z % DEEP == 0 and z > 0:
            spots.append((z // DEEP - 1, DEEP))
        if z == SIDE - 1:
            spots.append((z // DEEP, DEEP))
        for pair, at in spots:
            for half in range(2):
                out_ref[pair * 2 + half, at * HALF : (at + 1) * HALF, :] = plane[half * HALF : (half + 1) * HALF]
    for pair in range(SIDE // DEEP):
        for half in range(2):
            x = min((half + 1) * HALF, SIDE - 1)
            if pair < SIDE // DEEP - 1:
                extra = wide[pl.ds(x * SIDE + pair * DEEP, TAKEN + 1), :]
            else:
                two = wide[pl.ds(x * SIDE + pair * DEEP, DEEP), :]
                extra = jnp.concatenate([two, two[1:2], two[1:2]], axis=0)
            extra = jnp.where(place == TAKEN, row, extra)
            out_ref[pair * 2 + half, TAKEN * HALF : SENT, :] = extra.astype(jnp.bfloat16)


def pack(owner, block, count, level, moving):
    return pl.pallas_call(
        pack_kernel,
        out_shape=jax.ShapeDtypeStruct((OWNERS, SENT, WIDTH), jnp.bfloat16),
        in_specs=[in_smem()] * 4 + [in_vmem()],
        out_specs=in_vmem(),
        scratch_shapes=[pltpu.VMEM((SIDE * SIDE, WIDTH), jnp.float32)],
        name="pack",
    )(owner, block, count, level, moving)


def exchange_groups(parts, lane):
    turned = [[p] + [pltpu.roll(p, SIDE * s, 1) for s in range(1, BLOCKS)] for p in parts]
    out = []
    for b in range(BLOCKS):
        pick = [turned[a][(a - b) % BLOCKS] for a in range(BLOCKS)]
        out.append(
            jnp.where(
                lane < 2 * SIDE,
                jnp.where(lane < SIDE, pick[0], pick[1]),
                jnp.where(lane < 3 * SIDE, pick[2], pick[3]),
            )
        )
    return out


def column(a, i):
    return jnp.broadcast_to(a[:, i : i + 1], a.shape)


def hold_kernel(half_ref, got_ref, out_ref, wide, source, coef, mixed, spread):
    strip = HALF // BLOCKS
    rows = OWNERS * BLOCKS
    lane = lax.broadcasted_iota(jnp.int32, (OWNERS, WIDTH), 1)
    last_y = lane % SIDE == SIDE - 1
    for o in range(OWNERS):
        wide[pl.ds(o * PITCH, SENT), :] = got_ref[o].astype(jnp.float32)

    lists = wide[pl.ds(SENT - 1, OWNERS, stride=PITCH), :]
    where_k = lane.astype(jnp.float32)
    e = BLOCKS * SLOTS
    top = float(LEVELS)
    scales = []
    for g in range(BLOCKS):
        total = {}
        for k in range(SLOTS):
            at = g * SLOTS + k
            name = column(lists, at)
            base = e + g * 3 * SLOTS + k
            lx, lz, ly = (column(lists, base + a * SLOTS) for a in range(3))
            x1 = jnp.where(where_k == name, lx, 0.0)
            x0 = jnp.where(where_k == name, top - lx, 0.0)
            for dx in range(2):
                ax = x1 if dx else x0
                z1 = ax * lz
                for dz in range(2):
                    az = z1 if dz else top * ax - z1
                    y1 = az * ly
                    for dy in range(2):
                        ay = y1 if dy else top * az - y1
                        key = (dx, dz, dy)
                        total[key] = ay if k == 0 else total[key] + ay
        for (dx, dz, dy), c in total.items():
            hi = jnp.floor(c * (1.0 / 16.0)) * 16.0
            col = pl.ds(dy * WIDTH, WIDTH)
            coef[dz * 2 + dx, pl.ds(g * OWNERS, OWNERS), col] = hi.astype(jnp.bfloat16)
            coef[dz * 2 + dx, pl.ds(rows + g * OWNERS, OWNERS), col] = (c - hi).astype(jnp.bfloat16)
        scales.append((1.0 / column(lists, 4 * e + g)) * (1.0 / LEVELS**3))

    wrap = strip + 1
    for z in range(TAKEN):
        for t in range(wrap):
            at = [strip * q + t for q in range(BLOCKS)]
            parts = [
                wide[pl.ds(z * HALF + x if x < HALF else TAKEN * HALF + z, OWNERS, stride=PITCH), :] for x in at
            ]
            for g, u in enumerate(exchange_groups(parts, lane)):
                v = jnp.where(last_y, u, pltpu.roll(u, WIDTH - 1, 1))
                for dy, a in enumerate((u, v)):
                    source[pl.ds(dy * rows + g * OWNERS, OWNERS), pl.ds((z * wrap + t) * WIDTH, WIDTH)] = a.astype(
                        jnp.bfloat16
                    )

    piece = 2 * WIDTH
    for z in range(DEEP):
        for t in range(0, strip, 2):
            acc = None
            for dz in range(2):
                for dx in range(2):
                    col = ((z + dz) * wrap + t + dx) * WIDTH
                    one = jnp.dot(
                        coef[dz * 2 + dx], source[:, pl.ds(col, piece)], preferred_element_type=jnp.float32
                    )
                    acc = one if acc is None else acc + one
            for g in range(BLOCKS):
                lo = rows + g * OWNERS
                part = acc[g * OWNERS : (g + 1) * OWNERS] + acc[lo : lo + OWNERS]
                for i in range(2):
                    mixed[pl.ds(g * OWNERS, OWNERS), pl.ds((z * strip + t + i) * WIDTH, WIDTH)] = (
                        part[:, i * WIDTH : (i + 1) * WIDTH] * scales[g]
                    )

    for r in range(OWNERS):
        for z in range(DEEP):
            spread[pl.ds((r + 1) * OUT_PITCH + z * PART + HALF, PART - HALF), :] = jnp.zeros(
                (PART - HALF, WIDTH), jnp.float32
            )
    for z in range(DEEP):
        for t in range(strip):
            parts = [
                mixed[pl.ds(g * OWNERS, OWNERS), pl.ds((z * strip + t) * WIDTH, WIDTH)] for g in range(BLOCKS)
            ]
            for q, w in enumerate(exchange_groups(parts, lane)):
                spread[pl.ds(OUT_PITCH + z * PART + strip * q + t, OWNERS, stride=OUT_PITCH), :] = w
    half = half_ref[0]

    @pl.when(half == 0)
    def _():
        for z in range(DEEP):
            for k in range(RIM):
                w = spread[pl.ds(OUT_PITCH + z * PART + k, OWNERS, stride=OUT_PITCH), :]
                spread[pl.ds(z * PART + HALF + k, OWNERS, stride=OUT_PITCH), :] = w

    @pl.when(half == 1)
    def _():
        for z in range(DEEP):
            for k in range(RIM):
                w = spread[pl.ds(OUT_PITCH + z * PART + HALF - RIM + k, OWNERS, stride=OUT_PITCH), :]
                spread[pl.ds(2 * OUT_PITCH + z * PART + PART - RIM + k, OWNERS, stride=OUT_PITCH), :] = w

    for r in range(OWNERS):
        out_ref[r] = spread[pl.ds((r + 1) * OUT_PITCH, OUT_PITCH), :].astype(jnp.bfloat16)


def hold(half, got):
    strip = HALF // BLOCKS
    rows = OWNERS * BLOCKS
    return pl.pallas_call(
        hold_kernel,
        out_shape=jax.ShapeDtypeStruct((OWNERS, OUT_PITCH, WIDTH), jnp.bfloat16),
        in_specs=[in_smem(), in_vmem()],
        out_specs=in_vmem(),
        scratch_shapes=[
            pltpu.VMEM((OWNERS * PITCH, WIDTH), jnp.float32),
            pltpu.VMEM((2 * rows, TAKEN * (strip + 1) * WIDTH), jnp.bfloat16),
            pltpu.VMEM((4, 2 * rows, 2 * rows), jnp.bfloat16),
            pltpu.VMEM((rows, DEEP * strip * WIDTH), jnp.float32),
            pltpu.VMEM(((OWNERS + 2) * OUT_PITCH, WIDTH), jnp.float32),
        ],
        compiler_params=params(12),
        name="hold",
    )(half, got)


def distance():
    i = lax.broadcasted_iota(jnp.int32, (WIDTH, WIDTH), 0)
    j = lax.broadcasted_iota(jnp.int32, (WIDTH, WIDTH), 1)
    return jnp.abs(i - j)


def box_band():
    one = jnp.where(distance() <= BOX_RADIUS, 1.0, 0.0).astype(jnp.bfloat16)
    return one, jnp.concatenate([one, one], axis=0)


def smooth_band():
    d = distance()
    taps = smooth_weights(SMOOTH_RADIUS)
    left = jnp.zeros((WIDTH, WIDTH), jnp.float32)
    for t in range(SMOOTH_RADIUS + 1):
        left = jnp.where(d == t, taps[SMOOTH_RADIUS + t], left)
    parts = []
    for _ in range(2):
        part = left.astype(jnp.bfloat16)
        parts.append(part)
        left = left - part.astype(jnp.float32)
    return jnp.concatenate(parts, axis=0)


def times(a, band):
    return jnp.dot(a, band, preferred_element_type=jnp.float32)


def halves(product):
    hi = product.astype(jnp.bfloat16)
    return jnp.concatenate([hi, (product - hi.astype(jnp.float32)).astype(jnp.bfloat16)], axis=1)


def rows_at(i):
    if isinstance(i, int):
        return pl.ds(i * ROW, ROW)
    return pl.ds(pl.multiple_of(i * ROW, ROW), ROW)


def along(a, step):
    return pltpu.roll(a, (-step) % ROW, 0)


def box_x(a):
    two = a + along(a, -1)
    return ((along(two, -1) + a) + along(two, 2)) * (1.0 / (2 * BOX_RADIUS + 1) ** 3)


def box_zx(ref, which, i, count):
    r = [ref[which, rows_at(i + t), :] for t in range(2 * BOX_RADIUS + count)]
    if count == 1:
        return [box_x(((r[0] + r[1]) + (r[2] + r[3])) + r[4])]
    mid = (r[1] + r[2]) + (r[3] + r[4])
    return [box_x(r[0] + mid), box_x(mid + r[5])]


def mask_rows(ref):
    x = lax.broadcasted_iota(jnp.int32, (ROW, WIDTH), 0)
    m = ref[...].astype(jnp.float32)
    right = jnp.where(x < SIDE + SMOOTH_RADIUS, m[1:2], 0.0)
    return jnp.where(x < SIDE, m[0:1], jnp.where(x >= ROW - SMOOTH_RADIUS, m[2:3], right))


def fixed_sums(f, sums, q, rows, bands):
    sums[q, rows, :] = times(f, bands[0])
    wide = f.astype(jnp.float32)
    sums[q + 1, rows, :] = times(halves(wide * wide), bands[1])


def fixed_rows(sums, q, i, here, mask):
    means = box_zx(sums, q, i, len(here))
    squares = box_zx(sums, q + 1, i, len(here))
    out = []
    for h, m, p, sq in zip(here, mask, means, squares):
        out.append((p, h - p, m / (sq - p * p + var_eps)))
    return out


def fixed_kernel(fixed_ref, mask_ref, mean_ref, away_ref, gain_ref, sums):
    bands = box_band()
    chunk = 8 * ROW

    def by_y(i, carry):
        rows = pl.ds(pl.multiple_of(i * chunk, chunk), chunk)
        fixed_sums(fixed_ref[rows, :], sums, 0, rows, bands)
        return carry

    lax.fori_loop(0, SIDE // 8, by_y, 0)
    mask = mask_rows(mask_ref)

    def by_z(step, carry):
        i = 2 * step
        here = [fixed_ref[rows_at(i + BOX_RADIUS + t), :].astype(jnp.float32) for t in range(2)]
        for t, (mean, away, gain) in enumerate(fixed_rows(sums, 0, i, here, [mask, mask])):
            mean_ref[rows_at(i + t), :] = mean
            away_ref[rows_at(i + t), :] = away
            gain_ref[rows_at(i + t), :] = gain
        return carry

    lax.fori_loop(0, INNER // 2, by_z, 0)


def fixed_part(fixed, mask):
    out = jax.ShapeDtypeStruct((INNER * ROW, WIDTH), jnp.float32)
    return pl.pallas_call(
        fixed_kernel,
        out_shape=[out] * 3,
        in_specs=[in_vmem()] * 2,
        out_specs=[in_vmem()] * 3,
        scratch_shapes=[pltpu.VMEM((2, SIDE * ROW, WIDTH), jnp.float32)],
        compiler_params=params(8),
        cost_estimate=cost(5_000_000_000, 4_000_000),
        name="fixed_part",
    )(fixed, mask)


def sums_by_y(f, wide, sums, rows, bands):
    mw = wide[rows, :]
    m = mw.astype(jnp.bfloat16)
    sums[0, rows, :] = times(m, bands[0])
    sums[1, rows, :] = times(halves(mw * mw), bands[1])
    sums[2, rows, :] = times(halves(mw * f.astype(jnp.float32)), bands[1])


def force_rows(wide, sums, i, fixed, force, k, pitch):
    count = len(fixed)
    means = box_zx(sums, 0, i, count)
    squares = box_zx(sums, 1, i, count)
    products = box_zx(sums, 2, i, count)
    lane = lax.broadcasted_iota(jnp.int32, (ROW, WIDTH), 1)
    at = [wide[rows_at(i + BOX_RADIUS - 1 + t), :] for t in range(count + 2)]
    for t, (mean_f, away, gain) in enumerate(fixed):
        mean = means[t]
        q = (products[t] - mean_f * mean) / (squares[t] - mean * mean + var_eps)
        m = at[t + 1]
        term = gain * q * (away - q * (m - mean))
        up = jnp.where(lane == WIDTH - 1, 0.0, pltpu.roll(m, WIDTH - 1, 1))
        down = jnp.where(lane == 0, 0.0, pltpu.roll(m, 1, 1))
        steps = (along(m, 1) - along(m, -1), at[t + 2] - at[t], up - down)
        for c in range(3):
            force[rows_at(c * pitch + k + t), :] = (term * steps[c]).astype(jnp.bfloat16)


def smooth_rows(smooth_y, pitch, i, out_ref, z, count, peak):
    taps = smooth_weights(SMOOTH_RADIUS)[SMOOTH_RADIUS:]
    mid = SMOOTH_RADIUS
    total = [None] * count
    for c in range(3):
        g = [smooth_y[rows_at(c * pitch + i + t), :] for t in range(2 * SMOOTH_RADIUS + count)]
        for n in range(count):
            s = taps[0] * g[n + mid]
            for t in range(1, SMOOTH_RADIUS + 1):
                s += taps[t] * (g[n + mid - t] + g[n + mid + t])
            a = taps[0] * s
            for t in range(1, SMOOTH_RADIUS + 1):
                a += taps[t] * (along(s, -t) + along(s, t))
            a = a[:SIDE]
            out_ref[pl.ds(c * SIDE * SIDE + z + n, SIDE, stride=SIDE), :] = a
            total[n] = a * a if c == 0 else total[n] + a * a
    for one in total:
        peak = jnp.maximum(peak, one)
    return peak


def inner_kernel(warped_ref, fixed_ref, mean_ref, away_ref, gain_ref, out_ref, edge_ref, peak_ref, wide, sums, force, smooth_y):
    bands = box_band()
    double = smooth_band()
    chunk = 8 * ROW

    def by_y(i, carry):
        for step in range(4):
            pair = 4 * i + step
            for half in range(2):
                for z in range(DEEP):
                    src = (pair * 2 + half) * OUT_PITCH + z * PART
                    dst = (pair * DEEP + z) * ROW
                    own = warped_ref[pl.ds(pl.multiple_of(src, 8), HALF), :]
                    wide[pl.ds(pl.multiple_of(dst + half * HALF, 8), HALF), :] = own.astype(jnp.float32)
                    side = warped_ref[pl.ds(pl.multiple_of(src + HALF, 8), 8), :]
                    wide[pl.ds(pl.multiple_of(dst + SIDE + 8 * half, 8), 8), :] = side.astype(jnp.float32)
        rows = pl.ds(pl.multiple_of(i * chunk, chunk), chunk)
        sums_by_y(fixed_ref[rows, :], wide, sums, rows, bands)
        return carry

    lax.fori_loop(0, SIDE // 8, by_y, 0)

    def by_z(step, carry):
        i = 2 * step
        fixed = [(mean_ref[rows_at(i + t), :], away_ref[rows_at(i + t), :], gain_ref[rows_at(i + t), :]) for t in range(2)]
        force_rows(wide, sums, i, fixed, force, i, INNER)
        return carry

    lax.fori_loop(0, INNER // 2, by_z, 0)
    batch = 12 * ROW

    def smooth(i, carry):
        rows = pl.ds(pl.multiple_of(i * batch, batch), batch)
        f = force[rows, :]
        smooth_y[rows, :] = times(jnp.concatenate([f, f], axis=1), double)
        return carry

    lax.fori_loop(0, 3 * INNER // 12, smooth, 0)
    kept = 2 * SMOOTH_RADIUS * ROW
    for c in range(3):
        at = c * INNER * ROW
        edge_ref[c, 0:kept, :] = smooth_y[at : at + kept, :]
        edge_ref[c, kept : 2 * kept, :] = smooth_y[at + INNER * ROW - kept : at + INNER * ROW, :]
    peak_ref[...] = lax.fori_loop(
        0,
        CORE // 2,
        lambda i, peak: smooth_rows(smooth_y, INNER, 2 * i, out_ref, 2 * i + RIM, 2, peak),
        jnp.zeros((SIDE, WIDTH), jnp.float32),
    )


def rim_kernel(
    below_ref, above_ref, head_ref, tail_ref, mask_ref, edge_ref, first_ref,
    out_ref, peak_ref, wide, fwide, sums, force, smooth_y,
):
    bands = box_band()
    double = smooth_band()
    own = RIM - 1
    stack = RIM + own
    for ref, start, count, at in (
        (below_ref, 0, RIM, 0),
        (head_ref, 0, own, RIM),
        (tail_ref, RIM - own, own, stack),
        (above_ref, 0, RIM, stack + own),
    ):
        rows = pl.ds(at * ROW, count * ROW)
        wide[rows, :] = ref[pl.ds(start * ROW, count * ROW), :].astype(jnp.float32)
        fwide[rows, :] = ref[pl.ds((RIM + start) * ROW, count * ROW), :].astype(jnp.float32)
    chunk = stack * ROW

    def by_y(i, carry):
        rows = pl.ds(pl.multiple_of(i * chunk, ROW), chunk)
        f = fwide[rows, :].astype(jnp.bfloat16)
        sums_by_y(f, wide, sums, rows, bands)
        fixed_sums(f, sums, 3, rows, bands)
        return carry

    lax.fori_loop(0, 2, by_y, 0)
    last = pl.ds(2 * RIM * ROW, 8)
    masks = [mask_rows(below_ref.at[last, :]), mask_rows(mask_ref), mask_rows(above_ref.at[last, :])]

    def by_z(i, carry):
        for side in range(2):
            first = stack * side + i
            if side == 0:
                mask = jnp.where(i < SMOOTH_RADIUS, masks[0], masks[1])
            else:
                mask = jnp.where(i >= RIM - SMOOTH_RADIUS, masks[2], masks[1])
            fixed = fixed_rows(sums, 3, first, [fwide[rows_at(first + BOX_RADIUS), :]], [mask])
            force_rows(wide, sums, first, fixed, force, i + RIM * side, 2 * RIM)
        return carry

    lax.fori_loop(0, RIM, by_z, 0)
    kept = 2 * SMOOTH_RADIUS
    tall = RIM + kept
    for c in range(3):
        f = force[pl.ds(c * 2 * RIM * ROW, 2 * RIM * ROW), :]
        g = times(jnp.concatenate([f, f], axis=1), double)
        for side in range(2):
            base = c * 2 * tall + side * tall
            new = base + (kept if side else 0)
            smooth_y[pl.ds(new * ROW, RIM * ROW), :] = g[side * RIM * ROW : (side + 1) * RIM * ROW]
            old = base + (0 if side else RIM)
            smooth_y[pl.ds(old * ROW, kept * ROW), :] = edge_ref[c, pl.ds(side * kept * ROW, kept * ROW), :]

    def smooth(i, peak):
        for side in range(2):
            peak = smooth_rows(smooth_y, 2 * tall, tall * side + i, out_ref, (SIDE - RIM) * side + i, 1, peak)
        return peak

    peak = lax.fori_loop(0, RIM, smooth, first_ref[...])
    top = jnp.max(jnp.max(peak, axis=0, keepdims=True), axis=1, keepdims=True)
    peak_ref[...] = jnp.broadcast_to(top.reshape(1, 1, 1), peak_ref.shape)


def inner(warped, fixed, mean, away, gain):
    return pl.pallas_call(
        inner_kernel,
        out_shape=[
            jax.ShapeDtypeStruct((3 * SIDE * SIDE, WIDTH), jnp.float32),
            jax.ShapeDtypeStruct((3, 4 * SMOOTH_RADIUS * ROW, WIDTH), jnp.float32),
            jax.ShapeDtypeStruct((SIDE, WIDTH), jnp.float32),
        ],
        in_specs=[in_vmem()] * 5,
        out_specs=[in_vmem()] * 3,
        scratch_shapes=[
            pltpu.VMEM((SIDE * ROW, WIDTH), jnp.float32),
            pltpu.VMEM((3, SIDE * ROW, WIDTH), jnp.float32),
            pltpu.VMEM((3 * INNER * ROW, WIDTH), jnp.bfloat16),
            pltpu.VMEM((3 * INNER * ROW, WIDTH), jnp.float32),
        ],
        compiler_params=params(14),
        cost_estimate=cost(10_000_000_000, 8_000_000),
        name="inner",
    )(warped, fixed, mean, away, gain)


def rim(below, above, head, tail, mask, edge, first):
    stack = 2 * (2 * RIM - 1) * ROW
    tall = 2 * (RIM + 2 * SMOOTH_RADIUS) * ROW
    return pl.pallas_call(
        rim_kernel,
        out_shape=[
            jax.ShapeDtypeStruct((3 * SIDE * SIDE, WIDTH), jnp.float32),
            jax.ShapeDtypeStruct((OWNERS, 1, WIDTH), jnp.float32),
        ],
        in_specs=[in_vmem()] * 7,
        out_specs=[in_vmem()] * 2,
        scratch_shapes=[pltpu.VMEM((stack, WIDTH), jnp.float32)] * 2
        + [pltpu.VMEM((5, stack, WIDTH), jnp.float32)]
        + [
            pltpu.VMEM((3 * 2 * RIM * ROW, WIDTH), jnp.bfloat16),
            pltpu.VMEM((3 * tall, WIDTH), jnp.float32),
        ],
        compiler_params=params(14),
        name="rim",
    )(below, above, head, tail, mask, edge, first)


def relay_kernel(in_ref, out_ref):
    a = jnp.max(in_ref[...].reshape(in_ref.shape[0], WIDTH), axis=0, keepdims=True)
    out_ref[...] = jnp.broadcast_to(a.reshape(1, 1, WIDTH), out_ref.shape)


def relay(tiles, count):
    return pl.pallas_call(
        relay_kernel,
        out_shape=jax.ShapeDtypeStruct((count, 1, WIDTH), jnp.float32),
        in_specs=[in_vmem()],
        out_specs=in_vmem(),
        compiler_params=params(1),
        name="relay",
    )(tiles)


STEP_X = 8


def finish_kernel(peaks_ref, core_ref, rim_ref, out_ref):
    x0 = pl.program_id(0) * STEP_X
    peak = jnp.sqrt(jnp.max(peaks_ref[...].reshape(peaks_ref.shape[0], WIDTH), axis=0, keepdims=True))
    scale = step_length / (peak + peak_eps)
    z = lax.broadcasted_iota(jnp.int32, (SIDE, WIDTH), 0)
    at_rim = (z < RIM) | (z >= SIDE - RIM)
    for c in range(3):
        for x in range(STEP_X):
            rows = pl.ds(pl.multiple_of((c * SIDE + x0 + x) * SIDE, SIDE), SIDE)
            out_ref[c, x] = jnp.where(at_rim, rim_ref[rows, :], core_ref[rows, :]) * scale


def finish(peaks, core, rims):
    return pl.pallas_call(
        finish_kernel,
        out_shape=jax.ShapeDtypeStruct((3, SIDE, SIDE, WIDTH), jnp.float32),
        grid=(SIDE // STEP_X,),
        in_specs=[in_vmem()] * 3,
        out_specs=pl.BlockSpec((3, STEP_X, SIDE, WIDTH), lambda i: (0, i, 0, 0)),
        compiler_params=params(12),
        name="finish",
    )(peaks, core, rims)


def per_device(fixed_image, moving_image, fetch_owner, fetch_block, fetch_count, interp_level, block_mask):
    side, width = SIDE, WIDTH
    sent = pack(fetch_owner, fetch_block, fetch_count, interp_level.transpose(0, 1, 3, 2, 4), moving_image)
    got = lax.all_to_all(sent, "blk", split_axis=0, concat_axis=0, tiled=True)

    mask_row = jnp.repeat(block_mask.reshape(BLOCKS), side).astype(jnp.bfloat16)[None]
    last = jnp.concatenate([fixed_image[side - RIM :].reshape(-1, width), mask_row], axis=0)
    first = jnp.concatenate([fixed_image[:RIM].reshape(-1, width), mask_row], axis=0)
    left = lax.ppermute(last, "blk", shift_up("blk"))
    right = lax.ppermute(first, "blk", shift_down("blk"))
    turn = lambda a: a[:-1].reshape(RIM, side, width)
    fixed = jnp.concatenate(
        [fixed_image, turn(right), jnp.zeros((ROW - EXT, side, width), jnp.bfloat16), turn(left)], axis=0
    ).transpose(1, 0, 2)
    masks = jnp.concatenate([mask_row, right[-1:], left[-1:], jnp.zeros((5, width), jnp.bfloat16)], axis=0)
    mean, away, gain = fixed_part(fixed.reshape(side * ROW, width), masks)

    half = (lax.axis_index("blk") % 2).astype(jnp.int32).reshape(1)
    warped = lax.all_to_all(hold(half, got), "blk", split_axis=0, concat_axis=0, tiled=True)

    def z_rows(pairs):
        part = warped.reshape(side // DEEP, 2, DEEP, PART, width)[pairs]
        rows = [part[:, 0, :, :HALF], part[:, 1, :, :HALF], part[:, 0, :, HALF:], part[:, 1, :, HALF:]]
        return jnp.concatenate(rows, axis=2).reshape(-1, ROW, width)

    def message(moving_rows, fixed_rows):
        return jnp.concatenate([moving_rows.reshape(-1, width), fixed_rows.reshape(-1, width), masks], axis=0)

    tail = message(z_rows(slice(side // DEEP - 3, None))[1:], fixed[side - RIM :])
    head = message(z_rows(slice(0, 3))[:RIM], fixed[:RIM])
    below = lax.ppermute(tail, "slab", shift_up("slab"))
    above = lax.ppermute(head, "slab", shift_down("slab"))
    core, edge, top = inner(warped.reshape(side * ROW, width), fixed.reshape(side * ROW, width), mean, away, gain)
    rims, peak = rim(below, above, head, tail, masks, edge, top)
    peak = lax.all_to_all(peak, "blk", split_axis=0, concat_axis=0, tiled=True)
    peak = relay(peak, lax.axis_size("slab"))
    peak = lax.all_to_all(peak, "slab", split_axis=0, concat_axis=0, tiled=True)
    return finish(peak, core, rims)


def solution(mesh):
    in_specs = (
        P("blk", "slab", None),
        P("blk", "slab", None),
        P("blk", "slab", None, None),
        P("blk", "slab", None, None),
        P("blk", "slab", None),
        P("blk", "slab", None, None, None),
        P("blk", "slab", None),
    )
    return jax.shard_map(
        per_device, mesh=mesh, in_specs=in_specs, out_specs=P(None, "blk", "slab", None), check_vma=False
    )
```

```python
import math

import jax
import jax.numpy as jnp
from jax import lax
from jax.experimental import pallas as pl
from jax.experimental.pallas import tpu as pltpu
from jax.sharding import PartitionSpec as P

LEVELS = 8
BOX_RADIUS = 2
SMOOTH_RADIUS = 3
RIM = BOX_RADIUS + SMOOTH_RADIUS

sigma_smooth = 1.5
step_length = 2.0
var_eps = 1e-05
peak_eps = 1e-06


def smooth_weights(radius):
    raw = [math.exp(-(t * t) / (2.0 * sigma_smooth * sigma_smooth)) for t in range(-radius, radius + 1)]
    total = sum(raw)
    return [one / total for one in raw]


def shift_up(axis):
    n = lax.axis_size(axis)
    return [(i, i + 1) for i in range(n - 1)]


def shift_down(axis):
    n = lax.axis_size(axis)
    return [(i + 1, i) for i in range(n - 1)]


SIDE = 32
WIDTH = 128
BLOCKS = WIDTH // SIDE
SLOTS = 4
OWNERS = 32
DEEP = 2
HALF = SIDE // 2
TAKEN = DEEP + 1
SENT = TAKEN * HALF + TAKEN + 1
PITCH = 56
EXT = SIDE + 2 * RIM
OUT_PITCH = 48
PART = OUT_PITCH // DEEP
MID = SIDE + 2 * SMOOTH_RADIUS
INNER = SIDE - 2 * BOX_RADIUS
CORE = INNER - 2 * SMOOTH_RADIUS
ROW = OUT_PITCH
THIN = 40
MIB = 1 << 20


def params(mib):
    return pltpu.CompilerParams(vmem_limit_bytes=mib * MIB)


def cost(flops, nbytes):
    return pl.CostEstimate(flops=flops, bytes_accessed=nbytes, transcendentals=0)


def in_vmem():
    return pl.BlockSpec(memory_space=pltpu.VMEM)


def in_smem():
    return pl.BlockSpec(memory_space=pltpu.SMEM)


def pack_kernel(owner_ref, block_ref, count_ref, level_ref, moving_ref, out_ref, wide):
    lane = lax.broadcasted_iota(jnp.int32, (TAKEN + 1, WIDTH), 1)
    row = jnp.zeros((TAKEN + 1, WIDTH), jnp.int32)
    e = BLOCKS * SLOTS
    for g in range(BLOCKS):
        count = count_ref[0, 0, g]
        row = jnp.where(lane == 4 * e + g, count, row)
        for k in range(SLOTS):
            name = block_ref[0, 0, g, k] * OWNERS + owner_ref[0, 0, g, k]
            row = jnp.where(lane == g * SLOTS + k, jnp.where(k < count, name, -1), row)
            for axis in range(3):
                at = e + (g * 3 + axis) * SLOTS + k
                row = jnp.where(lane == at, level_ref[0, 0, axis, g, k], row)
    row = row.astype(jnp.float32)
    for x in range(SIDE):
        wide[pl.ds(x * SIDE, SIDE), :] = moving_ref[x].astype(jnp.float32)
    place = lax.broadcasted_iota(jnp.int32, (TAKEN + 1, WIDTH), 0)
    for z in range(SIDE):
        plane = wide[pl.ds(z, SIDE, stride=SIDE), :].astype(jnp.bfloat16)
        spots = [(z // DEEP, z % DEEP)]
        if z % DEEP == 0 and z > 0:
            spots.append((z // DEEP - 1, DEEP))
        if z == SIDE - 1:
            spots.append((z // DEEP, DEEP))
        for pair, at in spots:
            for half in range(2):
                out_ref[pair * 2 + half, at * HALF : (at + 1) * HALF, :] = plane[half * HALF : (half + 1) * HALF]
    for pair in range(SIDE // DEEP):
        for half in range(2):
            x = min((half + 1) * HALF, SIDE - 1)
            if pair < SIDE // DEEP - 1:
                extra = wide[pl.ds(x * SIDE + pair * DEEP, TAKEN + 1), :]
            else:
                two = wide[pl.ds(x * SIDE + pair * DEEP, DEEP), :]
                extra = jnp.concatenate([two, two[1:2], two[1:2]], axis=0)
            extra = jnp.where(place == TAKEN, row, extra)
            out_ref[pair * 2 + half, TAKEN * HALF : SENT, :] = extra.astype(jnp.bfloat16)


def pack(owner, block, count, level, moving):
    return pl.pallas_call(
        pack_kernel,
        out_shape=jax.ShapeDtypeStruct((OWNERS, SENT, WIDTH), jnp.bfloat16),
        in_specs=[in_smem()] * 4 + [in_vmem()],
        out_specs=in_vmem(),
        scratch_shapes=[pltpu.VMEM((SIDE * SIDE, WIDTH), jnp.float32)],
        name="pack",
    )(owner, block, count, level, moving)


def exchange_groups(parts, lane):
    parts = list(parts)
    low = lane < 2 * SIDE
    for a in range(2):
        p, q = parts[a], parts[a + 2]
        r = pltpu.roll(jnp.where(low, q, p), 2 * SIDE, 1)
        parts[a], parts[a + 2] = jnp.where(low, p, r), jnp.where(low, r, q)
    even = (lane // SIDE) % 2 == 0
    for a in (0, 2):
        p, q = parts[a], parts[a + 1]
        parts[a] = jnp.where(even, p, pltpu.roll(q, SIDE, 1))
        parts[a + 1] = jnp.where(even, pltpu.roll(p, WIDTH - SIDE, 1), q)
    return parts


def column(a, i):
    return jnp.broadcast_to(a[:, i : i + 1], a.shape)


def hold_kernel(half_ref, got_ref, out_ref, wide, source, coef, mixed, spread):
    strip = HALF // BLOCKS
    rows = OWNERS * BLOCKS
    lane = lax.broadcasted_iota(jnp.int32, (OWNERS, WIDTH), 1)
    last_y = lane % SIDE == SIDE - 1
    for o in range(OWNERS):
        wide[pl.ds(o * PITCH, SENT), :] = got_ref[o].astype(jnp.float32)

    lists = wide[pl.ds(SENT - 1, OWNERS, stride=PITCH), :]
    where_k = lane.astype(jnp.float32)
    e = BLOCKS * SLOTS
    top = float(LEVELS)
    scales = []
    for g in range(BLOCKS):
        total = {}
        for k in range(SLOTS):
            at = g * SLOTS + k
            name = column(lists, at)
            base = e + g * 3 * SLOTS + k
            lx, lz, ly = (column(lists, base + a * SLOTS) for a in range(3))
            x1 = jnp.where(where_k == name, lx, 0.0)
            x0 = jnp.where(where_k == name, top - lx, 0.0)
            for dx in range(2):
                ax = x1 if dx else x0
                z1 = ax * lz
                for dz in range(2):
                    az = z1 if dz else top * ax - z1
                    y1 = az * ly
                    for dy in range(2):
                        ay = y1 if dy else top * az - y1
                        key = (dx, dz, dy)
                        total[key] = ay if k == 0 else total[key] + ay
        for (dx, dz, dy), c in total.items():
            hi = jnp.floor(c * (1.0 / 16.0)) * 16.0
            col = pl.ds(dy * WIDTH, WIDTH)
            coef[dz * 2 + dx, pl.ds(g * OWNERS, OWNERS), col] = hi.astype(jnp.bfloat16)
            coef[dz * 2 + dx, pl.ds(rows + g * OWNERS, OWNERS), col] = (c - hi).astype(jnp.bfloat16)
        scales.append((1.0 / column(lists, 4 * e + g)) * (1.0 / LEVELS**3))

    wrap = strip + 1
    for z in range(TAKEN):
        for t in range(wrap):
            at = [strip * q + t for q in range(BLOCKS)]
            parts = [
                wide[pl.ds(z * HALF + x if x < HALF else TAKEN * HALF + z, OWNERS, stride=PITCH), :] for x in at
            ]
            for g, u in enumerate(exchange_groups(parts, lane)):
                v = jnp.where(last_y, u, pltpu.roll(u, WIDTH - 1, 1))
                for dy, a in enumerate((u, v)):
                    source[pl.ds(dy * rows + g * OWNERS, OWNERS), pl.ds((z * wrap + t) * WIDTH, WIDTH)] = a.astype(
                        jnp.bfloat16
                    )

    piece = 2 * WIDTH
    for z in range(DEEP):
        for t in range(0, strip, 2):
            acc = None
            for dz in range(2):
                for dx in range(2):
                    col = ((z + dz) * wrap + t + dx) * WIDTH
                    one = jnp.dot(
                        coef[dz * 2 + dx], source[:, pl.ds(col, piece)], preferred_element_type=jnp.float32
                    )
                    acc = one if acc is None else acc + one
            for g in range(BLOCKS):
                lo = rows + g * OWNERS
                part = acc[g * OWNERS : (g + 1) * OWNERS] + acc[lo : lo + OWNERS]
                for i in range(2):
                    mixed[pl.ds(g * OWNERS, OWNERS), pl.ds((z * strip + t + i) * WIDTH, WIDTH)] = (
                        part[:, i * WIDTH : (i + 1) * WIDTH] * scales[g]
                    )

    for r in range(OWNERS):
        for z in range(DEEP):
            spread[pl.ds((r + 1) * OUT_PITCH + z * PART + HALF, PART - HALF), :] = jnp.zeros(
                (PART - HALF, WIDTH), jnp.float32
            )
    for z in range(DEEP):
        for t in range(strip):
            parts = [
                mixed[pl.ds(g * OWNERS, OWNERS), pl.ds((z * strip + t) * WIDTH, WIDTH)] for g in range(BLOCKS)
            ]
            for q, w in enumerate(exchange_groups(parts, lane)):
                spread[pl.ds(OUT_PITCH + z * PART + strip * q + t, OWNERS, stride=OUT_PITCH), :] = w
    half = half_ref[0]

    @pl.when(half == 0)
    def _():
        for z in range(DEEP):
            for k in range(RIM):
                w = spread[pl.ds(OUT_PITCH + z * PART + k, OWNERS, stride=OUT_PITCH), :]
                spread[pl.ds(z * PART + HALF + k, OWNERS, stride=OUT_PITCH), :] = w

    @pl.when(half == 1)
    def _():
        for z in range(DEEP):
            for k in range(RIM):
                w = spread[pl.ds(OUT_PITCH + z * PART + HALF - RIM + k, OWNERS, stride=OUT_PITCH), :]
                spread[pl.ds(2 * OUT_PITCH + z * PART + PART - RIM + k, OWNERS, stride=OUT_PITCH), :] = w

    for r in range(OWNERS):
        out_ref[r] = spread[pl.ds((r + 1) * OUT_PITCH, OUT_PITCH), :].astype(jnp.bfloat16)


def hold(half, got):
    strip = HALF // BLOCKS
    rows = OWNERS * BLOCKS
    return pl.pallas_call(
        hold_kernel,
        out_shape=jax.ShapeDtypeStruct((OWNERS, OUT_PITCH, WIDTH), jnp.bfloat16),
        in_specs=[in_smem(), in_vmem()],
        out_specs=in_vmem(),
        scratch_shapes=[
            pltpu.VMEM((OWNERS * PITCH, WIDTH), jnp.float32),
            pltpu.VMEM((2 * rows, TAKEN * (strip + 1) * WIDTH), jnp.bfloat16),
            pltpu.VMEM((4, 2 * rows, 2 * rows), jnp.bfloat16),
            pltpu.VMEM((rows, DEEP * strip * WIDTH), jnp.float32),
            pltpu.VMEM(((OWNERS + 2) * OUT_PITCH, WIDTH), jnp.float32),
        ],
        compiler_params=params(12),
        name="hold",
    )(half, got)


def distance():
    i = lax.broadcasted_iota(jnp.int32, (WIDTH, WIDTH), 0)
    j = lax.broadcasted_iota(jnp.int32, (WIDTH, WIDTH), 1)
    return jnp.abs(i - j)


def box_band():
    one = jnp.where(distance() <= BOX_RADIUS, 1.0, 0.0).astype(jnp.bfloat16)
    return one, jnp.concatenate([one, one], axis=0)


def smooth_band():
    d = distance()
    taps = smooth_weights(SMOOTH_RADIUS)
    left = jnp.zeros((WIDTH, WIDTH), jnp.float32)
    for t in range(SMOOTH_RADIUS + 1):
        left = jnp.where(d == t, taps[SMOOTH_RADIUS + t], left)
    parts = []
    for _ in range(2):
        part = left.astype(jnp.bfloat16)
        parts.append(part)
        left = left - part.astype(jnp.float32)
    return jnp.concatenate(parts, axis=0)


def times(a, band):
    return jnp.dot(a, band, preferred_element_type=jnp.float32)


def halves(product):
    hi = product.astype(jnp.bfloat16)
    return jnp.concatenate([hi, (product - hi.astype(jnp.float32)).astype(jnp.bfloat16)], axis=1)


def rows_at(i):
    if isinstance(i, int):
        return pl.ds(i * ROW, ROW)
    return pl.ds(pl.multiple_of(i * ROW, ROW), ROW)


def thin_at(i):
    if isinstance(i, int):
        return pl.ds(i * THIN, THIN)
    return pl.ds(pl.multiple_of(i * THIN, 8), THIN)


def along(a, step):
    return pltpu.roll(a, (-step) % a.shape[0], 0)


def thin(a):
    x = lax.broadcasted_iota(jnp.int32, (8, WIDTH), 0)
    return jnp.concatenate([a[:SIDE], jnp.where(x < 4, a[SIDE:THIN], a[THIN:])], axis=0)


def box_x(a):
    two = a + along(a, -1)
    return thin((along(two, -1) + a) + along(two, 2)) * (1.0 / (2 * BOX_RADIUS + 1) ** 3)


def box_zx(ref, which, i, count):
    r = [ref[which, rows_at(i + t), :] for t in range(2 * BOX_RADIUS + count)]
    if count == 1:
        return [box_x(((r[0] + r[1]) + (r[2] + r[3])) + r[4])]
    mid = (r[1] + r[2]) + (r[3] + r[4])
    return [box_x(r[0] + mid), box_x(mid + r[5])]


def mask_rows(ref):
    x = lax.broadcasted_iota(jnp.int32, (THIN, WIDTH), 0)
    m = ref[...].astype(jnp.float32)
    right = jnp.where(x < SIDE + SMOOTH_RADIUS, m[1:2], 0.0)
    return jnp.where(x < SIDE, m[0:1], jnp.where(x >= THIN - SMOOTH_RADIUS, m[2:3], right))


def fixed_sums(f, sums, q, rows, bands):
    sums[q, rows, :] = times(f, bands[0])
    wide = f.astype(jnp.float32)
    sums[q + 1, rows, :] = times(halves(wide * wide), bands[1])


def fixed_rows(sums, q, i, here, mask):
    means = box_zx(sums, q, i, len(here))
    squares = box_zx(sums, q + 1, i, len(here))
    out = []
    for h, m, p, sq in zip(here, mask, means, squares):
        out.append((p, h - p, m / (sq - p * p + var_eps)))
    return out


def fixed_kernel(fixed_ref, mask_ref, mean_ref, away_ref, gain_ref, sums):
    bands = box_band()
    chunk = 8 * ROW

    def by_y(i, carry):
        rows = pl.ds(pl.multiple_of(i * chunk, chunk), chunk)
        fixed_sums(fixed_ref[rows, :], sums, 0, rows, bands)
        return carry

    lax.fori_loop(0, SIDE // 8, by_y, 0)
    mask = mask_rows(mask_ref)

    def by_z(step, carry):
        i = 2 * step
        here = [thin(fixed_ref[rows_at(i + BOX_RADIUS + t), :].astype(jnp.float32)) for t in range(2)]
        for t, (mean, away, gain) in enumerate(fixed_rows(sums, 0, i, here, [mask, mask])):
            mean_ref[thin_at(i + t), :] = mean
            away_ref[thin_at(i + t), :] = away
            gain_ref[thin_at(i + t), :] = gain
        return carry

    lax.fori_loop(0, INNER // 2, by_z, 0)


def fixed_part(fixed, mask):
    out = jax.ShapeDtypeStruct((INNER * THIN, WIDTH), jnp.float32)
    return pl.pallas_call(
        fixed_kernel,
        out_shape=[out] * 3,
        in_specs=[in_vmem()] * 2,
        out_specs=[in_vmem()] * 3,
        scratch_shapes=[pltpu.VMEM((2, SIDE * ROW, WIDTH), jnp.float32)],
        compiler_params=params(8),
        cost_estimate=cost(5_000_000_000, 4_000_000),
        name="fixed_part",
    )(fixed, mask)


def sums_by_y(f, wide, sums, rows, bands, with_fixed):
    mw = wide[rows, :]
    fw = f.astype(jnp.float32)
    n = mw.shape[0]
    plain = [mw.astype(jnp.bfloat16)] + ([f] if with_fixed else [])
    pairs = [mw * mw, mw * fw] + ([fw * fw] if with_fixed else [])
    one = times(jnp.concatenate(plain, axis=0), bands[0])
    two = times(jnp.concatenate([halves(p) for p in pairs], axis=0), bands[1])
    sums[0, rows, :] = one[:n]
    sums[1, rows, :] = two[:n]
    sums[2, rows, :] = two[n : 2 * n]
    if with_fixed:
        sums[3, rows, :] = one[n:]
        sums[4, rows, :] = two[2 * n :]


def force_rows(wide, sums, i, fixed, force, k, pitch):
    count = len(fixed)
    means = box_zx(sums, 0, i, count)
    squares = box_zx(sums, 1, i, count)
    products = box_zx(sums, 2, i, count)
    lane = lax.broadcasted_iota(jnp.int32, (THIN, WIDTH), 1)
    at = [thin(wide[rows_at(i + BOX_RADIUS - 1 + t), :]) for t in range(count + 2)]
    for t, (mean_f, away, gain) in enumerate(fixed):
        mean = means[t]
        q = (products[t] - mean_f * mean) / (squares[t] - mean * mean + var_eps)
        m = at[t + 1]
        term = gain * q * (away - q * (m - mean))
        up = jnp.where(lane == WIDTH - 1, 0.0, pltpu.roll(m, WIDTH - 1, 1))
        down = jnp.where(lane == 0, 0.0, pltpu.roll(m, 1, 1))
        steps = (along(m, 1) - along(m, -1), at[t + 2] - at[t], up - down)
        for c in range(3):
            force[thin_at(c * pitch + k + t), :] = term * steps[c]


def smooth_rows(smooth_y, pitch, i, out_ref, z, count, peak):
    taps = smooth_weights(SMOOTH_RADIUS)[SMOOTH_RADIUS:]
    mid = SMOOTH_RADIUS
    total = [None] * count
    for c in range(3):
        g = [smooth_y[thin_at(c * pitch + i + t), :] for t in range(2 * SMOOTH_RADIUS + count)]
        for n in range(count):
            s = taps[0] * g[n + mid]
            for t in range(1, SMOOTH_RADIUS + 1):
                s += taps[t] * (g[n + mid - t] + g[n + mid + t])
            a = taps[0] * s
            for t in range(1, SMOOTH_RADIUS + 1):
                a += taps[t] * (along(s, -t) + along(s, t))
            a = a[:SIDE]
            out_ref[pl.ds(c * SIDE * SIDE + z + n, SIDE, stride=SIDE), :] = a
            total[n] = a * a if c == 0 else total[n] + a * a
    for one in total:
        peak = jnp.maximum(peak, one)
    return peak


def smooth_along_y(force, i, pitch, count, out, j, out_pitch, double):
    f = [force[pl.ds((c * pitch + i) * THIN, count * THIN), :].astype(jnp.bfloat16) for c in range(3)]
    f = jnp.concatenate(f, axis=0)
    g = times(jnp.concatenate([f, f], axis=1), double)
    for c in range(3):
        out[pl.ds((c * out_pitch + j) * THIN, count * THIN), :] = g[c * count * THIN : (c + 1) * count * THIN]


def inner_kernel(warped_ref, fixed_ref, mean_ref, away_ref, gain_ref, out_ref, edge_ref, peak_ref, wide, sums, force, smooth_y):
    bands = box_band()
    double = smooth_band()
    step = 4

    def by_y(n):
        for pair in range(n * step // DEEP, (n + 1) * step // DEEP):
            for half in range(2):
                for z in range(DEEP):
                    src = (pair * 2 + half) * OUT_PITCH + z * PART
                    dst = (pair * DEEP + z) * ROW
                    own = warped_ref[pl.ds(src, HALF), :]
                    wide[pl.ds(dst + half * HALF, HALF), :] = own.astype(jnp.float32)
                    side = warped_ref[pl.ds(src + HALF, 8), :]
                    wide[pl.ds(dst + SIDE + 8 * half, 8), :] = side.astype(jnp.float32)
        rows = pl.ds(n * step * ROW, step * ROW)
        sums_by_y(fixed_ref[rows, :], wide, sums, rows, bands, False)

    by_y(0)
    peak = jnp.zeros((SIDE, WIDTH), jnp.float32)
    done = 0
    for n in range(INNER // step):
        by_y(n + 1)
        for i in range(n * step, (n + 1) * step, 2):
            fixed = [
                (mean_ref[thin_at(i + t), :], away_ref[thin_at(i + t), :], gain_ref[thin_at(i + t), :])
                for t in range(2)
            ]
            force_rows(wide, sums, i, fixed, force, i, INNER)
        smooth_along_y(force, n * step, INNER, step, smooth_y, n * step, INNER, double)
        while done + 1 + 2 * SMOOTH_RADIUS < (n + 1) * step:
            peak = smooth_rows(smooth_y, INNER, done, out_ref, done + RIM, 2, peak)
            done += 2
    kept = 2 * SMOOTH_RADIUS * THIN
    for c in range(3):
        at = c * INNER * THIN
        edge_ref[c, 0:kept, :] = smooth_y[at : at + kept, :]
        edge_ref[c, kept : 2 * kept, :] = smooth_y[at + INNER * THIN - kept : at + INNER * THIN, :]
    peak_ref[...] = peak


def rim_kernel(
    below_ref, above_ref, head_ref, tail_ref, mask_ref, edge_ref, first_ref,
    out_ref, peak_ref, wide, fwide, sums, force, smooth_y,
):
    bands = box_band()
    double = smooth_band()
    own = RIM - 1
    stack = RIM + own
    for ref, start, count, at in (
        (below_ref, 0, RIM, 0),
        (head_ref, 0, own, RIM),
        (tail_ref, RIM - own, own, stack),
        (above_ref, 0, RIM, stack + own),
    ):
        rows = pl.ds(at * ROW, count * ROW)
        wide[rows, :] = ref[pl.ds(start * ROW, count * ROW), :].astype(jnp.float32)
        fwide[rows, :] = ref[pl.ds((RIM + start) * ROW, count * ROW), :].astype(jnp.float32)
    last = pl.ds(2 * RIM * ROW, 8)
    masks = [mask_rows(below_ref.at[last, :]), mask_rows(mask_ref), mask_rows(above_ref.at[last, :])]
    kept = 2 * SMOOTH_RADIUS
    tall = RIM + kept
    for side in range(2):
        for c in range(3):
            old = c * 2 * tall + side * tall + (0 if side else RIM)
            smooth_y[pl.ds(old * THIN, kept * THIN), :] = edge_ref[c, pl.ds(side * kept * THIN, kept * THIN), :]
        for n in range(stack // 3):
            rows = pl.ds((side * stack + 3 * n) * ROW, 3 * ROW)
            sums_by_y(fwide[rows, :].astype(jnp.bfloat16), wide, sums, rows, bands, True)
    for i, count in ((0, 2), (2, 1), (3, 2)):
        for side in range(2):
            first = stack * side + i
            mask = []
            for t in range(i, i + count):
                outer = t < SMOOTH_RADIUS if side == 0 else t >= RIM - SMOOTH_RADIUS
                mask.append(masks[2 * side] if outer else masks[1])
            here = [thin(fwide[rows_at(first + BOX_RADIUS + t), :]) for t in range(count)]
            fixed = fixed_rows(sums, 3, first, here, mask)
            force_rows(wide, sums, first, fixed, force, i + RIM * side, 2 * RIM)
    peak = first_ref[...]
    for side in range(2):
        new = side * tall + (kept if side else 0)
        smooth_along_y(force, side * RIM, 2 * RIM, RIM, smooth_y, new, 2 * tall, double)
    for i, count in ((0, 2), (2, 2), (4, 1)):
        for side in range(2):
            peak = smooth_rows(smooth_y, 2 * tall, tall * side + i, out_ref, (SIDE - RIM) * side + i, count, peak)
    top = jnp.max(jnp.max(peak, axis=0, keepdims=True), axis=1, keepdims=True)
    peak_ref[...] = jnp.broadcast_to(top.reshape(1, 1, 1), peak_ref.shape)


def inner(warped, fixed, mean, away, gain):
    return pl.pallas_call(
        inner_kernel,
        out_shape=[
            jax.ShapeDtypeStruct((3 * SIDE * SIDE, WIDTH), jnp.float32),
            jax.ShapeDtypeStruct((3, 4 * SMOOTH_RADIUS * THIN, WIDTH), jnp.float32),
            jax.ShapeDtypeStruct((SIDE, WIDTH), jnp.float32),
        ],
        in_specs=[in_vmem()] * 5,
        out_specs=[in_vmem()] * 3,
        scratch_shapes=[
            pltpu.VMEM((SIDE * ROW, WIDTH), jnp.float32),
            pltpu.VMEM((3, SIDE * ROW, WIDTH), jnp.float32),
            pltpu.VMEM((3 * INNER * THIN, WIDTH), jnp.float32),
            pltpu.VMEM((3 * INNER * THIN, WIDTH), jnp.float32),
        ],
        compiler_params=params(14),
        cost_estimate=cost(10_000_000_000, 8_000_000),
        name="inner",
    )(warped, fixed, mean, away, gain)


def rim(below, above, head, tail, mask, edge, first):
    stack = 2 * (2 * RIM - 1) * ROW
    tall = 2 * (RIM + 2 * SMOOTH_RADIUS) * THIN
    return pl.pallas_call(
        rim_kernel,
        out_shape=[
            jax.ShapeDtypeStruct((3 * SIDE * SIDE, WIDTH), jnp.float32),
            jax.ShapeDtypeStruct((OWNERS, 1, WIDTH), jnp.float32),
        ],
        in_specs=[in_vmem()] * 7,
        out_specs=[in_vmem()] * 2,
        scratch_shapes=[pltpu.VMEM((stack, WIDTH), jnp.float32)] * 2
        + [pltpu.VMEM((5, stack, WIDTH), jnp.float32)]
        + [
            pltpu.VMEM((3 * 2 * RIM * THIN, WIDTH), jnp.float32),
            pltpu.VMEM((3 * tall, WIDTH), jnp.float32),
        ],
        compiler_params=params(14),
        name="rim",
    )(below, above, head, tail, mask, edge, first)


def relay_kernel(in_ref, out_ref):
    a = jnp.max(in_ref[...].reshape(in_ref.shape[0], WIDTH), axis=0, keepdims=True)
    out_ref[...] = jnp.broadcast_to(a.reshape(1, 1, WIDTH), out_ref.shape)


def relay(tiles, count):
    return pl.pallas_call(
        relay_kernel,
        out_shape=jax.ShapeDtypeStruct((count, 1, WIDTH), jnp.float32),
        in_specs=[in_vmem()],
        out_specs=in_vmem(),
        compiler_params=params(1),
        name="relay",
    )(tiles)


STEP_X = 8


def finish_kernel(peaks_ref, core_ref, rim_ref, out_ref):
    x0 = pl.program_id(0) * STEP_X
    peak = jnp.sqrt(jnp.max(peaks_ref[...].reshape(peaks_ref.shape[0], WIDTH), axis=0, keepdims=True))
    scale = step_length / (peak + peak_eps)
    z = lax.broadcasted_iota(jnp.int32, (SIDE, WIDTH), 0)
    at_rim = (z < RIM) | (z >= SIDE - RIM)
    for c in range(3):
        for x in range(STEP_X):
            rows = pl.ds(pl.multiple_of((c * SIDE + x0 + x) * SIDE, SIDE), SIDE)
            out_ref[c, x] = jnp.where(at_rim, rim_ref[rows, :], core_ref[rows, :]) * scale


def finish(peaks, core, rims):
    return pl.pallas_call(
        finish_kernel,
        out_shape=jax.ShapeDtypeStruct((3, SIDE, SIDE, WIDTH), jnp.float32),
        grid=(SIDE // STEP_X,),
        in_specs=[in_vmem()] * 3,
        out_specs=pl.BlockSpec((3, STEP_X, SIDE, WIDTH), lambda i: (0, i, 0, 0)),
        compiler_params=params(12),
        name="finish",
    )(peaks, core, rims)


def per_device(fixed_image, moving_image, fetch_owner, fetch_block, fetch_count, interp_level, block_mask):
    side, width = SIDE, WIDTH
    sent = pack(fetch_owner, fetch_block, fetch_count, interp_level.transpose(0, 1, 3, 2, 4), moving_image)
    got = lax.all_to_all(sent, "blk", split_axis=0, concat_axis=0, tiled=True)

    mask_row = jnp.repeat(block_mask.reshape(BLOCKS), side).astype(jnp.bfloat16)[None]
    last = jnp.concatenate([fixed_image[side - RIM :].reshape(-1, width), mask_row], axis=0)
    first = jnp.concatenate([fixed_image[:RIM].reshape(-1, width), mask_row], axis=0)
    left = lax.ppermute(last, "blk", shift_up("blk"))
    right = lax.ppermute(first, "blk", shift_down("blk"))
    turn = lambda a: a[:-1].reshape(RIM, side, width)
    fixed = jnp.concatenate(
        [fixed_image, turn(right), jnp.zeros((ROW - EXT, side, width), jnp.bfloat16), turn(left)], axis=0
    ).transpose(1, 0, 2)
    masks = jnp.concatenate([mask_row, right[-1:], left[-1:], jnp.zeros((5, width), jnp.bfloat16)], axis=0)
    mean, away, gain = fixed_part(fixed.reshape(side * ROW, width), masks)

    half = (lax.axis_index("blk") % 2).astype(jnp.int32).reshape(1)
    warped = lax.all_to_all(hold(half, got), "blk", split_axis=0, concat_axis=0, tiled=True)

    def z_rows(pairs):
        part = warped.reshape(side // DEEP, 2, DEEP, PART, width)[pairs]
        rows = [part[:, 0, :, :HALF], part[:, 1, :, :HALF], part[:, 0, :, HALF:], part[:, 1, :, HALF:]]
        return jnp.concatenate(rows, axis=2).reshape(-1, ROW, width)

    def message(moving_rows, fixed_rows):
        return jnp.concatenate([moving_rows.reshape(-1, width), fixed_rows.reshape(-1, width), masks], axis=0)

    tail = message(z_rows(slice(side // DEEP - 3, None))[1:], fixed[side - RIM :])
    head = message(z_rows(slice(0, 3))[:RIM], fixed[:RIM])
    below = lax.ppermute(tail, "slab", shift_up("slab"))
    above = lax.ppermute(head, "slab", shift_down("slab"))
    core, edge, top = inner(warped.reshape(side * ROW, width), fixed.reshape(side * ROW, width), mean, away, gain)
    rims, peak = rim(below, above, head, tail, masks, edge, top)
    peak = lax.all_to_all(peak, "blk", split_axis=0, concat_axis=0, tiled=True)
    peak = relay(peak, lax.axis_size("slab"))
    peak = lax.all_to_all(peak, "slab", split_axis=0, concat_axis=0, tiled=True)
    return finish(peak, core, rims)


def solution(mesh):
    in_specs = (
        P("blk", "slab", None),
        P("blk", "slab", None),
        P("blk", "slab", None, None),
        P("blk", "slab", None, None),
        P("blk", "slab", None),
        P("blk", "slab", None, None, None),
        P("blk", "slab", None),
    )
    return jax.shard_map(
        per_device, mesh=mesh, in_specs=in_specs, out_specs=P(None, "blk", "slab", None), check_vma=False
    )
```

```python
import math

import jax
import jax.numpy as jnp
from jax import lax
from jax.experimental import pallas as pl
from jax.experimental.pallas import tpu as pltpu
from jax.sharding import PartitionSpec as P

LEVELS = 8
BOX_RADIUS = 2
SMOOTH_RADIUS = 3
RIM = BOX_RADIUS + SMOOTH_RADIUS

sigma_smooth = 1.5
step_length = 2.0
var_eps = 1e-05
peak_eps = 1e-06


def smooth_weights(radius):
    raw = [math.exp(-(t * t) / (2.0 * sigma_smooth * sigma_smooth)) for t in range(-radius, radius + 1)]
    total = sum(raw)
    return [one / total for one in raw]


def shift_up(axis):
    n = lax.axis_size(axis)
    return [(i, i + 1) for i in range(n - 1)]


def shift_down(axis):
    n = lax.axis_size(axis)
    return [(i + 1, i) for i in range(n - 1)]


SIDE = 32
WIDTH = 128
BLOCKS = WIDTH // SIDE
SLOTS = 4
OWNERS = 32
DEEP = 2
HALF = SIDE // 2
TAKEN = DEEP + 1
SENT = TAKEN * HALF + TAKEN + 1
PITCH = 56
EXT = SIDE + 2 * RIM
OUT_PITCH = 48
PART = OUT_PITCH // DEEP
MID = SIDE + 2 * SMOOTH_RADIUS
INNER = SIDE - 2 * BOX_RADIUS
CORE = INNER - 2 * SMOOTH_RADIUS
ROW = OUT_PITCH
THIN = 40
MIB = 1 << 20
STEP_X = 8


def params(mib):
    return pltpu.CompilerParams(vmem_limit_bytes=mib * MIB)


def cost(flops, nbytes):
    return pl.CostEstimate(flops=flops, bytes_accessed=nbytes, transcendentals=0)


def in_vmem():
    return pl.BlockSpec(memory_space=pltpu.VMEM)


def in_place():
    return pl.BlockSpec(memory_space=pl.ANY)


def in_smem():
    return pl.BlockSpec(memory_space=pltpu.SMEM)


def pack_kernel(owner_ref, block_ref, count_ref, level_ref, moving_ref, out_ref, wide, block, sems):
    lane = lax.broadcasted_iota(jnp.int32, (TAKEN + 1, WIDTH), 1)
    row = jnp.zeros((TAKEN + 1, WIDTH), jnp.int32)
    e = BLOCKS * SLOTS
    for g in range(BLOCKS):
        count = count_ref[0, 0, g]
        row = jnp.where(lane == 4 * e + g, count, row)
        for k in range(SLOTS):
            name = block_ref[0, 0, g, k] * OWNERS + owner_ref[0, 0, g, k]
            row = jnp.where(lane == g * SLOTS + k, jnp.where(k < count, name, -1), row)
            for axis in range(3):
                at = e + (g * 3 + axis) * SLOTS + k
                row = jnp.where(lane == at, level_ref[0, 0, axis, g, k], row)
    row = row.astype(jnp.float32)
    for x in range(SIDE):
        wide[pl.ds(x * SIDE, SIDE), :] = moving_ref[x].astype(jnp.float32)
    place = lax.broadcasted_iota(jnp.int32, (TAKEN + 1, WIDTH), 0)
    copies = []
    for pair in range(SIDE // DEEP):
        for at in range(TAKEN):
            z = min(pair * DEEP + at, SIDE - 1)
            plane = wide[pl.ds(z, SIDE, stride=SIDE), :].astype(jnp.bfloat16)
            for half in range(2):
                block[pair * 2 + half, at * HALF : (at + 1) * HALF, :] = plane[half * HALF : (half + 1) * HALF]
        for half in range(2):
            x = min((half + 1) * HALF, SIDE - 1)
            if pair < SIDE // DEEP - 1:
                extra = wide[pl.ds(x * SIDE + pair * DEEP, TAKEN + 1), :]
            else:
                two = wide[pl.ds(x * SIDE + pair * DEEP, DEEP), :]
                extra = jnp.concatenate([two, two[1:2], two[1:2]], axis=0)
            extra = jnp.where(place == TAKEN, row, extra)
            block[pair * 2 + half, TAKEN * HALF : SENT, :] = extra.astype(jnp.bfloat16)
        if pair % 4 == 3:
            at = pl.ds((pair - 3) * 2, 8)
            copies.append(pltpu.make_async_copy(block.at[at], out_ref.at[at], sems.at[len(copies)]))
            copies[-1].start()
    for copy in copies:
        copy.wait()


def pack(owner, block, count, level, moving):
    return pl.pallas_call(
        pack_kernel,
        out_shape=jax.ShapeDtypeStruct((OWNERS, SENT, WIDTH), jnp.bfloat16),
        in_specs=[in_smem()] * 4 + [in_vmem()],
        out_specs=in_place(),
        scratch_shapes=[
            pltpu.VMEM((SIDE * SIDE, WIDTH), jnp.float32),
            pltpu.VMEM((OWNERS, SENT, WIDTH), jnp.bfloat16),
            pltpu.SemaphoreType.DMA((4,)),
        ],
        name="pack",
    )(owner, block, count, level, moving)


def exchange_groups(parts, lane):
    parts = list(parts)
    low = lane < 2 * SIDE
    for a in range(2):
        p, q = parts[a], parts[a + 2]
        r = pltpu.roll(jnp.where(low, q, p), 2 * SIDE, 1)
        parts[a], parts[a + 2] = jnp.where(low, p, r), jnp.where(low, r, q)
    even = (lane // SIDE) % 2 == 0
    for a in (0, 2):
        p, q = parts[a], parts[a + 1]
        parts[a] = jnp.where(even, p, pltpu.roll(q, SIDE, 1))
        parts[a + 1] = jnp.where(even, pltpu.roll(p, WIDTH - SIDE, 1), q)
    return parts


def column(a, i):
    return jnp.broadcast_to(a[:, i : i + 1], a.shape)


def hold_kernel(half_ref, got_ref, out_ref, wide, source, coef, mixed, spread, block, sems):
    strip = HALF // BLOCKS
    rows = OWNERS * BLOCKS
    lane = lax.broadcasted_iota(jnp.int32, (OWNERS, WIDTH), 1)
    last_y = lane % SIDE == SIDE - 1
    for o in range(OWNERS):
        wide[pl.ds(o * PITCH, SENT), :] = got_ref[o].astype(jnp.float32)

    lists = wide[pl.ds(SENT - 1, OWNERS, stride=PITCH), :]
    where_k = lane.astype(jnp.float32)
    e = BLOCKS * SLOTS
    top = float(LEVELS)
    scales = []
    for g in range(BLOCKS):
        total = {}
        for k in range(SLOTS):
            at = g * SLOTS + k
            name = column(lists, at)
            base = e + g * 3 * SLOTS + k
            lx, lz, ly = (column(lists, base + a * SLOTS) for a in range(3))
            x1 = jnp.where(where_k == name, lx, 0.0)
            x0 = jnp.where(where_k == name, top - lx, 0.0)
            for dx in range(2):
                ax = x1 if dx else x0
                z1 = ax * lz
                for dz in range(2):
                    az = z1 if dz else top * ax - z1
                    y1 = az * ly
                    for dy in range(2):
                        ay = y1 if dy else top * az - y1
                        key = (dx, dz, dy)
                        total[key] = ay if k == 0 else total[key] + ay
        for (dx, dz, dy), c in total.items():
            hi = jnp.floor(c * (1.0 / 16.0)) * 16.0
            col = pl.ds(dy * WIDTH, WIDTH)
            coef[dz * 2 + dx, pl.ds(g * OWNERS, OWNERS), col] = hi.astype(jnp.bfloat16)
            coef[dz * 2 + dx, pl.ds(rows + g * OWNERS, OWNERS), col] = (c - hi).astype(jnp.bfloat16)
        scales.append((1.0 / column(lists, 4 * e + g)) * (1.0 / LEVELS**3))

    wrap = strip + 1
    for z in range(TAKEN):
        for t in range(wrap):
            at = [strip * q + t for q in range(BLOCKS)]
            parts = [
                wide[pl.ds(z * HALF + x if x < HALF else TAKEN * HALF + z, OWNERS, stride=PITCH), :] for x in at
            ]
            for g, u in enumerate(exchange_groups(parts, lane)):
                v = jnp.where(last_y, u, pltpu.roll(u, WIDTH - 1, 1))
                for dy, a in enumerate((u, v)):
                    source[pl.ds(dy * rows + g * OWNERS, OWNERS), pl.ds((z * wrap + t) * WIDTH, WIDTH)] = a.astype(
                        jnp.bfloat16
                    )

    piece = 2 * WIDTH
    for z in range(DEEP):
        for t in range(0, strip, 2):
            acc = None
            for dz in range(2):
                for dx in range(2):
                    col = ((z + dz) * wrap + t + dx) * WIDTH
                    one = jnp.dot(
                        coef[dz * 2 + dx], source[:, pl.ds(col, piece)], preferred_element_type=jnp.float32
                    )
                    acc = one if acc is None else acc + one
            for g in range(BLOCKS):
                lo = rows + g * OWNERS
                part = acc[g * OWNERS : (g + 1) * OWNERS] + acc[lo : lo + OWNERS]
                for i in range(2):
                    mixed[pl.ds(g * OWNERS, OWNERS), pl.ds((z * strip + t + i) * WIDTH, WIDTH)] = (
                        part[:, i * WIDTH : (i + 1) * WIDTH] * scales[g]
                    )

    for r in range(OWNERS):
        for z in range(DEEP):
            spread[pl.ds((r + 1) * OUT_PITCH + z * PART + HALF, PART - HALF), :] = jnp.zeros(
                (PART - HALF, WIDTH), jnp.float32
            )
    for z in range(DEEP):
        for t in range(strip):
            parts = [
                mixed[pl.ds(g * OWNERS, OWNERS), pl.ds((z * strip + t) * WIDTH, WIDTH)] for g in range(BLOCKS)
            ]
            for q, w in enumerate(exchange_groups(parts, lane)):
                spread[pl.ds(OUT_PITCH + z * PART + strip * q + t, OWNERS, stride=OUT_PITCH), :] = w
    half = half_ref[0]

    @pl.when(half == 0)
    def _():
        for z in range(DEEP):
            for k in range(RIM):
                w = spread[pl.ds(OUT_PITCH + z * PART + k, OWNERS, stride=OUT_PITCH), :]
                spread[pl.ds(z * PART + HALF + k, OWNERS, stride=OUT_PITCH), :] = w

    @pl.when(half == 1)
    def _():
        for z in range(DEEP):
            for k in range(RIM):
                w = spread[pl.ds(OUT_PITCH + z * PART + HALF - RIM + k, OWNERS, stride=OUT_PITCH), :]
                spread[pl.ds(2 * OUT_PITCH + z * PART + PART - RIM + k, OWNERS, stride=OUT_PITCH), :] = w

    copies = []
    for r in range(OWNERS):
        block[r] = spread[pl.ds((r + 1) * OUT_PITCH, OUT_PITCH), :].astype(jnp.bfloat16)
        if r % STEP_X == STEP_X - 1:
            at = pl.ds(r + 1 - STEP_X, STEP_X)
            copies.append(pltpu.make_async_copy(block.at[at], out_ref.at[at], sems.at[len(copies)]))
            copies[-1].start()
    for copy in copies:
        copy.wait()


def hold(half, got):
    strip = HALF // BLOCKS
    rows = OWNERS * BLOCKS
    return pl.pallas_call(
        hold_kernel,
        out_shape=jax.ShapeDtypeStruct((OWNERS, OUT_PITCH, WIDTH), jnp.bfloat16),
        in_specs=[in_smem(), in_vmem()],
        out_specs=in_place(),
        scratch_shapes=[
            pltpu.VMEM((OWNERS * PITCH, WIDTH), jnp.float32),
            pltpu.VMEM((2 * rows, TAKEN * (strip + 1) * WIDTH), jnp.bfloat16),
            pltpu.VMEM((4, 2 * rows, 2 * rows), jnp.bfloat16),
            pltpu.VMEM((rows, DEEP * strip * WIDTH), jnp.float32),
            pltpu.VMEM(((OWNERS + 2) * OUT_PITCH, WIDTH), jnp.float32),
            pltpu.VMEM((OWNERS, OUT_PITCH, WIDTH), jnp.bfloat16),
            pltpu.SemaphoreType.DMA((OWNERS // STEP_X,)),
        ],
        compiler_params=params(12),
        name="hold",
    )(half, got)


def distance():
    i = lax.broadcasted_iota(jnp.int32, (WIDTH, WIDTH), 0)
    j = lax.broadcasted_iota(jnp.int32, (WIDTH, WIDTH), 1)
    return jnp.abs(i - j)


def box_band():
    one = jnp.where(distance() <= BOX_RADIUS, 1.0, 0.0).astype(jnp.bfloat16)
    return one, jnp.concatenate([one, one], axis=0)


def smooth_band():
    d = distance()
    taps = smooth_weights(SMOOTH_RADIUS)
    left = jnp.zeros((WIDTH, WIDTH), jnp.float32)
    for t in range(SMOOTH_RADIUS + 1):
        left = jnp.where(d == t, taps[SMOOTH_RADIUS + t], left)
    parts = []
    for _ in range(2):
        part = left.astype(jnp.bfloat16)
        parts.append(part)
        left = left - part.astype(jnp.float32)
    return jnp.concatenate(parts, axis=0)


def times(a, band):
    return jnp.dot(a, band, preferred_element_type=jnp.float32)


def halves(product):
    hi = product.astype(jnp.bfloat16)
    return jnp.concatenate([hi, (product - hi.astype(jnp.float32)).astype(jnp.bfloat16)], axis=1)


def rows_at(i):
    if isinstance(i, int):
        return pl.ds(i * ROW, ROW)
    return pl.ds(pl.multiple_of(i * ROW, ROW), ROW)


def thin_at(i):
    if isinstance(i, int):
        return pl.ds(i * THIN, THIN)
    return pl.ds(pl.multiple_of(i * THIN, 8), THIN)


def along(a, step):
    return pltpu.roll(a, (-step) % a.shape[0], 0)


def thin(a):
    x = lax.broadcasted_iota(jnp.int32, (8, WIDTH), 0)
    return jnp.concatenate([a[:SIDE], jnp.where(x < 4, a[SIDE:THIN], a[THIN:])], axis=0)


def box_x(a):
    two = a + along(a, -1)
    return thin((along(two, -1) + a) + along(two, 2)) * (1.0 / (2 * BOX_RADIUS + 1) ** 3)


def box_zx(ref, which, i, count):
    r = [ref[which, rows_at(i + t), :] for t in range(2 * BOX_RADIUS + count)]
    if count == 1:
        return [box_x(((r[0] + r[1]) + (r[2] + r[3])) + r[4])]
    mid = (r[1] + r[2]) + (r[3] + r[4])
    return [box_x(r[0] + mid), box_x(mid + r[5])]


def mask_rows(ref):
    x = lax.broadcasted_iota(jnp.int32, (THIN, WIDTH), 0)
    m = ref[...].astype(jnp.float32)
    right = jnp.where(x < SIDE + SMOOTH_RADIUS, m[1:2], 0.0)
    return jnp.where(x < SIDE, m[0:1], jnp.where(x >= THIN - SMOOTH_RADIUS, m[2:3], right))


def fixed_sums(f, sums, q, rows, bands):
    sums[q, rows, :] = times(f, bands[0])
    wide = f.astype(jnp.float32)
    sums[q + 1, rows, :] = times(halves(wide * wide), bands[1])


def fixed_rows(sums, q, i, here, mask):
    means = box_zx(sums, q, i, len(here))
    squares = box_zx(sums, q + 1, i, len(here))
    out = []
    for h, m, p, sq in zip(here, mask, means, squares):
        out.append((p, h - p, m / (sq - p * p + var_eps)))
    return out


def fixed_kernel(fixed_ref, mask_ref, mean_ref, away_ref, gain_ref, sums):
    bands = box_band()
    chunk = 8 * ROW

    def by_y(i, carry):
        rows = pl.ds(pl.multiple_of(i * chunk, chunk), chunk)
        fixed_sums(fixed_ref[rows, :], sums, 0, rows, bands)
        return carry

    lax.fori_loop(0, SIDE // 8, by_y, 0)
    mask = mask_rows(mask_ref)

    def by_z(step, carry):
        i = 2 * step
        here = [thin(fixed_ref[rows_at(i + BOX_RADIUS + t), :].astype(jnp.float32)) for t in range(2)]
        for t, (mean, away, gain) in enumerate(fixed_rows(sums, 0, i, here, [mask, mask])):
            mean_ref[thin_at(i + t), :] = mean
            away_ref[thin_at(i + t), :] = away
            gain_ref[thin_at(i + t), :] = gain
        return carry

    lax.fori_loop(0, INNER // 2, by_z, 0)


def fixed_part(fixed, mask):
    out = jax.ShapeDtypeStruct((INNER * THIN, WIDTH), jnp.float32)
    return pl.pallas_call(
        fixed_kernel,
        out_shape=[out] * 3,
        in_specs=[in_vmem()] * 2,
        out_specs=[in_vmem()] * 3,
        scratch_shapes=[pltpu.VMEM((2, SIDE * ROW, WIDTH), jnp.float32)],
        compiler_params=params(8),
        cost_estimate=cost(5_000_000_000, 4_000_000),
        name="fixed_part",
    )(fixed, mask)


def sums_by_y(f, wide, sums, rows, bands, with_fixed):
    mw = wide[rows, :]
    fw = f.astype(jnp.float32)
    n = mw.shape[0]
    plain = [mw.astype(jnp.bfloat16)] + ([f] if with_fixed else [])
    pairs = [mw * mw, mw * fw] + ([fw * fw] if with_fixed else [])
    one = times(jnp.concatenate(plain, axis=0), bands[0])
    two = times(jnp.concatenate([halves(p) for p in pairs], axis=0), bands[1])
    sums[0, rows, :] = one[:n]
    sums[1, rows, :] = two[:n]
    sums[2, rows, :] = two[n : 2 * n]
    if with_fixed:
        sums[3, rows, :] = one[n:]
        sums[4, rows, :] = two[2 * n :]


def force_rows(wide, sums, i, fixed, force, k, pitch):
    count = len(fixed)
    means = box_zx(sums, 0, i, count)
    squares = box_zx(sums, 1, i, count)
    products = box_zx(sums, 2, i, count)
    lane = lax.broadcasted_iota(jnp.int32, (THIN, WIDTH), 1)
    at = [thin(wide[rows_at(i + BOX_RADIUS - 1 + t), :]) for t in range(count + 2)]
    for t, (mean_f, away, gain) in enumerate(fixed):
        mean = means[t]
        q = (products[t] - mean_f * mean) / (squares[t] - mean * mean + var_eps)
        m = at[t + 1]
        term = gain * q * (away - q * (m - mean))
        up = jnp.where(lane == WIDTH - 1, 0.0, pltpu.roll(m, WIDTH - 1, 1))
        down = jnp.where(lane == 0, 0.0, pltpu.roll(m, 1, 1))
        steps = (along(m, 1) - along(m, -1), at[t + 2] - at[t], up - down)
        for c in range(3):
            force[thin_at(c * pitch + k + t), :] = term * steps[c]


def smooth_rows(smooth_y, pitch, i, out_ref, z, count, peak):
    taps = smooth_weights(SMOOTH_RADIUS)[SMOOTH_RADIUS:]
    mid = SMOOTH_RADIUS
    total = [None] * count
    for c in range(3):
        g = [smooth_y[thin_at(c * pitch + i + t), :] for t in range(2 * SMOOTH_RADIUS + count)]
        for n in range(count):
            s = taps[0] * g[n + mid]
            for t in range(1, SMOOTH_RADIUS + 1):
                s += taps[t] * (g[n + mid - t] + g[n + mid + t])
            a = taps[0] * s
            for t in range(1, SMOOTH_RADIUS + 1):
                a += taps[t] * (along(s, -t) + along(s, t))
            a = a[:SIDE]
            out_ref[pl.ds(c * SIDE * SIDE + z + n, SIDE, stride=SIDE), :] = a
            total[n] = a * a if c == 0 else total[n] + a * a
    for one in total:
        peak = jnp.maximum(peak, one)
    return peak


def smooth_along_y(force, i, pitch, count, out, j, out_pitch, double):
    f = [force[pl.ds((c * pitch + i) * THIN, count * THIN), :].astype(jnp.bfloat16) for c in range(3)]
    f = jnp.concatenate(f, axis=0)
    g = times(jnp.concatenate([f, f], axis=1), double)
    for c in range(3):
        out[pl.ds((c * out_pitch + j) * THIN, count * THIN), :] = g[c * count * THIN : (c + 1) * count * THIN]


def inner_kernel(warped_ref, fixed_ref, mean_ref, away_ref, gain_ref, out_ref, edge_ref, peak_ref, wide, sums, force, smooth_y):
    bands = box_band()
    double = smooth_band()
    step = 4

    def by_y(n):
        for pair in range(n * step // DEEP, (n + 1) * step // DEEP):
            for half in range(2):
                for z in range(DEEP):
                    src = (pair * 2 + half) * OUT_PITCH + z * PART
                    dst = (pair * DEEP + z) * ROW
                    own = warped_ref[pl.ds(src, HALF), :]
                    wide[pl.ds(dst + half * HALF, HALF), :] = own.astype(jnp.float32)
                    side = warped_ref[pl.ds(src + HALF, 8), :]
                    wide[pl.ds(dst + SIDE + 8 * half, 8), :] = side.astype(jnp.float32)
        rows = pl.ds(n * step * ROW, step * ROW)
        sums_by_y(fixed_ref[rows, :], wide, sums, rows, bands, False)

    by_y(0)
    peak = jnp.zeros((SIDE, WIDTH), jnp.float32)
    done = 0
    for n in range(INNER // step):
        by_y(n + 1)
        for i in range(n * step, (n + 1) * step, 2):
            fixed = [
                (mean_ref[thin_at(i + t), :], away_ref[thin_at(i + t), :], gain_ref[thin_at(i + t), :])
                for t in range(2)
            ]
            force_rows(wide, sums, i, fixed, force, i, INNER)
        smooth_along_y(force, n * step, INNER, step, smooth_y, n * step, INNER, double)
        while done + 1 + 2 * SMOOTH_RADIUS < (n + 1) * step:
            peak = smooth_rows(smooth_y, INNER, done, out_ref, done + RIM, 2, peak)
            done += 2
    kept = 2 * SMOOTH_RADIUS * THIN
    for c in range(3):
        at = c * INNER * THIN
        edge_ref[c, 0:kept, :] = smooth_y[at : at + kept, :]
        edge_ref[c, kept : 2 * kept, :] = smooth_y[at + INNER * THIN - kept : at + INNER * THIN, :]
    peak_ref[...] = peak


def rim_kernel(
    below_ref, above_ref, head_ref, tail_ref, mask_ref, edge_ref, first_ref,
    out_ref, peak_ref, wide, fwide, sums, force, smooth_y,
):
    bands = box_band()
    double = smooth_band()
    own = RIM - 1
    stack = RIM + own
    for ref, start, count, at in (
        (below_ref, 0, RIM, 0),
        (head_ref, 0, own, RIM),
        (tail_ref, RIM - own, own, stack),
        (above_ref, 0, RIM, stack + own),
    ):
        rows = pl.ds(at * ROW, count * ROW)
        wide[rows, :] = ref[pl.ds(start * ROW, count * ROW), :].astype(jnp.float32)
        fwide[rows, :] = ref[pl.ds((RIM + start) * ROW, count * ROW), :].astype(jnp.float32)
    last = pl.ds(2 * RIM * ROW, 8)
    masks = [mask_rows(below_ref.at[last, :]), mask_rows(mask_ref), mask_rows(above_ref.at[last, :])]
    kept = 2 * SMOOTH_RADIUS
    tall = RIM + kept
    for side in range(2):
        for c in range(3):
            old = c * 2 * tall + side * tall + (0 if side else RIM)
            smooth_y[pl.ds(old * THIN, kept * THIN), :] = edge_ref[c, pl.ds(side * kept * THIN, kept * THIN), :]
        for n in range(stack // 3):
            rows = pl.ds((side * stack + 3 * n) * ROW, 3 * ROW)
            sums_by_y(fwide[rows, :].astype(jnp.bfloat16), wide, sums, rows, bands, True)
    for i, count in ((0, 2), (2, 1), (3, 2)):
        for side in range(2):
            first = stack * side + i
            mask = []
            for t in range(i, i + count):
                outer = t < SMOOTH_RADIUS if side == 0 else t >= RIM - SMOOTH_RADIUS
                mask.append(masks[2 * side] if outer else masks[1])
            here = [thin(fwide[rows_at(first + BOX_RADIUS + t), :]) for t in range(count)]
            fixed = fixed_rows(sums, 3, first, here, mask)
            force_rows(wide, sums, first, fixed, force, i + RIM * side, 2 * RIM)
    peak = first_ref[...]
    for side in range(2):
        new = side * tall + (kept if side else 0)
        smooth_along_y(force, side * RIM, 2 * RIM, RIM, smooth_y, new, 2 * tall, double)
    for i, count in ((0, 2), (2, 2), (4, 1)):
        for side in range(2):
            peak = smooth_rows(smooth_y, 2 * tall, tall * side + i, out_ref, (SIDE - RIM) * side + i, count, peak)
    top = jnp.max(jnp.max(peak, axis=0, keepdims=True), axis=1, keepdims=True)
    peak_ref[...] = jnp.broadcast_to(top.reshape(1, 1, 1), peak_ref.shape)


def inner(warped, fixed, mean, away, gain):
    return pl.pallas_call(
        inner_kernel,
        out_shape=[
            jax.ShapeDtypeStruct((3 * SIDE * SIDE, WIDTH), jnp.float32),
            jax.ShapeDtypeStruct((3, 4 * SMOOTH_RADIUS * THIN, WIDTH), jnp.float32),
            jax.ShapeDtypeStruct((SIDE, WIDTH), jnp.float32),
        ],
        in_specs=[in_vmem()] * 5,
        out_specs=[in_vmem()] * 3,
        scratch_shapes=[
            pltpu.VMEM((SIDE * ROW, WIDTH), jnp.float32),
            pltpu.VMEM((3, SIDE * ROW, WIDTH), jnp.float32),
            pltpu.VMEM((3 * INNER * THIN, WIDTH), jnp.float32),
            pltpu.VMEM((3 * INNER * THIN, WIDTH), jnp.float32),
        ],
        compiler_params=params(14),
        cost_estimate=cost(10_000_000_000, 8_000_000),
        name="inner",
    )(warped, fixed, mean, away, gain)


def rim(below, above, head, tail, mask, edge, first):
    stack = 2 * (2 * RIM - 1) * ROW
    tall = 2 * (RIM + 2 * SMOOTH_RADIUS) * THIN
    return pl.pallas_call(
        rim_kernel,
        out_shape=[
            jax.ShapeDtypeStruct((3 * SIDE * SIDE, WIDTH), jnp.float32),
            jax.ShapeDtypeStruct((OWNERS, 1, WIDTH), jnp.float32),
        ],
        in_specs=[in_vmem()] * 7,
        out_specs=[in_vmem()] * 2,
        scratch_shapes=[pltpu.VMEM((stack, WIDTH), jnp.float32)] * 2
        + [pltpu.VMEM((5, stack, WIDTH), jnp.float32)]
        + [
            pltpu.VMEM((3 * 2 * RIM * THIN, WIDTH), jnp.float32),
            pltpu.VMEM((3 * tall, WIDTH), jnp.float32),
        ],
        compiler_params=params(14),
        name="rim",
    )(below, above, head, tail, mask, edge, first)


def relay_kernel(in_ref, out_ref):
    a = jnp.max(in_ref[...].reshape(in_ref.shape[0], WIDTH), axis=0, keepdims=True)
    out_ref[...] = jnp.broadcast_to(a.reshape(1, 1, WIDTH), out_ref.shape)


def relay(tiles, count):
    return pl.pallas_call(
        relay_kernel,
        out_shape=jax.ShapeDtypeStruct((count, 1, WIDTH), jnp.float32),
        in_specs=[in_vmem()],
        out_specs=in_vmem(),
        compiler_params=params(1),
        name="relay",
    )(tiles)


def finish_kernel(peaks_ref, core_ref, rim_ref, out_ref, block, sems):
    peak = jnp.sqrt(jnp.max(peaks_ref[...].reshape(peaks_ref.shape[0], WIDTH), axis=0, keepdims=True))
    scale = jnp.broadcast_to(step_length / (peak + peak_eps), (SIDE, WIDTH))
    z = lax.broadcasted_iota(jnp.int32, (SIDE, WIDTH), 0)
    at_rim = (z < RIM) | (z >= SIDE - RIM)
    copies = []
    for c in range(3):
        for part in range(SIDE // STEP_X):
            for x in range(part * STEP_X, (part + 1) * STEP_X):
                rows = pl.ds((c * SIDE + x) * SIDE, SIDE)
                block[c, x] = jnp.where(at_rim, rim_ref[rows, :], core_ref[rows, :]) * scale
            at = pl.ds(part * STEP_X, STEP_X)
            copies.append(pltpu.make_async_copy(block.at[c, at], out_ref.at[c, at], sems.at[len(copies)]))
            copies[-1].start()
    for copy in copies:
        copy.wait()


def finish(peaks, core, rims):
    return pl.pallas_call(
        finish_kernel,
        out_shape=jax.ShapeDtypeStruct((3, SIDE, SIDE, WIDTH), jnp.float32),
        in_specs=[in_vmem()] * 3,
        out_specs=in_place(),
        scratch_shapes=[
            pltpu.VMEM((3, SIDE, SIDE, WIDTH), jnp.float32),
            pltpu.SemaphoreType.DMA((3 * SIDE // STEP_X,)),
        ],
        compiler_params=params(12),
        name="finish",
    )(peaks, core, rims)


def per_device(fixed_image, moving_image, fetch_owner, fetch_block, fetch_count, interp_level, block_mask):
    side, width = SIDE, WIDTH
    sent = pack(fetch_owner, fetch_block, fetch_count, interp_level.transpose(0, 1, 3, 2, 4), moving_image)
    got = lax.all_to_all(sent, "blk", split_axis=0, concat_axis=0, tiled=True)

    mask_row = jnp.repeat(block_mask.reshape(BLOCKS), side).astype(jnp.bfloat16)[None]
    last = jnp.concatenate([fixed_image[side - RIM :].reshape(-1, width), mask_row], axis=0)
    first = jnp.concatenate([fixed_image[:RIM].reshape(-1, width), mask_row], axis=0)
    left = lax.ppermute(last, "blk", shift_up("blk"))
    right = lax.ppermute(first, "blk", shift_down("blk"))
    turn = lambda a: a[:-1].reshape(RIM, side, width)
    fixed = jnp.concatenate(
        [fixed_image, turn(right), jnp.zeros((ROW - EXT, side, width), jnp.bfloat16), turn(left)], axis=0
    ).transpose(1, 0, 2)
    masks = jnp.concatenate([mask_row, right[-1:], left[-1:], jnp.zeros((5, width), jnp.bfloat16)], axis=0)
    mean, away, gain = fixed_part(fixed.reshape(side * ROW, width), masks)

    half = (lax.axis_index("blk") % 2).astype(jnp.int32).reshape(1)
    warped = lax.all_to_all(hold(half, got), "blk", split_axis=0, concat_axis=0, tiled=True)

    def z_rows(pairs):
        part = warped.reshape(side // DEEP, 2, DEEP, PART, width)[pairs]
        rows = [part[:, 0, :, :HALF], part[:, 1, :, :HALF], part[:, 0, :, HALF:], part[:, 1, :, HALF:]]
        return jnp.concatenate(rows, axis=2).reshape(-1, ROW, width)

    def message(moving_rows, fixed_rows):
        return jnp.concatenate([moving_rows.reshape(-1, width), fixed_rows.reshape(-1, width), masks], axis=0)

    tail = message(z_rows(slice(side // DEEP - 3, None))[1:], fixed[side - RIM :])
    head = message(z_rows(slice(0, 3))[:RIM], fixed[:RIM])
    below = lax.ppermute(tail, "slab", shift_up("slab"))
    above = lax.ppermute(head, "slab", shift_down("slab"))
    core, edge, top = inner(warped.reshape(side * ROW, width), fixed.reshape(side * ROW, width), mean, away, gain)
    rims, peak = rim(below, above, head, tail, masks, edge, top)
    peak = lax.all_to_all(peak, "blk", split_axis=0, concat_axis=0, tiled=True)
    peak = relay(peak, lax.axis_size("slab"))
    peak = lax.all_to_all(peak, "slab", split_axis=0, concat_axis=0, tiled=True)
    return finish(peak, core, rims)


def solution(mesh):
    in_specs = (
        P("blk", "slab", None),
        P("blk", "slab", None),
        P("blk", "slab", None, None),
        P("blk", "slab", None, None),
        P("blk", "slab", None),
        P("blk", "slab", None, None, None),
        P("blk", "slab", None),
    )
    return jax.shard_map(
        per_device, mesh=mesh, in_specs=in_specs, out_specs=P(None, "blk", "slab", None), check_vma=False
    )
```

```python
import math

import jax
import jax.numpy as jnp
from jax import lax
from jax.experimental import pallas as pl
from jax.experimental.pallas import tpu as pltpu
from jax.sharding import Mesh, PartitionSpec as P

LEVELS = 8
BOX_RADIUS = 2
SMOOTH_RADIUS = 3
RIM = BOX_RADIUS + SMOOTH_RADIUS

sigma_smooth = 1.5
step_length = 2.0
var_eps = 1e-05
peak_eps = 1e-06


def smooth_weights(radius):
    raw = [math.exp(-(t * t) / (2.0 * sigma_smooth * sigma_smooth)) for t in range(-radius, radius + 1)]
    total = sum(raw)
    return [one / total for one in raw]


def shift_up(axis):
    n = lax.axis_size(axis)
    return [(i, i + 1) for i in range(n - 1)]


def shift_down(axis):
    n = lax.axis_size(axis)
    return [(i + 1, i) for i in range(n - 1)]


SIDE = 32
WIDTH = 128
BLOCKS = WIDTH // SIDE
SLOTS = 4
OWNERS = 32
DEEP = 2
HALF = SIDE // 2
TAKEN = DEEP + 1
SENT = TAKEN * HALF + TAKEN + 1
PITCH = 56
EXT = SIDE + 2 * RIM
OUT_PITCH = 48
PART = OUT_PITCH // DEEP
MID = SIDE + 2 * SMOOTH_RADIUS
INNER = SIDE - 2 * BOX_RADIUS
CORE = INNER - 2 * SMOOTH_RADIUS
ROW = OUT_PITCH
THIN = 40
MIB = 1 << 20
STEP_X = 8


def params(mib):
    return pltpu.CompilerParams(vmem_limit_bytes=mib * MIB)


def cost(flops, nbytes):
    return pl.CostEstimate(flops=flops, bytes_accessed=nbytes, transcendentals=0)


def in_vmem():
    return pl.BlockSpec(memory_space=pltpu.VMEM)


def in_place():
    return pl.BlockSpec(memory_space=pl.ANY)


def in_smem():
    return pl.BlockSpec(memory_space=pltpu.SMEM)


def pack_kernel(owner_ref, block_ref, count_ref, level_ref, moving_ref, out_ref, wide, block, sems):
    lane = lax.broadcasted_iota(jnp.int32, (TAKEN + 1, WIDTH), 1)
    row = jnp.zeros((TAKEN + 1, WIDTH), jnp.int32)
    e = BLOCKS * SLOTS
    for g in range(BLOCKS):
        count = count_ref[0, 0, g]
        row = jnp.where(lane == 4 * e + g, count, row)
        for k in range(SLOTS):
            name = block_ref[0, 0, g, k] * OWNERS + owner_ref[0, 0, g, k]
            row = jnp.where(lane == g * SLOTS + k, jnp.where(k < count, name, -1), row)
            for axis in range(3):
                at = e + (g * 3 + axis) * SLOTS + k
                row = jnp.where(lane == at, level_ref[0, 0, axis, g, k], row)
    row = row.astype(jnp.float32)
    for x in range(SIDE):
        wide[pl.ds(x * SIDE, SIDE), :] = moving_ref[x].astype(jnp.float32)
    place = lax.broadcasted_iota(jnp.int32, (TAKEN + 1, WIDTH), 0)
    copies = []
    for pair in range(SIDE // DEEP):
        for at in range(TAKEN):
            z = min(pair * DEEP + at, SIDE - 1)
            plane = wide[pl.ds(z, SIDE, stride=SIDE), :].astype(jnp.bfloat16)
            for half in range(2):
                block[pair * 2 + half, at * HALF : (at + 1) * HALF, :] = plane[half * HALF : (half + 1) * HALF]
        for half in range(2):
            x = min((half + 1) * HALF, SIDE - 1)
            if pair < SIDE // DEEP - 1:
                extra = wide[pl.ds(x * SIDE + pair * DEEP, TAKEN + 1), :]
            else:
                two = wide[pl.ds(x * SIDE + pair * DEEP, DEEP), :]
                extra = jnp.concatenate([two, two[1:2], two[1:2]], axis=0)
            extra = jnp.where(place == TAKEN, row, extra)
            block[pair * 2 + half, TAKEN * HALF : SENT, :] = extra.astype(jnp.bfloat16)
        if pair % 4 == 3:
            at = pl.ds((pair - 3) * 2, 8)
            copies.append(pltpu.make_async_copy(block.at[at], out_ref.at[at], sems.at[len(copies)]))
            copies[-1].start()
    for copy in copies:
        copy.wait()


def pack(owner, block, count, level, moving):
    return pl.pallas_call(
        pack_kernel,
        out_shape=jax.ShapeDtypeStruct((OWNERS, SENT, WIDTH), jnp.bfloat16),
        in_specs=[in_smem()] * 4 + [in_vmem()],
        out_specs=in_place(),
        scratch_shapes=[
            pltpu.VMEM((SIDE * SIDE, WIDTH), jnp.float32),
            pltpu.VMEM((OWNERS, SENT, WIDTH), jnp.bfloat16),
            pltpu.SemaphoreType.DMA((4,)),
        ],
        name="pack",
    )(owner, block, count, level, moving)


def exchange_groups(parts, lane):
    parts = list(parts)
    low = lane < 2 * SIDE
    for a in range(2):
        p, q = parts[a], parts[a + 2]
        r = pltpu.roll(jnp.where(low, q, p), 2 * SIDE, 1)
        parts[a], parts[a + 2] = jnp.where(low, p, r), jnp.where(low, r, q)
    even = (lane // SIDE) % 2 == 0
    for a in (0, 2):
        p, q = parts[a], parts[a + 1]
        parts[a] = jnp.where(even, p, pltpu.roll(q, SIDE, 1))
        parts[a + 1] = jnp.where(even, pltpu.roll(p, WIDTH - SIDE, 1), q)
    return parts


def column(a, i):
    return jnp.broadcast_to(a[:, i : i + 1], a.shape)


def hold_kernel(half_ref, got_ref, out_ref, wide, source, coef, mixed, spread, block, sems):
    strip = HALF // BLOCKS
    rows = OWNERS * BLOCKS
    lane = lax.broadcasted_iota(jnp.int32, (OWNERS, WIDTH), 1)
    last_y = lane % SIDE == SIDE - 1
    for o in range(OWNERS):
        wide[pl.ds(o * PITCH, SENT), :] = got_ref[o].astype(jnp.float32)

    lists = wide[pl.ds(SENT - 1, OWNERS, stride=PITCH), :]
    where_k = lane.astype(jnp.float32)
    e = BLOCKS * SLOTS
    top = float(LEVELS)
    scales = []
    for g in range(BLOCKS):
        total = {}
        for k in range(SLOTS):
            at = g * SLOTS + k
            name = column(lists, at)
            base = e + g * 3 * SLOTS + k
            lx, lz, ly = (column(lists, base + a * SLOTS) for a in range(3))
            x1 = jnp.where(where_k == name, lx, 0.0)
            x0 = jnp.where(where_k == name, top - lx, 0.0)
            for dx in range(2):
                ax = x1 if dx else x0
                z1 = ax * lz
                for dz in range(2):
                    az = z1 if dz else top * ax - z1
                    y1 = az * ly
                    for dy in range(2):
                        ay = y1 if dy else top * az - y1
                        key = (dx, dz, dy)
                        total[key] = ay if k == 0 else total[key] + ay
        for (dx, dz, dy), c in total.items():
            hi = jnp.floor(c * (1.0 / 16.0)) * 16.0
            col = pl.ds(dy * WIDTH, WIDTH)
            coef[dz * 2 + dx, pl.ds(g * OWNERS, OWNERS), col] = hi.astype(jnp.bfloat16)
            coef[dz * 2 + dx, pl.ds(rows + g * OWNERS, OWNERS), col] = (c - hi).astype(jnp.bfloat16)
        scales.append((1.0 / column(lists, 4 * e + g)) * (1.0 / LEVELS**3))

    wrap = strip + 1
    for z in range(TAKEN):
        for t in range(wrap):
            at = [strip * q + t for q in range(BLOCKS)]
            parts = [
                wide[pl.ds(z * HALF + x if x < HALF else TAKEN * HALF + z, OWNERS, stride=PITCH), :] for x in at
            ]
            for g, u in enumerate(exchange_groups(parts, lane)):
                v = jnp.where(last_y, u, pltpu.roll(u, WIDTH - 1, 1))
                for dy, a in enumerate((u, v)):
                    source[pl.ds(dy * rows + g * OWNERS, OWNERS), pl.ds((z * wrap + t) * WIDTH, WIDTH)] = a.astype(
                        jnp.bfloat16
                    )

    piece = 2 * WIDTH
    for z in range(DEEP):
        for t in range(0, strip, 2):
            acc = None
            for dz in range(2):
                for dx in range(2):
                    col = ((z + dz) * wrap + t + dx) * WIDTH
                    one = jnp.dot(
                        coef[dz * 2 + dx], source[:, pl.ds(col, piece)], preferred_element_type=jnp.float32
                    )
                    acc = one if acc is None else acc + one
            for g in range(BLOCKS):
                lo = rows + g * OWNERS
                part = acc[g * OWNERS : (g + 1) * OWNERS] + acc[lo : lo + OWNERS]
                for i in range(2):
                    mixed[pl.ds(g * OWNERS, OWNERS), pl.ds((z * strip + t + i) * WIDTH, WIDTH)] = (
                        part[:, i * WIDTH : (i + 1) * WIDTH] * scales[g]
                    )

    for r in range(OWNERS):
        for z in range(DEEP):
            spread[pl.ds((r + 1) * OUT_PITCH + z * PART + HALF, PART - HALF), :] = jnp.zeros(
                (PART - HALF, WIDTH), jnp.float32
            )
    for z in range(DEEP):
        for t in range(strip):
            parts = [
                mixed[pl.ds(g * OWNERS, OWNERS), pl.ds((z * strip + t) * WIDTH, WIDTH)] for g in range(BLOCKS)
            ]
            for q, w in enumerate(exchange_groups(parts, lane)):
                spread[pl.ds(OUT_PITCH + z * PART + strip * q + t, OWNERS, stride=OUT_PITCH), :] = w
    half = half_ref[0]

    @pl.when(half == 0)
    def _():
        for z in range(DEEP):
            for k in range(RIM):
                w = spread[pl.ds(OUT_PITCH + z * PART + k, OWNERS, stride=OUT_PITCH), :]
                spread[pl.ds(z * PART + HALF + k, OWNERS, stride=OUT_PITCH), :] = w

    @pl.when(half == 1)
    def _():
        for z in range(DEEP):
            for k in range(RIM):
                w = spread[pl.ds(OUT_PITCH + z * PART + HALF - RIM + k, OWNERS, stride=OUT_PITCH), :]
                spread[pl.ds(2 * OUT_PITCH + z * PART + PART - RIM + k, OWNERS, stride=OUT_PITCH), :] = w

    copies = []
    for r in range(OWNERS):
        block[r] = spread[pl.ds((r + 1) * OUT_PITCH, OUT_PITCH), :].astype(jnp.bfloat16)
        if r % STEP_X == STEP_X - 1:
            at = pl.ds(r + 1 - STEP_X, STEP_X)
            copies.append(pltpu.make_async_copy(block.at[at], out_ref.at[at], sems.at[len(copies)]))
            copies[-1].start()
    for copy in copies:
        copy.wait()


def hold(half, got):
    strip = HALF // BLOCKS
    rows = OWNERS * BLOCKS
    return pl.pallas_call(
        hold_kernel,
        out_shape=jax.ShapeDtypeStruct((OWNERS, OUT_PITCH, WIDTH), jnp.bfloat16),
        in_specs=[in_smem(), in_vmem()],
        out_specs=in_place(),
        scratch_shapes=[
            pltpu.VMEM((OWNERS * PITCH, WIDTH), jnp.float32),
            pltpu.VMEM((2 * rows, TAKEN * (strip + 1) * WIDTH), jnp.bfloat16),
            pltpu.VMEM((4, 2 * rows, 2 * rows), jnp.bfloat16),
            pltpu.VMEM((rows, DEEP * strip * WIDTH), jnp.float32),
            pltpu.VMEM(((OWNERS + 2) * OUT_PITCH, WIDTH), jnp.float32),
            pltpu.VMEM((OWNERS, OUT_PITCH, WIDTH), jnp.bfloat16),
            pltpu.SemaphoreType.DMA((OWNERS // STEP_X,)),
        ],
        compiler_params=params(12),
        name="hold",
    )(half, got)


def distance():
    i = lax.broadcasted_iota(jnp.int32, (WIDTH, WIDTH), 0)
    j = lax.broadcasted_iota(jnp.int32, (WIDTH, WIDTH), 1)
    return jnp.abs(i - j)


def box_band():
    one = jnp.where(distance() <= BOX_RADIUS, 1.0, 0.0).astype(jnp.bfloat16)
    return one, jnp.concatenate([one, one], axis=0)


def smooth_band():
    d = distance()
    taps = smooth_weights(SMOOTH_RADIUS)
    left = jnp.zeros((WIDTH, WIDTH), jnp.float32)
    for t in range(SMOOTH_RADIUS + 1):
        left = jnp.where(d == t, taps[SMOOTH_RADIUS + t], left)
    parts = []
    for _ in range(2):
        part = left.astype(jnp.bfloat16)
        parts.append(part)
        left = left - part.astype(jnp.float32)
    return jnp.concatenate(parts, axis=0)


def times(a, band):
    return jnp.dot(a, band, preferred_element_type=jnp.float32)


def halves(product):
    hi = product.astype(jnp.bfloat16)
    return jnp.concatenate([hi, (product - hi.astype(jnp.float32)).astype(jnp.bfloat16)], axis=1)


def rows_at(i):
    if isinstance(i, int):
        return pl.ds(i * ROW, ROW)
    return pl.ds(pl.multiple_of(i * ROW, ROW), ROW)


def thin_at(i):
    if isinstance(i, int):
        return pl.ds(i * THIN, THIN)
    return pl.ds(pl.multiple_of(i * THIN, 8), THIN)


def along(a, step):
    return pltpu.roll(a, (-step) % a.shape[0], 0)


def thin(a):
    x = lax.broadcasted_iota(jnp.int32, (8, WIDTH), 0)
    return jnp.concatenate([a[:SIDE], jnp.where(x < 4, a[SIDE:THIN], a[THIN:])], axis=0)


def box_x(a):
    two = a + along(a, -1)
    return thin((along(two, -1) + a) + along(two, 2)) * (1.0 / (2 * BOX_RADIUS + 1) ** 3)


def box_zx(ref, which, i, count):
    r = [ref[which, rows_at(i + t), :] for t in range(2 * BOX_RADIUS + count)]
    if count == 1:
        return [box_x(((r[0] + r[1]) + (r[2] + r[3])) + r[4])]
    mid = (r[1] + r[2]) + (r[3] + r[4])
    return [box_x(r[0] + mid), box_x(mid + r[5])]


def mask_rows(ref):
    x = lax.broadcasted_iota(jnp.int32, (THIN, WIDTH), 0)
    m = ref[...].astype(jnp.float32)
    right = jnp.where(x < SIDE + SMOOTH_RADIUS, m[1:2], 0.0)
    return jnp.where(x < SIDE, m[0:1], jnp.where(x >= THIN - SMOOTH_RADIUS, m[2:3], right))


def fixed_sums(f, sums, q, rows, bands):
    sums[q, rows, :] = times(f, bands[0])
    wide = f.astype(jnp.float32)
    sums[q + 1, rows, :] = times(halves(wide * wide), bands[1])


def fixed_rows(sums, q, i, here, mask):
    means = box_zx(sums, q, i, len(here))
    squares = box_zx(sums, q + 1, i, len(here))
    out = []
    for h, m, p, sq in zip(here, mask, means, squares):
        out.append((p, h - p, m / (sq - p * p + var_eps)))
    return out


def fixed_kernel(fixed_ref, mask_ref, mean_ref, away_ref, gain_ref, sums):
    bands = box_band()
    chunk = 8 * ROW

    def by_y(i, carry):
        rows = pl.ds(pl.multiple_of(i * chunk, chunk), chunk)
        fixed_sums(fixed_ref[rows, :], sums, 0, rows, bands)
        return carry

    lax.fori_loop(0, SIDE // 8, by_y, 0)
    mask = mask_rows(mask_ref)

    def by_z(step, carry):
        i = 2 * step
        here = [thin(fixed_ref[rows_at(i + BOX_RADIUS + t), :].astype(jnp.float32)) for t in range(2)]
        for t, (mean, away, gain) in enumerate(fixed_rows(sums, 0, i, here, [mask, mask])):
            mean_ref[thin_at(i + t), :] = mean
            away_ref[thin_at(i + t), :] = away
            gain_ref[thin_at(i + t), :] = gain
        return carry

    lax.fori_loop(0, INNER // 2, by_z, 0)


def fixed_part(fixed, mask):
    out = jax.ShapeDtypeStruct((INNER * THIN, WIDTH), jnp.float32)
    return pl.pallas_call(
        fixed_kernel,
        out_shape=[out] * 3,
        in_specs=[in_vmem()] * 2,
        out_specs=[in_vmem()] * 3,
        scratch_shapes=[pltpu.VMEM((2, SIDE * ROW, WIDTH), jnp.float32)],
        compiler_params=params(8),
        cost_estimate=cost(5_000_000_000, 4_000_000),
        name="fixed_part",
    )(fixed, mask)


def sums_by_y(f, wide, sums, rows, bands, with_fixed):
    mw = wide[rows, :]
    fw = f.astype(jnp.float32)
    n = mw.shape[0]
    plain = [mw.astype(jnp.bfloat16)] + ([f] if with_fixed else [])
    pairs = [mw * mw, mw * fw] + ([fw * fw] if with_fixed else [])
    one = times(jnp.concatenate(plain, axis=0), bands[0])
    two = times(jnp.concatenate([halves(p) for p in pairs], axis=0), bands[1])
    sums[0, rows, :] = one[:n]
    sums[1, rows, :] = two[:n]
    sums[2, rows, :] = two[n : 2 * n]
    if with_fixed:
        sums[3, rows, :] = one[n:]
        sums[4, rows, :] = two[2 * n :]


def force_rows(wide, sums, i, fixed, force, k, pitch):
    count = len(fixed)
    means = box_zx(sums, 0, i, count)
    squares = box_zx(sums, 1, i, count)
    products = box_zx(sums, 2, i, count)
    lane = lax.broadcasted_iota(jnp.int32, (THIN, WIDTH), 1)
    at = [thin(wide[rows_at(i + BOX_RADIUS - 1 + t), :]) for t in range(count + 2)]
    for t, (mean_f, away, gain) in enumerate(fixed):
        mean = means[t]
        q = (products[t] - mean_f * mean) / (squares[t] - mean * mean + var_eps)
        m = at[t + 1]
        term = gain * q * (away - q * (m - mean))
        up = jnp.where(lane == WIDTH - 1, 0.0, pltpu.roll(m, WIDTH - 1, 1))
        down = jnp.where(lane == 0, 0.0, pltpu.roll(m, 1, 1))
        steps = (along(m, 1) - along(m, -1), at[t + 2] - at[t], up - down)
        for c in range(3):
            force[thin_at(c * pitch + k + t), :] = term * steps[c]


def smooth_rows(smooth_y, pitch, i, out_ref, z, count, peak):
    taps = smooth_weights(SMOOTH_RADIUS)[SMOOTH_RADIUS:]
    mid = SMOOTH_RADIUS
    total = [None] * count
    for c in range(3):
        g = [smooth_y[thin_at(c * pitch + i + t), :] for t in range(2 * SMOOTH_RADIUS + count)]
        for n in range(count):
            s = taps[0] * g[n + mid]
            for t in range(1, SMOOTH_RADIUS + 1):
                s += taps[t] * (g[n + mid - t] + g[n + mid + t])
            a = taps[0] * s
            for t in range(1, SMOOTH_RADIUS + 1):
                a += taps[t] * (along(s, -t) + along(s, t))
            a = a[:SIDE]
            out_ref[pl.ds(c * SIDE * SIDE + z + n, SIDE, stride=SIDE), :] = a
            total[n] = a * a if c == 0 else total[n] + a * a
    for one in total:
        peak = jnp.maximum(peak, one)
    return peak


def smooth_along_y(force, i, pitch, count, out, j, out_pitch, double):
    f = [force[pl.ds((c * pitch + i) * THIN, count * THIN), :].astype(jnp.bfloat16) for c in range(3)]
    f = jnp.concatenate(f, axis=0)
    g = times(jnp.concatenate([f, f], axis=1), double)
    for c in range(3):
        out[pl.ds((c * out_pitch + j) * THIN, count * THIN), :] = g[c * count * THIN : (c + 1) * count * THIN]


def inner_kernel(warped_ref, fixed_ref, mean_ref, away_ref, gain_ref, out_ref, edge_ref, peak_ref, wide, sums, force, smooth_y):
    bands = box_band()
    double = smooth_band()
    step = 4

    def by_y(n):
        for pair in range(n * step // DEEP, (n + 1) * step // DEEP):
            for half in range(2):
                for z in range(DEEP):
                    src = (pair * 2 + half) * OUT_PITCH + z * PART
                    dst = (pair * DEEP + z) * ROW
                    own = warped_ref[pl.ds(src, HALF), :]
                    wide[pl.ds(dst + half * HALF, HALF), :] = own.astype(jnp.float32)
                    side = warped_ref[pl.ds(src + HALF, 8), :]
                    wide[pl.ds(dst + SIDE + 8 * half, 8), :] = side.astype(jnp.float32)
        rows = pl.ds(n * step * ROW, step * ROW)
        sums_by_y(fixed_ref[rows, :], wide, sums, rows, bands, False)

    by_y(0)
    peak = jnp.zeros((SIDE, WIDTH), jnp.float32)
    done = 0
    for n in range(INNER // step):
        by_y(n + 1)
        for i in range(n * step, (n + 1) * step, 2):
            fixed = [
                (mean_ref[thin_at(i + t), :], away_ref[thin_at(i + t), :], gain_ref[thin_at(i + t), :])
                for t in range(2)
            ]
            force_rows(wide, sums, i, fixed, force, i, INNER)
        smooth_along_y(force, n * step, INNER, step, smooth_y, n * step, INNER, double)
        while done + 1 + 2 * SMOOTH_RADIUS < (n + 1) * step:
            peak = smooth_rows(smooth_y, INNER, done, out_ref, done + RIM, 2, peak)
            done += 2
    kept = 2 * SMOOTH_RADIUS * THIN
    for c in range(3):
        at = c * INNER * THIN
        edge_ref[c, 0:kept, :] = smooth_y[at : at + kept, :]
        edge_ref[c, kept : 2 * kept, :] = smooth_y[at + INNER * THIN - kept : at + INNER * THIN, :]
    peak_ref[...] = peak


def rim_kernel(
    below_ref, above_ref, head_ref, tail_ref, mask_ref, edge_ref, first_ref,
    out_ref, peak_ref, wide, fwide, sums, force, smooth_y,
):
    bands = box_band()
    double = smooth_band()
    own = RIM - 1
    stack = RIM + own
    for ref, start, count, at in (
        (below_ref, 0, RIM, 0),
        (head_ref, 0, own, RIM),
        (tail_ref, RIM - own, own, stack),
        (above_ref, 0, RIM, stack + own),
    ):
        rows = pl.ds(at * ROW, count * ROW)
        wide[rows, :] = ref[pl.ds(start * ROW, count * ROW), :].astype(jnp.float32)
        fwide[rows, :] = ref[pl.ds((RIM + start) * ROW, count * ROW), :].astype(jnp.float32)
    last = pl.ds(2 * RIM * ROW, 8)
    masks = [mask_rows(below_ref.at[last, :]), mask_rows(mask_ref), mask_rows(above_ref.at[last, :])]
    kept = 2 * SMOOTH_RADIUS
    tall = RIM + kept
    for side in range(2):
        for c in range(3):
            old = c * 2 * tall + side * tall + (0 if side else RIM)
            smooth_y[pl.ds(old * THIN, kept * THIN), :] = edge_ref[c, pl.ds(side * kept * THIN, kept * THIN), :]
        for n in range(stack // 3):
            rows = pl.ds((side * stack + 3 * n) * ROW, 3 * ROW)
            sums_by_y(fwide[rows, :].astype(jnp.bfloat16), wide, sums, rows, bands, True)
    for i, count in ((0, 2), (2, 1), (3, 2)):
        for side in range(2):
            first = stack * side + i
            mask = []
            for t in range(i, i + count):
                outer = t < SMOOTH_RADIUS if side == 0 else t >= RIM - SMOOTH_RADIUS
                mask.append(masks[2 * side] if outer else masks[1])
            here = [thin(fwide[rows_at(first + BOX_RADIUS + t), :]) for t in range(count)]
            fixed = fixed_rows(sums, 3, first, here, mask)
            force_rows(wide, sums, first, fixed, force, i + RIM * side, 2 * RIM)
    peak = first_ref[...]
    for side in range(2):
        new = side * tall + (kept if side else 0)
        smooth_along_y(force, side * RIM, 2 * RIM, RIM, smooth_y, new, 2 * tall, double)
    for i, count in ((0, 2), (2, 2), (4, 1)):
        for side in range(2):
            peak = smooth_rows(smooth_y, 2 * tall, tall * side + i, out_ref, (SIDE - RIM) * side + i, count, peak)
    top = jnp.max(jnp.max(peak, axis=0, keepdims=True), axis=1, keepdims=True)
    peak_ref[...] = jnp.broadcast_to(top.reshape(1, 1, 1), peak_ref.shape)


def inner(warped, fixed, mean, away, gain):
    return pl.pallas_call(
        inner_kernel,
        out_shape=[
            jax.ShapeDtypeStruct((3 * SIDE * SIDE, WIDTH), jnp.float32),
            jax.ShapeDtypeStruct((3, 4 * SMOOTH_RADIUS * THIN, WIDTH), jnp.float32),
            jax.ShapeDtypeStruct((SIDE, WIDTH), jnp.float32),
        ],
        in_specs=[in_vmem()] * 5,
        out_specs=[in_vmem()] * 3,
        scratch_shapes=[
            pltpu.VMEM((SIDE * ROW, WIDTH), jnp.float32),
            pltpu.VMEM((3, SIDE * ROW, WIDTH), jnp.float32),
            pltpu.VMEM((3 * INNER * THIN, WIDTH), jnp.float32),
            pltpu.VMEM((3 * INNER * THIN, WIDTH), jnp.float32),
        ],
        compiler_params=params(14),
        cost_estimate=cost(10_000_000_000, 8_000_000),
        name="inner",
    )(warped, fixed, mean, away, gain)


def rim(below, above, head, tail, mask, edge, first):
    stack = 2 * (2 * RIM - 1) * ROW
    tall = 2 * (RIM + 2 * SMOOTH_RADIUS) * THIN
    return pl.pallas_call(
        rim_kernel,
        out_shape=[
            jax.ShapeDtypeStruct((3 * SIDE * SIDE, WIDTH), jnp.float32),
            jax.ShapeDtypeStruct((16, 1, WIDTH), jnp.float32),
        ],
        in_specs=[in_vmem()] * 7,
        out_specs=[in_vmem()] * 2,
        scratch_shapes=[pltpu.VMEM((stack, WIDTH), jnp.float32)] * 2
        + [pltpu.VMEM((5, stack, WIDTH), jnp.float32)]
        + [
            pltpu.VMEM((3 * 2 * RIM * THIN, WIDTH), jnp.float32),
            pltpu.VMEM((3 * tall, WIDTH), jnp.float32),
        ],
        compiler_params=params(14),
        name="rim",
    )(below, above, head, tail, mask, edge, first)


def relay_kernel(in_ref, out_ref):
    a = jnp.max(in_ref[...].reshape(in_ref.shape[0], WIDTH), axis=0, keepdims=True)
    out_ref[...] = jnp.broadcast_to(a.reshape(1, 1, WIDTH), out_ref.shape)


def relay(tiles, count):
    return pl.pallas_call(
        relay_kernel,
        out_shape=jax.ShapeDtypeStruct((count, 1, WIDTH), jnp.float32),
        in_specs=[in_vmem()],
        out_specs=in_vmem(),
        compiler_params=params(1),
        name="relay",
    )(tiles)


def finish_kernel(peaks_ref, core_ref, rim_ref, out_ref, block, sems):
    peak = jnp.sqrt(jnp.max(peaks_ref[...].reshape(peaks_ref.shape[0], WIDTH), axis=0, keepdims=True))
    scale = jnp.broadcast_to(step_length / (peak + peak_eps), (SIDE, WIDTH))
    z = lax.broadcasted_iota(jnp.int32, (SIDE, WIDTH), 0)
    at_rim = (z < RIM) | (z >= SIDE - RIM)
    copies = []
    for c in range(3):
        for part in range(SIDE // STEP_X):
            for x in range(part * STEP_X, (part + 1) * STEP_X):
                rows = pl.ds((c * SIDE + x) * SIDE, SIDE)
                block[c, x] = jnp.where(at_rim, rim_ref[rows, :], core_ref[rows, :]) * scale
            at = pl.ds(part * STEP_X, STEP_X)
            copies.append(pltpu.make_async_copy(block.at[c, at], out_ref.at[c, at], sems.at[len(copies)]))
            copies[-1].start()
    for copy in copies:
        copy.wait()


def finish(peaks, core, rims):
    return pl.pallas_call(
        finish_kernel,
        out_shape=jax.ShapeDtypeStruct((3, SIDE, SIDE, WIDTH), jnp.float32),
        in_specs=[in_vmem()] * 3,
        out_specs=in_place(),
        scratch_shapes=[
            pltpu.VMEM((3, SIDE, SIDE, WIDTH), jnp.float32),
            pltpu.SemaphoreType.DMA((3 * SIDE // STEP_X,)),
        ],
        compiler_params=params(12),
        name="finish",
    )(peaks, core, rims)


SLAB = ("z", "h")
BLK = ("y", "l", "c")
NEAR = ("y", "l")
FAR = ("z", "h", "c")


def per_device(fixed_image, moving_image, fetch_owner, fetch_block, fetch_count, interp_level, block_mask):
    side, width = SIDE, WIDTH
    sent = pack(fetch_owner, fetch_block, fetch_count, interp_level.transpose(0, 1, 3, 2, 4), moving_image)
    got = lax.all_to_all(sent, BLK, split_axis=0, concat_axis=0, tiled=True)

    mask_row = jnp.repeat(block_mask.reshape(BLOCKS), side).astype(jnp.bfloat16)[None]
    last = jnp.concatenate([fixed_image[side - RIM :].reshape(-1, width), mask_row], axis=0)
    first = jnp.concatenate([fixed_image[:RIM].reshape(-1, width), mask_row], axis=0)
    left = lax.ppermute(last, BLK, shift_up(BLK))
    right = lax.ppermute(first, BLK, shift_down(BLK))
    turn = lambda a: a[:-1].reshape(RIM, side, width)
    fixed = jnp.concatenate(
        [fixed_image, turn(right), jnp.zeros((ROW - EXT, side, width), jnp.bfloat16), turn(left)], axis=0
    ).transpose(1, 0, 2)
    masks = jnp.concatenate([mask_row, right[-1:], left[-1:], jnp.zeros((5, width), jnp.bfloat16)], axis=0)
    mean, away, gain = fixed_part(fixed.reshape(side * ROW, width), masks)

    half = (lax.axis_index(BLK) % 2).astype(jnp.int32).reshape(1)
    warped = lax.all_to_all(hold(half, got), BLK, split_axis=0, concat_axis=0, tiled=True)

    def z_rows(pairs):
        part = warped.reshape(side // DEEP, 2, DEEP, PART, width)[pairs]
        rows = [part[:, 0, :, :HALF], part[:, 1, :, :HALF], part[:, 0, :, HALF:], part[:, 1, :, HALF:]]
        return jnp.concatenate(rows, axis=2).reshape(-1, ROW, width)

    def message(moving_rows, fixed_rows):
        return jnp.concatenate([moving_rows.reshape(-1, width), fixed_rows.reshape(-1, width), masks], axis=0)

    tail = message(z_rows(slice(side // DEEP - 3, None))[1:], fixed[side - RIM :])
    head = message(z_rows(slice(0, 3))[:RIM], fixed[:RIM])
    below = lax.ppermute(tail, SLAB, shift_up(SLAB))
    above = lax.ppermute(head, SLAB, shift_down(SLAB))
    core, edge, top = inner(warped.reshape(side * ROW, width), fixed.reshape(side * ROW, width), mean, away, gain)
    rims, peak = rim(below, above, head, tail, masks, edge, top)
    peak = lax.all_to_all(peak, NEAR, split_axis=0, concat_axis=0, tiled=True)
    peak = relay(peak, 32)
    peak = lax.all_to_all(peak, FAR, split_axis=0, concat_axis=0, tiled=True)
    return finish(peak, core, rims)


def solution(mesh):
    fine = Mesh(mesh.devices.reshape(8, 2, 8, 2, 2), SLAB + BLK)
    in_specs = (
        P(BLK, SLAB, None),
        P(BLK, SLAB, None),
        P(BLK, SLAB, None, None),
        P(BLK, SLAB, None, None),
        P(BLK, SLAB, None),
        P(BLK, SLAB, None, None, None),
        P(BLK, SLAB, None),
    )
    return jax.shard_map(
        per_device, mesh=fine, in_specs=in_specs, out_specs=P(None, BLK, SLAB, None), check_vma=False
    )
```

```python
import math

import jax
import jax.numpy as jnp
from jax import lax
from jax.experimental import pallas as pl
from jax.experimental.pallas import tpu as pltpu
from jax.sharding import PartitionSpec as P

LEVELS = 8
BOX_RADIUS = 2
SMOOTH_RADIUS = 3
RIM = BOX_RADIUS + SMOOTH_RADIUS

sigma_smooth = 1.5
step_length = 2.0
var_eps = 1e-05
peak_eps = 1e-06


def smooth_weights(radius):
    raw = [math.exp(-(t * t) / (2.0 * sigma_smooth * sigma_smooth)) for t in range(-radius, radius + 1)]
    total = sum(raw)
    return [one / total for one in raw]


def shift_up(axis):
    n = lax.axis_size(axis)
    return [(i, i + 1) for i in range(n - 1)]


def shift_down(axis):
    n = lax.axis_size(axis)
    return [(i + 1, i) for i in range(n - 1)]


SIDE = 32
WIDTH = 128
BLOCKS = WIDTH // SIDE
SLOTS = 4
OWNERS = 32
DEEP = 2
HALF = SIDE // 2
TAKEN = DEEP + 1
SENT = TAKEN * HALF + TAKEN + 1
PITCH = 56
EXT = SIDE + 2 * RIM
OUT_PITCH = 48
PART = OUT_PITCH // DEEP
MID = SIDE + 2 * SMOOTH_RADIUS
INNER = SIDE - 2 * BOX_RADIUS
CORE = INNER - 2 * SMOOTH_RADIUS
ROW = OUT_PITCH
THIN = 40
MIB = 1 << 20
STEP_X = 8


def params(mib):
    return pltpu.CompilerParams(vmem_limit_bytes=mib * MIB)


def cost(flops, nbytes):
    return pl.CostEstimate(flops=flops, bytes_accessed=nbytes, transcendentals=0)


def in_vmem():
    return pl.BlockSpec(memory_space=pltpu.VMEM)


def in_place():
    return pl.BlockSpec(memory_space=pl.ANY)


def in_smem():
    return pl.BlockSpec(memory_space=pltpu.SMEM)


def pack_kernel(owner_ref, block_ref, count_ref, level_ref, moving_ref, out_ref, wide, block, sems):
    lane = lax.broadcasted_iota(jnp.int32, (TAKEN + 1, WIDTH), 1)
    row = jnp.zeros((TAKEN + 1, WIDTH), jnp.int32)
    e = BLOCKS * SLOTS
    for g in range(BLOCKS):
        count = count_ref[0, 0, g]
        row = jnp.where(lane == 4 * e + g, count, row)
        for k in range(SLOTS):
            name = block_ref[0, 0, g, k] * OWNERS + owner_ref[0, 0, g, k]
            row = jnp.where(lane == g * SLOTS + k, jnp.where(k < count, name, -1), row)
            for axis in range(3):
                at = e + (g * 3 + axis) * SLOTS + k
                row = jnp.where(lane == at, level_ref[0, 0, axis, g, k], row)
    row = row.astype(jnp.float32)
    for x in range(SIDE):
        wide[pl.ds(x * SIDE, SIDE), :] = moving_ref[x].astype(jnp.float32)
    place = lax.broadcasted_iota(jnp.int32, (TAKEN + 1, WIDTH), 0)
    copies = []
    for pair in range(SIDE // DEEP):
        for at in range(TAKEN):
            z = min(pair * DEEP + at, SIDE - 1)
            plane = wide[pl.ds(z, SIDE, stride=SIDE), :].astype(jnp.bfloat16)
            for half in range(2):
                block[pair * 2 + half, at * HALF : (at + 1) * HALF, :] = plane[half * HALF : (half + 1) * HALF]
        for half in range(2):
            x = min((half + 1) * HALF, SIDE - 1)
            if pair < SIDE // DEEP - 1:
                extra = wide[pl.ds(x * SIDE + pair * DEEP, TAKEN + 1), :]
            else:
                two = wide[pl.ds(x * SIDE + pair * DEEP, DEEP), :]
                extra = jnp.concatenate([two, two[1:2], two[1:2]], axis=0)
            extra = jnp.where(place == TAKEN, row, extra)
            block[pair * 2 + half, TAKEN * HALF : SENT, :] = extra.astype(jnp.bfloat16)
        if pair % 4 == 3:
            at = pl.ds((pair - 3) * 2, 8)
            copies.append(pltpu.make_async_copy(block.at[at], out_ref.at[at], sems.at[len(copies)]))
            copies[-1].start()
    for copy in copies:
        copy.wait()


def pack(owner, block, count, level, moving):
    return pl.pallas_call(
        pack_kernel,
        out_shape=jax.ShapeDtypeStruct((OWNERS, SENT, WIDTH), jnp.bfloat16),
        in_specs=[in_smem()] * 4 + [in_vmem()],
        out_specs=in_place(),
        scratch_shapes=[
            pltpu.VMEM((SIDE * SIDE, WIDTH), jnp.float32),
            pltpu.VMEM((OWNERS, SENT, WIDTH), jnp.bfloat16),
            pltpu.SemaphoreType.DMA((4,)),
        ],
        name="pack",
    )(owner, block, count, level, moving)


def exchange_groups(parts, lane):
    parts = list(parts)
    low = lane < 2 * SIDE
    for a in range(2):
        p, q = parts[a], parts[a + 2]
        r = pltpu.roll(jnp.where(low, q, p), 2 * SIDE, 1)
        parts[a], parts[a + 2] = jnp.where(low, p, r), jnp.where(low, r, q)
    even = (lane // SIDE) % 2 == 0
    for a in (0, 2):
        p, q = parts[a], parts[a + 1]
        parts[a] = jnp.where(even, p, pltpu.roll(q, SIDE, 1))
        parts[a + 1] = jnp.where(even, pltpu.roll(p, WIDTH - SIDE, 1), q)
    return parts


def column(a, i):
    return jnp.broadcast_to(a[:, i : i + 1], a.shape)


def hold_kernel(half_ref, got_ref, out_ref, wide, source, coef, mixed, spread, block, sems):
    strip = HALF // BLOCKS
    rows = OWNERS * BLOCKS
    lane = lax.broadcasted_iota(jnp.int32, (OWNERS, WIDTH), 1)
    last_y = lane % SIDE == SIDE - 1
    for o in range(OWNERS):
        wide[pl.ds(o * PITCH, SENT), :] = got_ref[o].astype(jnp.float32)

    lists = wide[pl.ds(SENT - 1, OWNERS, stride=PITCH), :]
    where_k = lane.astype(jnp.float32)
    e = BLOCKS * SLOTS
    top = float(LEVELS)
    scales = []
    for g in range(BLOCKS):
        total = {}
        for k in range(SLOTS):
            at = g * SLOTS + k
            name = column(lists, at)
            base = e + g * 3 * SLOTS + k
            lx, lz, ly = (column(lists, base + a * SLOTS) for a in range(3))
            x1 = jnp.where(where_k == name, lx, 0.0)
            x0 = jnp.where(where_k == name, top - lx, 0.0)
            for dx in range(2):
                ax = x1 if dx else x0
                z1 = ax * lz
                for dz in range(2):
                    az = z1 if dz else top * ax - z1
                    y1 = az * ly
                    for dy in range(2):
                        ay = y1 if dy else top * az - y1
                        key = (dx, dz, dy)
                        total[key] = ay if k == 0 else total[key] + ay
        for (dx, dz, dy), c in total.items():
            hi = jnp.floor(c * (1.0 / 16.0)) * 16.0
            col = pl.ds(dy * WIDTH, WIDTH)
            coef[dz * 2 + dx, pl.ds(g * OWNERS, OWNERS), col] = hi.astype(jnp.bfloat16)
            coef[dz * 2 + dx, pl.ds(rows + g * OWNERS, OWNERS), col] = (c - hi).astype(jnp.bfloat16)
        scales.append((1.0 / column(lists, 4 * e + g)) * (1.0 / LEVELS**3))

    wrap = strip + 1
    for z in range(TAKEN):
        for t in range(wrap):
            at = [strip * q + t for q in range(BLOCKS)]
            parts = [
                wide[pl.ds(z * HALF + x if x < HALF else TAKEN * HALF + z, OWNERS, stride=PITCH), :] for x in at
            ]
            for g, u in enumerate(exchange_groups(parts, lane)):
                v = jnp.where(last_y, u, pltpu.roll(u, WIDTH - 1, 1))
                for dy, a in enumerate((u, v)):
                    source[pl.ds(dy * rows + g * OWNERS, OWNERS), pl.ds((z * wrap + t) * WIDTH, WIDTH)] = a.astype(
                        jnp.bfloat16
                    )

    piece = 2 * WIDTH
    for z in range(DEEP):
        for t in range(0, strip, 2):
            acc = None
            for dz in range(2):
                for dx in range(2):
                    col = ((z + dz) * wrap + t + dx) * WIDTH
                    one = jnp.dot(
                        coef[dz * 2 + dx], source[:, pl.ds(col, piece)], preferred_element_type=jnp.float32
                    )
                    acc = one if acc is None else acc + one
            for g in range(BLOCKS):
                lo = rows + g * OWNERS
                part = acc[g * OWNERS : (g + 1) * OWNERS] + acc[lo : lo + OWNERS]
                for i in range(2):
                    mixed[pl.ds(g * OWNERS, OWNERS), pl.ds((z * strip + t + i) * WIDTH, WIDTH)] = (
                        part[:, i * WIDTH : (i + 1) * WIDTH] * scales[g]
                    )

    for r in range(OWNERS):
        for z in range(DEEP):
            spread[pl.ds((r + 1) * OUT_PITCH + z * PART + HALF, PART - HALF), :] = jnp.zeros(
                (PART - HALF, WIDTH), jnp.float32
            )
    for z in range(DEEP):
        for t in range(strip):
            parts = [
                mixed[pl.ds(g * OWNERS, OWNERS), pl.ds((z * strip + t) * WIDTH, WIDTH)] for g in range(BLOCKS)
            ]
            for q, w in enumerate(exchange_groups(parts, lane)):
                spread[pl.ds(OUT_PITCH + z * PART + strip * q + t, OWNERS, stride=OUT_PITCH), :] = w
    half = half_ref[0]

    @pl.when(half == 0)
    def _():
        for z in range(DEEP):
            for k in range(RIM):
                w = spread[pl.ds(OUT_PITCH + z * PART + k, OWNERS, stride=OUT_PITCH), :]
                spread[pl.ds(z * PART + HALF + k, OWNERS, stride=OUT_PITCH), :] = w

    @pl.when(half == 1)
    def _():
        for z in range(DEEP):
            for k in range(RIM):
                w = spread[pl.ds(OUT_PITCH + z * PART + HALF - RIM + k, OWNERS, stride=OUT_PITCH), :]
                spread[pl.ds(2 * OUT_PITCH + z * PART + PART - RIM + k, OWNERS, stride=OUT_PITCH), :] = w

    copies = []
    for r in range(OWNERS):
        block[r] = spread[pl.ds((r + 1) * OUT_PITCH, OUT_PITCH), :].astype(jnp.bfloat16)
        if r % STEP_X == STEP_X - 1:
            at = pl.ds(r + 1 - STEP_X, STEP_X)
            copies.append(pltpu.make_async_copy(block.at[at], out_ref.at[at], sems.at[len(copies)]))
            copies[-1].start()
    for copy in copies:
        copy.wait()


def hold(half, got):
    strip = HALF // BLOCKS
    rows = OWNERS * BLOCKS
    return pl.pallas_call(
        hold_kernel,
        out_shape=jax.ShapeDtypeStruct((OWNERS, OUT_PITCH, WIDTH), jnp.bfloat16),
        in_specs=[in_smem(), in_vmem()],
        out_specs=in_place(),
        scratch_shapes=[
            pltpu.VMEM((OWNERS * PITCH, WIDTH), jnp.float32),
            pltpu.VMEM((2 * rows, TAKEN * (strip + 1) * WIDTH), jnp.bfloat16),
            pltpu.VMEM((4, 2 * rows, 2 * rows), jnp.bfloat16),
            pltpu.VMEM((rows, DEEP * strip * WIDTH), jnp.float32),
            pltpu.VMEM(((OWNERS + 2) * OUT_PITCH, WIDTH), jnp.float32),
            pltpu.VMEM((OWNERS, OUT_PITCH, WIDTH), jnp.bfloat16),
            pltpu.SemaphoreType.DMA((OWNERS // STEP_X,)),
        ],
        compiler_params=params(12),
        name="hold",
    )(half, got)


def distance():
    i = lax.broadcasted_iota(jnp.int32, (WIDTH, WIDTH), 0)
    j = lax.broadcasted_iota(jnp.int32, (WIDTH, WIDTH), 1)
    return jnp.abs(i - j)


def box_band():
    one = jnp.where(distance() <= BOX_RADIUS, 1.0, 0.0).astype(jnp.bfloat16)
    return one, jnp.concatenate([one, one], axis=0)


def smooth_band():
    d = distance()
    taps = smooth_weights(SMOOTH_RADIUS)
    left = jnp.zeros((WIDTH, WIDTH), jnp.float32)
    for t in range(SMOOTH_RADIUS + 1):
        left = jnp.where(d == t, taps[SMOOTH_RADIUS + t], left)
    parts = []
    for _ in range(2):
        part = left.astype(jnp.bfloat16)
        parts.append(part)
        left = left - part.astype(jnp.float32)
    return jnp.concatenate(parts, axis=0)


def times(a, band):
    return jnp.dot(a, band, preferred_element_type=jnp.float32)


def halves(product):
    hi = product.astype(jnp.bfloat16)
    return jnp.concatenate([hi, (product - hi.astype(jnp.float32)).astype(jnp.bfloat16)], axis=1)


def rows_at(i):
    if isinstance(i, int):
        return pl.ds(i * ROW, ROW)
    return pl.ds(pl.multiple_of(i * ROW, ROW), ROW)


def thin_at(i):
    if isinstance(i, int):
        return pl.ds(i * THIN, THIN)
    return pl.ds(pl.multiple_of(i * THIN, 8), THIN)


def along(a, step):
    return pltpu.roll(a, (-step) % a.shape[0], 0)


def thin(a):
    x = lax.broadcasted_iota(jnp.int32, (8, WIDTH), 0)
    return jnp.concatenate([a[:SIDE], jnp.where(x < 4, a[SIDE:THIN], a[THIN:])], axis=0)


def box_x(a):
    two = a + along(a, -1)
    return thin((along(two, -1) + a) + along(two, 2)) * (1.0 / (2 * BOX_RADIUS + 1) ** 3)


def box_zx(ref, which, i, count):
    r = [ref[which, rows_at(i + t), :] for t in range(2 * BOX_RADIUS + count)]
    if count == 1:
        return [box_x(((r[0] + r[1]) + (r[2] + r[3])) + r[4])]
    mid = (r[1] + r[2]) + (r[3] + r[4])
    return [box_x(r[0] + mid), box_x(mid + r[5])]


def mask_rows(ref):
    x = lax.broadcasted_iota(jnp.int32, (THIN, WIDTH), 0)
    m = ref[...].astype(jnp.float32)
    right = jnp.where(x < SIDE + SMOOTH_RADIUS, m[1:2], 0.0)
    return jnp.where(x < SIDE, m[0:1], jnp.where(x >= THIN - SMOOTH_RADIUS, m[2:3], right))


def fixed_sums(f, sums, q, rows, bands):
    sums[q, rows, :] = times(f, bands[0])
    wide = f.astype(jnp.float32)
    sums[q + 1, rows, :] = times(halves(wide * wide), bands[1])


def fixed_rows(sums, q, i, here, mask):
    means = box_zx(sums, q, i, len(here))
    squares = box_zx(sums, q + 1, i, len(here))
    out = []
    for h, m, p, sq in zip(here, mask, means, squares):
        out.append((p, h - p, m / (sq - p * p + var_eps)))
    return out


def fixed_kernel(fixed_ref, mask_ref, mean_ref, away_ref, gain_ref, sums):
    bands = box_band()
    chunk = 8 * ROW

    def by_y(i, carry):
        rows = pl.ds(pl.multiple_of(i * chunk, chunk), chunk)
        fixed_sums(fixed_ref[rows, :], sums, 0, rows, bands)
        return carry

    lax.fori_loop(0, SIDE // 8, by_y, 0)
    mask = mask_rows(mask_ref)

    def by_z(step, carry):
        i = 2 * step
        here = [thin(fixed_ref[rows_at(i + BOX_RADIUS + t), :].astype(jnp.float32)) for t in range(2)]
        for t, (mean, away, gain) in enumerate(fixed_rows(sums, 0, i, here, [mask, mask])):
            mean_ref[thin_at(i + t), :] = mean
            away_ref[thin_at(i + t), :] = away
            gain_ref[thin_at(i + t), :] = gain
        return carry

    lax.fori_loop(0, INNER // 2, by_z, 0)


def fixed_part(fixed, mask):
    out = jax.ShapeDtypeStruct((INNER * THIN, WIDTH), jnp.float32)
    return pl.pallas_call(
        fixed_kernel,
        out_shape=[out] * 3,
        in_specs=[in_vmem()] * 2,
        out_specs=[in_vmem()] * 3,
        scratch_shapes=[pltpu.VMEM((2, SIDE * ROW, WIDTH), jnp.float32)],
        compiler_params=params(8),
        cost_estimate=cost(5_000_000_000, 4_000_000),
        name="fixed_part",
    )(fixed, mask)


def sums_by_y(f, wide, sums, rows, bands, with_fixed):
    mw = wide[rows, :]
    fw = f.astype(jnp.float32)
    n = mw.shape[0]
    plain = [mw.astype(jnp.bfloat16)] + ([f] if with_fixed else [])
    pairs = [mw * mw, mw * fw] + ([fw * fw] if with_fixed else [])
    one = times(jnp.concatenate(plain, axis=0), bands[0])
    two = times(jnp.concatenate([halves(p) for p in pairs], axis=0), bands[1])
    sums[0, rows, :] = one[:n]
    sums[1, rows, :] = two[:n]
    sums[2, rows, :] = two[n : 2 * n]
    if with_fixed:
        sums[3, rows, :] = one[n:]
        sums[4, rows, :] = two[2 * n :]


def force_rows(wide, sums, i, fixed, force, k, pitch):
    count = len(fixed)
    means = box_zx(sums, 0, i, count)
    squares = box_zx(sums, 1, i, count)
    products = box_zx(sums, 2, i, count)
    lane = lax.broadcasted_iota(jnp.int32, (THIN, WIDTH), 1)
    at = [thin(wide[rows_at(i + BOX_RADIUS - 1 + t), :]) for t in range(count + 2)]
    for t, (mean_f, away, gain) in enumerate(fixed):
        mean = means[t]
        q = (products[t] - mean_f * mean) / (squares[t] - mean * mean + var_eps)
        m = at[t + 1]
        term = gain * q * (away - q * (m - mean))
        up = jnp.where(lane == WIDTH - 1, 0.0, pltpu.roll(m, WIDTH - 1, 1))
        down = jnp.where(lane == 0, 0.0, pltpu.roll(m, 1, 1))
        steps = (along(m, 1) - along(m, -1), at[t + 2] - at[t], up - down)
        for c in range(3):
            force[thin_at(c * pitch + k + t), :] = term * steps[c]


def smooth_rows(row, i, out_ref, z, count, peak):
    taps = smooth_weights(SMOOTH_RADIUS)[SMOOTH_RADIUS:]
    mid = SMOOTH_RADIUS
    total = [None] * count
    for c in range(3):
        g = [row(c, i + t) for t in range(2 * SMOOTH_RADIUS + count)]
        for n in range(count):
            s = taps[0] * g[n + mid]
            for t in range(1, SMOOTH_RADIUS + 1):
                s += taps[t] * (g[n + mid - t] + g[n + mid + t])
            a = taps[0] * s
            for t in range(1, SMOOTH_RADIUS + 1):
                a += taps[t] * (along(s, -t) + along(s, t))
            a = a[:SIDE]
            out_ref[pl.ds(c * SIDE * SIDE + z + n, SIDE, stride=SIDE), :] = a
            total[n] = a * a if c == 0 else total[n] + a * a
    for one in total:
        peak = jnp.maximum(peak, one)
    return peak


def smooth_along_y(force, i, pitch, count, out, j, out_pitch, double):
    f = [force[pl.ds((c * pitch + i) * THIN, count * THIN), :].astype(jnp.bfloat16) for c in range(3)]
    f = jnp.concatenate(f, axis=0)
    g = times(jnp.concatenate([f, f], axis=1), double)
    for c in range(3):
        out[pl.ds((c * out_pitch + j) * THIN, count * THIN), :] = g[c * count * THIN : (c + 1) * count * THIN]


def inner_kernel(warped_ref, fixed_ref, mean_ref, away_ref, gain_ref, out_ref, edge_ref, peak_ref, wide, sums, force, smooth_y):
    bands = box_band()
    double = smooth_band()
    step = 4

    def by_y(n):
        for pair in range(n * step // DEEP, (n + 1) * step // DEEP):
            for half in range(2):
                for z in range(DEEP):
                    src = (pair * 2 + half) * OUT_PITCH + z * PART
                    dst = (pair * DEEP + z) * ROW
                    own = warped_ref[pl.ds(src, HALF), :]
                    wide[pl.ds(dst + half * HALF, HALF), :] = own.astype(jnp.float32)
                    side = warped_ref[pl.ds(src + HALF, 8), :]
                    wide[pl.ds(dst + SIDE + 8 * half, 8), :] = side.astype(jnp.float32)
        rows = pl.ds(n * step * ROW, step * ROW)
        sums_by_y(fixed_ref[rows, :], wide, sums, rows, bands, False)

    by_y(0)
    peak = jnp.zeros((SIDE, WIDTH), jnp.float32)
    done = 0
    for n in range(INNER // step):
        by_y(n + 1)
        for i in range(n * step, (n + 1) * step, 2):
            fixed = [
                (mean_ref[thin_at(i + t), :], away_ref[thin_at(i + t), :], gain_ref[thin_at(i + t), :])
                for t in range(2)
            ]
            force_rows(wide, sums, i, fixed, force, i, INNER)
        smooth_along_y(force, n * step, INNER, step, smooth_y, n * step, INNER, double)
        while done + 1 + 2 * SMOOTH_RADIUS < (n + 1) * step:
            peak = smooth_rows(
                lambda c, i: smooth_y[thin_at(c * INNER + i), :], done, out_ref, done + RIM, 2, peak
            )
            done += 2
    kept = 2 * SMOOTH_RADIUS * THIN
    for c in range(3):
        at = c * INNER * THIN
        edge_ref[c, 0:kept, :] = smooth_y[at : at + kept, :]
        edge_ref[c, kept : 2 * kept, :] = smooth_y[at + INNER * THIN - kept : at + INNER * THIN, :]
    peak_ref[...] = peak


def rim_kernel(
    below_ref, above_ref, head_ref, tail_ref, mask_ref, edge_ref, first_ref,
    out_ref, peak_ref, wide, fwide, sums, force, smooth_y,
):
    bands = box_band()
    double = smooth_band()
    own = RIM - 1
    stack = RIM + own
    for ref, start, count, at in (
        (below_ref, 0, RIM, 0),
        (head_ref, 0, own, RIM),
        (tail_ref, RIM - own, own, stack),
        (above_ref, 0, RIM, stack + own),
    ):
        rows = pl.ds(at * ROW, count * ROW)
        wide[rows, :] = ref[pl.ds(start * ROW, count * ROW), :].astype(jnp.float32)
        fwide[rows, :] = ref[pl.ds((RIM + start) * ROW, count * ROW), :].astype(jnp.float32)
    last = pl.ds(2 * RIM * ROW, 8)
    masks = [mask_rows(below_ref.at[last, :]), mask_rows(mask_ref), mask_rows(above_ref.at[last, :])]
    kept = 2 * SMOOTH_RADIUS
    tall = RIM + kept
    for side in range(2):
        for n in range(stack // 3):
            rows = pl.ds((side * stack + 3 * n) * ROW, 3 * ROW)
            sums_by_y(fwide[rows, :].astype(jnp.bfloat16), wide, sums, rows, bands, True)
    for i, count in ((0, 2), (2, 1), (3, 2)):
        for side in range(2):
            first = stack * side + i
            mask = []
            for t in range(i, i + count):
                outer = t < SMOOTH_RADIUS if side == 0 else t >= RIM - SMOOTH_RADIUS
                mask.append(masks[2 * side] if outer else masks[1])
            here = [thin(fwide[rows_at(first + BOX_RADIUS + t), :]) for t in range(count)]
            fixed = fixed_rows(sums, 3, first, here, mask)
            force_rows(wide, sums, first, fixed, force, i + RIM * side, 2 * RIM)
    peak = first_ref[...]
    for side in range(2):
        smooth_along_y(force, side * RIM, 2 * RIM, RIM, smooth_y, side * RIM, 2 * RIM, double)

    def row(c, i):
        side, j = i // tall, i % tall
        if side == 0 and j >= RIM or side == 1 and j < kept:
            return edge_ref[c, thin_at(j - RIM if side == 0 else kept + j), :]
        return smooth_y[thin_at(c * 2 * RIM + (j if side == 0 else RIM + j - kept)), :]

    for i, count in ((0, 2), (2, 2), (4, 1)):
        for side in range(2):
            peak = smooth_rows(row, tall * side + i, out_ref, (SIDE - RIM) * side + i, count, peak)
    top = jnp.max(jnp.max(peak, axis=0, keepdims=True), axis=1, keepdims=True)
    peak_ref[...] = jnp.broadcast_to(top.reshape(1, 1, 1), peak_ref.shape)


def inner(warped, fixed, mean, away, gain):
    return pl.pallas_call(
        inner_kernel,
        out_shape=[
            jax.ShapeDtypeStruct((3 * SIDE * SIDE, WIDTH), jnp.float32),
            jax.ShapeDtypeStruct((3, 4 * SMOOTH_RADIUS * THIN, WIDTH), jnp.float32),
            jax.ShapeDtypeStruct((SIDE, WIDTH), jnp.float32),
        ],
        in_specs=[in_vmem()] * 5,
        out_specs=[in_vmem()] * 3,
        scratch_shapes=[
            pltpu.VMEM((SIDE * ROW, WIDTH), jnp.float32),
            pltpu.VMEM((3, SIDE * ROW, WIDTH), jnp.float32),
            pltpu.VMEM((3 * INNER * THIN, WIDTH), jnp.float32),
            pltpu.VMEM((3 * INNER * THIN, WIDTH), jnp.float32),
        ],
        compiler_params=params(14),
        cost_estimate=cost(10_000_000_000, 8_000_000),
        name="inner",
    )(warped, fixed, mean, away, gain)


def rim(below, above, head, tail, mask, edge, first):
    stack = 2 * (2 * RIM - 1) * ROW
    tall = 2 * RIM * THIN
    return pl.pallas_call(
        rim_kernel,
        out_shape=[
            jax.ShapeDtypeStruct((3 * SIDE * SIDE, WIDTH), jnp.float32),
            jax.ShapeDtypeStruct((OWNERS, 1, WIDTH), jnp.float32),
        ],
        in_specs=[in_vmem()] * 7,
        out_specs=[in_vmem()] * 2,
        scratch_shapes=[pltpu.VMEM((stack, WIDTH), jnp.float32)] * 2
        + [pltpu.VMEM((5, stack, WIDTH), jnp.float32)]
        + [
            pltpu.VMEM((3 * 2 * RIM * THIN, WIDTH), jnp.float32),
            pltpu.VMEM((3 * tall, WIDTH), jnp.float32),
        ],
        compiler_params=params(14),
        name="rim",
    )(below, above, head, tail, mask, edge, first)


def relay_kernel(in_ref, out_ref):
    a = jnp.max(in_ref[...].reshape(in_ref.shape[0], WIDTH), axis=0, keepdims=True)
    out_ref[...] = jnp.broadcast_to(a.reshape(1, 1, WIDTH), out_ref.shape)


def relay(tiles, count):
    return pl.pallas_call(
        relay_kernel,
        out_shape=jax.ShapeDtypeStruct((count, 1, WIDTH), jnp.float32),
        in_specs=[in_vmem()],
        out_specs=in_vmem(),
        compiler_params=params(1),
        name="relay",
    )(tiles)


def finish_kernel(peaks_ref, core_ref, rim_ref, out_ref, block, sems):
    peak = jnp.sqrt(jnp.max(peaks_ref[...].reshape(peaks_ref.shape[0], WIDTH), axis=0, keepdims=True))
    scale = jnp.broadcast_to(step_length / (peak + peak_eps), (SIDE, WIDTH))
    z = lax.broadcasted_iota(jnp.int32, (SIDE, WIDTH), 0)
    at_rim = (z < RIM) | (z >= SIDE - RIM)
    copies = []
    for c in range(3):
        for part in range(SIDE // STEP_X):
            for x in range(part * STEP_X, (part + 1) * STEP_X):
                rows = pl.ds((c * SIDE + x) * SIDE, SIDE)
                block[c, x] = jnp.where(at_rim, rim_ref[rows, :], core_ref[rows, :]) * scale
            at = pl.ds(part * STEP_X, STEP_X)
            copies.append(pltpu.make_async_copy(block.at[c, at], out_ref.at[c, at], sems.at[len(copies)]))
            copies[-1].start()
    for copy in copies:
        copy.wait()


def finish(peaks, core, rims):
    return pl.pallas_call(
        finish_kernel,
        out_shape=jax.ShapeDtypeStruct((3, SIDE, SIDE, WIDTH), jnp.float32),
        in_specs=[in_vmem()] * 3,
        out_specs=in_place(),
        scratch_shapes=[
            pltpu.VMEM((3, SIDE, SIDE, WIDTH), jnp.float32),
            pltpu.SemaphoreType.DMA((3 * SIDE // STEP_X,)),
        ],
        compiler_params=params(12),
        name="finish",
    )(peaks, core, rims)


def per_device(fixed_image, moving_image, fetch_owner, fetch_block, fetch_count, interp_level, block_mask):
    side, width = SIDE, WIDTH
    sent = pack(fetch_owner, fetch_block, fetch_count, interp_level.transpose(0, 1, 3, 2, 4), moving_image)
    got = lax.all_to_all(sent, "blk", split_axis=0, concat_axis=0, tiled=True)

    mask_row = jnp.repeat(block_mask.reshape(BLOCKS), side).astype(jnp.bfloat16)[None]
    last = jnp.concatenate([fixed_image[side - RIM :].reshape(-1, width), mask_row], axis=0)
    first = jnp.concatenate([fixed_image[:RIM].reshape(-1, width), mask_row], axis=0)
    left = lax.ppermute(last, "blk", shift_up("blk"))
    right = lax.ppermute(first, "blk", shift_down("blk"))
    turn = lambda a: a[:-1].reshape(RIM, side, width)
    fixed = jnp.concatenate(
        [fixed_image, turn(right), jnp.zeros((ROW - EXT, side, width), jnp.bfloat16), turn(left)], axis=0
    ).transpose(1, 0, 2)
    masks = jnp.concatenate([mask_row, right[-1:], left[-1:], jnp.zeros((5, width), jnp.bfloat16)], axis=0)
    mean, away, gain = fixed_part(fixed.reshape(side * ROW, width), masks)

    half = (lax.axis_index("blk") % 2).astype(jnp.int32).reshape(1)
    warped = lax.all_to_all(hold(half, got), "blk", split_axis=0, concat_axis=0, tiled=True)

    def z_rows(pairs):
        part = warped.reshape(side // DEEP, 2, DEEP, PART, width)[pairs]
        rows = [part[:, 0, :, :HALF], part[:, 1, :, :HALF], part[:, 0, :, HALF:], part[:, 1, :, HALF:]]
        return jnp.concatenate(rows, axis=2).reshape(-1, ROW, width)

    def message(moving_rows, fixed_rows):
        return jnp.concatenate([moving_rows.reshape(-1, width), fixed_rows.reshape(-1, width), masks], axis=0)

    tail = message(z_rows(slice(side // DEEP - 3, None))[1:], fixed[side - RIM :])
    head = message(z_rows(slice(0, 3))[:RIM], fixed[:RIM])
    below = lax.ppermute(tail, "slab", shift_up("slab"))
    above = lax.ppermute(head, "slab", shift_down("slab"))
    core, edge, top = inner(warped.reshape(side * ROW, width), fixed.reshape(side * ROW, width), mean, away, gain)
    rims, peak = rim(below, above, head, tail, masks, edge, top)
    peak = lax.all_to_all(peak, "blk", split_axis=0, concat_axis=0, tiled=True)
    peak = relay(peak, lax.axis_size("slab"))
    peak = lax.all_to_all(peak, "slab", split_axis=0, concat_axis=0, tiled=True)
    return finish(peak, core, rims)


def solution(mesh):
    in_specs = (
        P("blk", "slab", None),
        P("blk", "slab", None),
        P("blk", "slab", None, None),
        P("blk", "slab", None, None),
        P("blk", "slab", None),
        P("blk", "slab", None, None, None),
        P("blk", "slab", None),
    )
    return jax.shard_map(
        per_device, mesh=mesh, in_specs=in_specs, out_specs=P(None, "blk", "slab", None), check_vma=False
    )
```
